32 devices in a mesh: gx: 8 (over z, y), gy: 4 (over x, core).
Axes of the slice: x: 2, y: 2, z: 4, core: 2. Of those that a mesh axis runs over, the one named last changes fastest.
Arguments:
- positions: float32 [3, 8192, 128], P(None, ('gx', 'gy')), may hold values from 0 to 1
- masses: float32 [8192, 128], P(('gx', 'gy')), may hold values from 0.004 to 0.012
- smoothing: float32 [8192, 128], P(('gx', 'gy')), may hold values from 0.55 to 1
- entropy: float32 [8192, 128], P(('gx', 'gy')), may hold values from 0.5 to 2
- density: float32 [8192, 128], P(('gx', 'gy')), may hold values from 0.5 to 2
- active_cells: int32 [128], P(('gx', 'gy')), may hold values from 0 to 8191, as said below
- active_count: int32 [32], P(('gx', 'gy')), may hold values from 1 to 4, 84 in all
- neighbours: int32 [128, 27], P(('gx', 'gy')), may hold values from 0 to 8191, as said below
- mig_source: int32 [4096], P(('gx', 'gy')), may hold values from 0 to 32767
- mig_dest: int32 [4096, 1], P(('gx', 'gy')), may hold values from 0 to 31; in each aligned block of 128 rows (0 to 127, 128 to 255, ...) at most 8 rows name the same one
Outputs:
- new_density: float32 [8192, 128], P(('gx', 'gy'))
- acceleration: float32 [3, 128, 128], P(None, ('gx', 'gy'))
- arrivals: float32 [7, 8192], P(None, ('gx', 'gy'))
The draws below stay inside these ranges and needn't reach their ends.
Inputs may be any that keep to these rules, and one draw needn't show every extreme that they name: `active_cells`: the 4 entries of device d are distinct cells of device d. The middle entry (index 13) of a slot is its active cell. Every other entry is a cell of the slot's own device, or a cell of the device just before or just after it in the cell order lying within 64 cells of the end they share. Over all slots of one device, at most 8 distinct cells of each of these two devices are named, and every device with neighbours on both sides names exactly 8 on each side. `mig_dest`: within the 128 rows of one device no destination appears more than 8 times; some destination appears exactly 8 times.
All inputs are finite; a program needn't handle non-finite values. No bound on the sum of `active_count` on one device may be relied on, other than what follows from the above.
Results may differ from the reference program's by a relative error of at most 0.0003.
Values sent between devices are 32-bit elements; how exact they have to be, the bound alone decides.
No kernel may reach another device: no remote copies, remote signals or barrier semaphores. Data moves between devices by JAX's collectives and lax.ppermute only.
A program may use at most 64 MiB of HBM per device.

```python
import math
import jax
import jax.numpy as jnp
import numpy as np
from jax import lax

P_SIZE = 128
NBR = 27
CELLS_DEV = 256
MIG_DEV = 128
RIM = 64
ACT_MAX = 4
GHOST_MAX = 8
MIG_CAP = 8
NCELLS = 8192
NACT = 128
NMIG = 4096
N_GX = 8
N_GY = 4


def cell_lists(key):
    devices = N_GX * N_GY
    entries = ACT_MAX * NBR
    device_keys = jax.random.split(jax.random.fold_in(key, 17), devices)

    def ordering_of(one_key):
        return jax.random.permutation(one_key, CELLS_DEV)
    ordering = jax.vmap(ordering_of)(device_keys)
    device_ids = jnp.arange(devices)
    chosen = ordering[:, :ACT_MAX] + (device_ids * CELLS_DEV)[:, None]
    active = chosen.reshape(-1).astype(jnp.int32)
    pool_keys = jax.random.split(jax.random.fold_in(key, 41), devices)

    def left_pool(one_key):
        return jax.random.permutation(one_key, RIM)[:GHOST_MAX]

    def right_pool(one_key):
        return jax.random.permutation(jax.random.fold_in(one_key, 1), RIM)[:GHOST_MAX]
    left_cells = device_ids[:, None] * CELLS_DEV - RIM + jax.vmap(left_pool)(pool_keys)
    right_cells = (device_ids[:, None] + 1) * CELLS_DEV + jax.vmap(right_pool)(pool_keys)
    own_cells = jax.random.randint(jax.random.fold_in(key, 29), (devices, entries), 0, CELLS_DEV) + device_ids[:, None] * CELLS_DEV
    kinds = jax.random.randint(jax.random.fold_in(key, 53), (devices, entries), 0, 4)
    pool_pick = jax.random.randint(jax.random.fold_in(key, 59), (devices, entries), 0, GHOST_MAX)
    flat = jnp.arange(entries)
    column = flat % NBR
    rank = flat - flat // NBR - (column > NBR // 2).astype(jnp.int32)
    forced_left = (rank < GHOST_MAX)[None, :]
    forced_right = jnp.logical_and(rank >= GHOST_MAX, rank < 2 * GHOST_MAX)[None, :]
    kinds = jnp.where(forced_left, 2, jnp.where(forced_right, 3, kinds))
    pool_pick = jnp.where(forced_left, rank[None, :], jnp.where(forced_right, rank[None, :] - GHOST_MAX, pool_pick))
    left_value = jnp.take_along_axis(left_cells, pool_pick, axis=1)
    right_value = jnp.take_along_axis(right_cells, pool_pick, axis=1)
    has_left = (device_ids > 0)[:, None]
    has_right = (device_ids < devices - 1)[:, None]
    picked = jnp.where(jnp.logical_and(kinds == 2, has_left), left_value, jnp.where(jnp.logical_and(kinds == 3, has_right), right_value, own_cells))
    picked = picked.reshape(devices * ACT_MAX, NBR)
    centre = (jnp.arange(NBR) == NBR // 2)[None, :]
    neighbour_ids = jnp.where(centre, active[:, None], picked).astype(jnp.int32)
    return (active, neighbour_ids)


def draw_active_cells(key, part):
    return cell_lists(key)[0]


def draw_neighbours(key, part):
    return cell_lists(key)[1]


def plant(drawn, stream_key, smallest, largest):
    index_at = [jax.random.randint(jax.random.fold_in(stream_key, axis), (), 0, length) for axis, length in enumerate(drawn.shape)]
    main_axis = drawn.shape.index(max(drawn.shape))
    neighbour = index_at[:main_axis] + [(index_at[main_axis] + 1) % drawn.shape[main_axis]] + index_at[main_axis + 1:]
    return drawn.at[tuple(index_at)].set(smallest).at[tuple(neighbour)].set(largest)


def shard_levels(rng, shape, cuts, least, largest):
    def one(dim, shards_of):
        steps = jax.random.uniform(jax.random.fold_in(jax.random.fold_in(rng, 6), dim), (shards_of,), jnp.float32, least / len(cuts), largest / len(cuts))
        return jnp.repeat(jnp.exp(steps), shape[dim] // shards_of).reshape((-1,) + (1,) * (len(shape) - dim - 1))

    gain = one(*cuts[0])
    for cut in cuts[1:]:
        gain = gain * one(*cut)
    return gain


def split_up(number_of, total, reach, skew):
    portions = [(1 << 20) // math.isqrt(rank ** skew) + 1 for rank in range(2, number_of + 1)]
    surplus, given = total - reach - (number_of - 1), [1] * (number_of - 1)
    while surplus > 0:
        candidates = [i for i in range(number_of - 1) if given[i] < reach]
        mass, remaining = sum([portions[i] for i in candidates]), surplus
        for i in candidates:
            addition = min(reach - given[i], max(1, remaining * portions[i] // mass), surplus)
            given[i] = given[i] + addition
            surplus = surplus - addition
    return np.array([reach] + given)


def uneven(key, number_of, total, most, slope):
    if number_of == 2:
        one = jax.random.randint(key, (), max(1, total - most), min(most, total - 1) + 1)
        return jnp.stack([one, total - one])
    sizes = jnp.asarray(split_up(number_of, total, most, slope), jnp.int32)
    pairs = (number_of - 1) // 2
    source_of, sink = sizes[1:1 + 2 * pairs:2], sizes[2:2 + 2 * pairs:2]
    margin = jnp.minimum(source_of - 1, most - sink)
    moved = jax.random.randint(jax.random.fold_in(key, 1), (pairs,), 0, 1 << 20) % (margin + 1)
    sizes = sizes.at[1:1 + 2 * pairs:2].set(source_of - moved).at[2:2 + 2 * pairs:2].set(sink + moved)
    return sizes[jax.random.permutation(jax.random.fold_in(key, 2), number_of)]


def deal_out(key, own, number, rows, count, top, bound, skew):
    order = jax.random.permutation(key, count)
    heavy_load, usual = load_shares(count, rows * top, bound, skew, True), load_shares(count, rows * top, bound, skew, False)
    places = jnp.arange(count)

    def named(tallies, offset_by):
        used = int((tallies > 0).sum())
        fixed = max(1, used // 4)
        shifted = fixed + (places - fixed + offset_by * (used - fixed)) % max(1, count - fixed)
        return jnp.zeros((count,), jnp.int32).at[order[jnp.where(places < fixed, places, shifted)]].set(jnp.asarray(tallies, jnp.int32))

    tallies = jnp.where(number % 4 == 0, named(heavy_load, number // 4), named(usual, number - number // 4 - 1))
    mixed = jax.random.permutation(jax.random.fold_in(own, 3), count)
    source_of, sink = mixed[0:count // 2 * 2:2], mixed[1:count // 2 * 2:2]
    room = jnp.minimum(tallies[source_of] - 1, bound - tallies[sink]) // 2
    room = jnp.where((source_of == order[0]) | (sink == order[0]) | (tallies[sink] == 0), 0, jnp.maximum(room, 0))
    shifted = jax.random.randint(jax.random.fold_in(own, 4), (count // 2,), 0, 1 << 20) % (room + 1)
    tallies = tallies.at[source_of].add(-shifted).at[sink].add(shifted)
    items = jnp.searchsorted(jnp.cumsum(tallies), jnp.arange(rows * top), side="right").astype(jnp.int32)
    grid = items.reshape(top, rows).T
    grid = grid[jax.random.permutation(jax.random.fold_in(own, 1), rows)]
    offset_by = jax.random.randint(jax.random.fold_in(own, 2), (rows, 1), 0, top)
    return jnp.take_along_axis(grid, (jnp.arange(top)[None, :] + offset_by) % top, axis=1)


def load_shares(number_of, total, most, lean, full):
    portions = [(1 << 20) // math.isqrt(rank ** lean) + 1 for rank in range(1, number_of + 1)]
    largest = most if full else min(most, max(-(-total // number_of), total * portions[0] // sum(portions)))
    least = 1 if total - largest >= number_of - 1 else 0
    holding, rest = [largest] + [least] * (number_of - 1), total - largest - least * (number_of - 1)
    while rest > 0:
        movable = [i for i in range(1, number_of) if holding[i] < largest] or [i for i in range(1, number_of) if holding[i] < most]
        whole, budget = sum([portions[i] for i in movable]), rest
        for i in movable:
            extra = min(most - holding[i], max(1, budget * portions[i] // whole), rest)
            holding[i] = holding[i] + extra
            rest = rest - extra
    return np.array(holding)


def setup_inputs(seed: int = 0) -> dict:
    splits = jax.random.split(jax.random.key(seed), 11)
    positions = jnp.clip(1.0 * jax.random.uniform(splits[0], (3, NCELLS, P_SIZE), jnp.float32) ** shard_levels(splits[0], (3, NCELLS, P_SIZE), ((1, 32),), -0.2, 0.2), 0.0, 1.0)
    masses = jnp.clip(jnp.exp(math.log(0.012) - 1.09861225 * jax.random.uniform(splits[1], (NCELLS, P_SIZE), jnp.float32) ** shard_levels(splits[1], (NCELLS, P_SIZE), ((0, 32),), -0.2, 0.2)), 0.004, 0.012)
    smoothing = jnp.clip(0.55 + 0.45 * jax.random.uniform(splits[2], (NCELLS, P_SIZE), jnp.float32) ** shard_levels(splits[2], (NCELLS, P_SIZE), ((0, 32),), -0.2, 0.2), 0.55, 1.0)
    entropy = jnp.clip(jnp.exp(math.log(2.0) - 1.3862944 * jax.random.uniform(splits[3], (NCELLS, P_SIZE), jnp.float32) ** shard_levels(splits[3], (NCELLS, P_SIZE), ((0, 32),), -0.2, 0.2)), 0.5, 2.0)
    density = jnp.clip(jnp.exp(math.log(2.0) - 1.3862944 * jax.random.uniform(splits[4], (NCELLS, P_SIZE), jnp.float32) ** shard_levels(splits[4], (NCELLS, P_SIZE), ((0, 32),), -0.2, 0.2)), 0.5, 2.0)
    active_cells = draw_active_cells(jax.random.fold_in(splits[10], 71), 0)
    active_count = uneven(splits[6], N_GX * N_GY, N_GX * N_GY * (ACT_MAX + 1) // 2 + ACT_MAX, ACT_MAX, 2).astype(jnp.int32)
    neighbours = draw_neighbours(jax.random.fold_in(splits[10], 71), 0)
    mig_source = plant(jax.random.randint(splits[8], (NMIG,), 0, CELLS_DEV * P_SIZE), jax.random.fold_in(splits[8], 1), 0, (CELLS_DEV * P_SIZE) - 1).astype(jnp.int32)
    mig_dest_keys = jax.random.split(jax.random.fold_in(splits[9], 1), NMIG // MIG_DEV)
    mig_dest_turns = jax.random.permutation(jax.random.fold_in(splits[9], 3), NMIG // MIG_DEV)
    mig_dest = jax.vmap(lambda own, number: deal_out(jax.random.fold_in(splits[9], 2), own, number, MIG_DEV, N_GX * N_GY, 1, MIG_CAP, 2))(mig_dest_keys, mig_dest_turns).reshape((NMIG, 1))
    return {"positions": positions, "masses": masses, "smoothing": smoothing, "entropy": entropy, "density": density, "active_cells": active_cells, "active_count": active_count, "neighbours": neighbours, "mig_source": mig_source, "mig_dest": mig_dest}


kernel_norm = 8.0 / math.pi

def stencil_offsets():
    index = jnp.arange(NBR)
    return jnp.stack([index // 9 - 1, index // 3 % 3 - 1, index % 3 - 1]).astype(jnp.float32)

def kernel_value(ratio):
    inner = 1.0 - 6.0 * ratio * ratio + 6.0 * ratio * ratio * ratio
    outer = 2.0 * (1.0 - ratio) ** 3
    return jnp.where(ratio < 0.5, inner, jnp.where(ratio < 1.0, outer, 0.0))

def kernel_slope(ratio):
    safe_ratio = jnp.maximum(ratio, 0.5)
    inner = -12.0 + 18.0 * ratio
    outer = -6.0 * (1.0 - ratio) ** 2 / safe_ratio
    return jnp.where(ratio < 0.5, inner, jnp.where(ratio < 1.0, outer, 0.0))

def pair_geometry(own_pos, other_pos):
    separation = own_pos[:, :, None, None] - other_pos[:, None, :, :]
    distance = jnp.sqrt(lax.optimization_barrier(jnp.sum(separation * separation, axis=0)))
    return (separation, distance)

def density_cell(own_pos, own_len, other_pos, other_mass):
    separation, distance = pair_geometry(own_pos, other_pos)
    weights = kernel_value(distance / own_len[:, None, None])
    return kernel_norm * lax.optimization_barrier(jnp.sum(other_mass[None] * weights, axis=(1, 2))) / own_len ** 3

def force_cell(own_pos, own_len, own_rho, own_press, other_pos, other_mass, other_len, other_rho, other_press):
    separation, distance = pair_geometry(own_pos, other_pos)
    own_term = (own_press / own_rho ** 2 * kernel_norm / own_len ** 5)[:, None, None] * kernel_slope(distance / own_len[:, None, None])
    other_term = (other_press / other_rho ** 2 * kernel_norm / other_len ** 5)[None] * kernel_slope(distance / other_len[None])
    factor = other_mass[None] * (own_term + other_term)
    return -lax.optimization_barrier(jnp.sum(factor[None] * separation, axis=(2, 3)))

def reference(positions, masses, smoothing, entropy, density, active_cells, active_count, neighbours, mig_source, mig_dest):
    devices = N_GX * N_GY
    stencil = stencil_offsets()
    live_slot = jnp.arange(NACT) % ACT_MAX < jnp.repeat(active_count, ACT_MAX)

    def density_one(inputs):
        cell, near_ids = inputs
        other_pos = positions[:, near_ids, :] + stencil[:, :, None]
        return density_cell(positions[:, cell, :], smoothing[cell], other_pos, masses[near_ids])
    rho = lax.map(density_one, (active_cells, neighbours))
    kept = jnp.where(live_slot[:, None], rho, density[active_cells])
    new_density = density.at[active_cells].set(kept)
    pressure = entropy * jnp.exp(5.0 / 3.0 * jnp.log(new_density))

    def force_one(inputs):
        cell, near_ids = inputs
        other_pos = positions[:, near_ids, :] + stencil[:, :, None]
        return force_cell(positions[:, cell, :], smoothing[cell], new_density[cell], pressure[cell], other_pos, masses[near_ids], smoothing[near_ids], new_density[near_ids], pressure[near_ids])
    accel_rows = lax.map(force_one, (active_cells, neighbours))
    acceleration = jnp.transpose(accel_rows, (1, 0, 2)) * live_slot[None, :, None].astype(jnp.float32)
    source_dev = (jnp.arange(NMIG) // MIG_DEV).astype(jnp.int32)
    cell_ids = (source_dev * CELLS_DEV + mig_source // P_SIZE).astype(jnp.int32)
    lane_ids = (mig_source % P_SIZE).astype(jnp.int32)
    state = jnp.concatenate([positions[:, cell_ids, lane_ids], masses[cell_ids, lane_ids][None], smoothing[cell_ids, lane_ids][None], entropy[cell_ids, lane_ids][None], new_density[cell_ids, lane_ids][None]], axis=0)
    destination = mig_dest[:, 0].reshape(devices, MIG_DEV)
    same = destination[:, :, None] == destination[:, None, :]
    earlier = jnp.arange(MIG_DEV)[None, :] < jnp.arange(MIG_DEV)[:, None]
    slot_rank = lax.optimization_barrier(jnp.sum(jnp.logical_and(same, earlier[None]), axis=2)).astype(jnp.int32).reshape(-1)
    column = (mig_dest[:, 0] * devices * MIG_CAP + source_dev * MIG_CAP + slot_rank).astype(jnp.int32)
    arrivals = jnp.zeros((7, devices * devices * MIG_CAP), jnp.float32).at[:, column].set(state)
    return (new_density, acceleration, arrivals)
```

```python
import functools
import math

import jax
import jax.numpy as jnp
from jax import lax
from jax.experimental import pallas as pl
from jax.experimental.pallas import tpu as pltpu
from jax.sharding import PartitionSpec as P

P_SIZE = 128
NBR = 27
RIM = 64
STATE = 7
PLANES = 6
ROWS = 32
TINY = 1e-12
AXES = ("gx", "gy")

kernel_norm = 8.0 / math.pi
log_six_norm = math.log(6.0 * kernel_norm)
f32 = jnp.float32
VMEM = pl.BlockSpec(memory_space=pltpu.VMEM)
SMEM = pl.BlockSpec(memory_space=pltpu.SMEM)
PARAMS = pltpu.CompilerParams(vmem_limit_bytes=16 << 20)


def own_index():
    return lax.axis_index("gx") * lax.axis_size("gy") + lax.axis_index("gy")


def beta_of(inverse_len, entropy, density):
    power = 0.5 * (log_six_norm + jnp.log(entropy)) - jnp.log(density) * (1.0 / 6.0)
    return inverse_len * inverse_len * jnp.exp(power)


def row_sums(block):
    return jnp.sum(block.T, axis=0, keepdims=True)


def offset_tile(entry):
    row = lax.broadcasted_iota(jnp.int32, (8, P_SIZE), 0)
    shift = (entry // 9 - 1, entry // 3 % 3 - 1, entry % 3 - 1)
    tile = jnp.zeros((8, P_SIZE), f32)
    for axis in range(3):
        if shift[axis]:
            tile = jnp.where(row == axis, float(shift[axis]), tile)
    return tile


def pack_kernel(
    pos_ref, mass_ref, len_ref, ent_ref, rho_ref, act_ref, cnt_ref, a_ref, b_ref, tab_ref, ih_ref, beta_ref
):
    cells = mass_ref.shape[0]
    me = own_index()
    inverse_len = 1.0 / len_ref[...]
    ih_ref[...] = inverse_len
    beta_ref[...] = beta_of(inverse_len, ent_ref[...], rho_ref[...])
    lane = lax.broadcasted_iota(jnp.int32, (8, P_SIZE), 1)
    names = jnp.full((8, P_SIZE), -1.0, f32)
    for slot in range(act_ref.shape[0]):
        mine = act_ref[slot] - me * cells
        live = slot < cnt_ref[0]
        names = jnp.where(jnp.logical_and(lane == slot, live), mine.astype(f32), names)

        @pl.when(live)
        def _():
            beta_ref[pl.ds(mine, 1), :] = jnp.zeros((1, P_SIZE), f32)

    odd = me % 2
    start_a = pl.multiple_of((1 - odd) * (cells - RIM), RIM)
    start_b = pl.multiple_of(odd * (cells - RIM), RIM)
    for out_ref, start in ((b_ref, start_b), (a_ref, start_a)):
        rows = pl.ds(start, RIM)
        for axis in range(3):
            out_ref[pl.ds(axis * RIM, RIM), :] = pos_ref[axis, rows, :]
        out_ref[pl.ds(3 * RIM, RIM), :] = mass_ref[rows, :]
        out_ref[pl.ds(4 * RIM, RIM), :] = ih_ref[rows, :]
        out_ref[pl.ds(5 * RIM, RIM), :] = beta_ref[rows, :]
        out_ref[pl.ds(PLANES * RIM, 8), :] = names
    own = pl.ds(RIM, cells)
    for axis in range(3):
        tab_ref[own, axis, :] = pos_ref[axis] - 0.5
    tab_ref[own, 4, :] = mass_ref[...]
    tab_ref[own, 5, :] = ih_ref[...]
    tab_ref[own, 6, :] = beta_ref[...]
    tab_ref[own, 7, :] = beta_ref[...] * ih_ref[...]


def migrant_kernel(
    capacity,
    pos_ref,
    mass_ref,
    len_ref,
    ent_ref,
    rho_ref,
    source_ref,
    dest_ref,
    act_ref,
    cnt_ref,
    base_ref,
    code_ref,
    place_ref,
):
    cells = mass_ref.shape[0]
    me = own_index()
    targets = base_ref.shape[0]
    source = source_ref[...]
    cell_row = source // P_SIZE
    code_row = jnp.zeros_like(source)
    for slot in range(act_ref.shape[0]):
        mine = act_ref[slot] - me * cells
        named = jnp.logical_and(cell_row == mine, slot < cnt_ref[0])
        code_row = jnp.where(named, slot + 1, code_row)
    row_id = lax.broadcasted_iota(jnp.int32, (8, P_SIZE), 0)
    stack = jnp.zeros((8, P_SIZE), f32)
    for index, part in enumerate((cell_row, source % P_SIZE, dest_ref[...], code_row)):
        stack = jnp.where(row_id == index, part.astype(f32), stack)
    columns = stack.T
    shape = (P_SIZE, P_SIZE)
    cell, lane_of, dest, code = [jnp.broadcast_to(columns[:, i : i + 1], shape) for i in range(4)]
    lane = lax.broadcasted_iota(jnp.int32, shape, 1)
    row = lax.broadcasted_iota(jnp.int32, shape, 0)
    lane_f = lane.astype(f32)
    hit = lane_f == lane_of
    same = jnp.logical_and(dest == dest_ref[...].astype(f32), lane < row)
    rank = jnp.sum(jnp.where(same, 1.0, 0.0), axis=1, keepdims=True)
    wide = lax.broadcasted_iota(jnp.int32, (P_SIZE, cells), 1).astype(f32)
    pick = jnp.where(wide == columns[:, 0:1], 1.0, 0.0)
    spot = lane_f - rank
    sent = jnp.zeros(shape, f32)
    planes = [pos_ref[0], pos_ref[1], pos_ref[2], mass_ref[...], len_ref[...], ent_ref[...], rho_ref[...]]
    for index, plane in enumerate(planes):
        found = jnp.dot(pick, plane, precision=lax.Precision.HIGHEST, preferred_element_type=f32)
        keep = jnp.logical_and(hit, code == 0.0) if index == STATE - 1 else hit
        value = jnp.sum(jnp.where(keep, found, 0.0), axis=1, keepdims=True)
        sent = jnp.where(spot == float(index * capacity), value, sent)
    aim = lax.broadcasted_iota(jnp.int32, (targets, P_SIZE), 0) == dest_ref[...]
    aim = jnp.where(aim, 1.0, 0.0)
    base_ref[...] = jnp.dot(aim, sent, precision=lax.Precision.HIGHEST, preferred_element_type=f32)
    code_ref[...] = jnp.where(hit, code, 0.0)
    place_ref[...] = jnp.where(spot == float((STATE - 1) * capacity), 1.0, 0.0)


def gather_entries(slot, base, nbr_ref, tab_ref, near_ref):
    for entry in range(NBR):
        near_ref[entry] = tab_ref[nbr_ref[slot, entry] - base] + offset_tile(entry)


def own_columns(tile, rows, out_ref):
    columns = tile.T
    for index, row in enumerate(rows):
        out_ref[index] = jnp.broadcast_to(columns[:, row : row + 1], (P_SIZE, P_SIZE))


def density_kernel(
    rho_ref,
    ent_ref,
    a_ref,
    b_ref,
    tab_in,
    base_ref,
    code_ref,
    place_ref,
    dest_ref,
    act_ref,
    cnt_ref,
    nbr_ref,
    new_ref,
    out_ref,
    tab_ref,
    near_ref,
    own_ref,
    acc_ref,
    made_ref,
    beta_ref,
):
    cells = rho_ref.shape[0]
    me = own_index()
    odd = me % 2
    left_a = odd * (RIM * 0) + (1 - odd) * (cells + RIM)
    for in_ref, start in ((a_ref, left_a), (b_ref, cells + RIM - left_a)):
        rows = pl.ds(start, RIM)
        plane = [in_ref[pl.ds(i * RIM, RIM), :] for i in range(PLANES)]
        for axis in range(3):
            tab_ref[rows, axis, :] = plane[axis] - 0.5
        tab_ref[rows, 4, :] = plane[3]
        tab_ref[rows, 5, :] = plane[4]
        tab_ref[rows, 6, :] = plane[5]
        tab_ref[rows, 7, :] = plane[5] * plane[4]
    new_ref[...] = rho_ref[...]
    made_ref[...] = jnp.zeros_like(made_ref)
    beta_ref[...] = jnp.zeros_like(beta_ref)

    @pl.loop(0, cnt_ref[0])
    def _(slot):
        mine = act_ref[slot] - me * cells
        tile = tab_ref[RIM + mine]
        gather_entries(slot, me * cells - RIM, nbr_ref, tab_ref, near_ref)
        own_columns(tile, (0, 1, 2, 5), own_ref)

        @pl.loop(0, P_SIZE // ROWS)
        def _(part):
            rows = pl.ds(pl.multiple_of(part * ROWS, ROWS), ROWS)
            x, y, z, scale = [own_ref[i, rows, :] for i in range(4)]
            total = jnp.zeros((ROWS, P_SIZE), f32)
            for entry in range(NBR):
                dx = x - near_ref[entry, 0:1, :]
                dy = y - near_ref[entry, 1:2, :]
                dz = z - near_ref[entry, 2:3, :]
                square = jnp.maximum(dx * dx + dy * dy + dz * dz, TINY)
                ratio = square * lax.rsqrt(square) * scale
                outer = jnp.maximum(1.0 - ratio, 0.0)
                inner = jnp.maximum(0.5 - ratio, 0.0)
                weight = outer * outer * outer - 4.0 * (inner * inner * inner)
                total = total + weight * near_ref[entry, 4:5, :]
            acc_ref[rows, :] = total

        inverse_len = tile[5:6, :]
        made = row_sums(acc_ref[...]) * (2.0 * kernel_norm) * inverse_len * inverse_len * inverse_len
        beta = beta_of(inverse_len, ent_ref[pl.ds(mine, 1), :], made)
        new_ref[pl.ds(mine, 1), :] = made
        tab_ref[RIM + mine, 6:7, :] = beta
        tab_ref[RIM + mine, 7:8, :] = beta * inverse_len
        made_ref[pl.ds(slot, 1), :] = made
        beta_ref[pl.ds(slot, 1), :] = beta

    code = code_ref[...]
    chosen = jnp.zeros_like(code)
    slots = act_ref.shape[0]
    for slot in range(slots):
        chosen = jnp.where(code == float(slot + 1), made_ref[slot : slot + 1, :], chosen)
    late = place_ref[...] * jnp.sum(chosen, axis=1, keepdims=True)
    targets = base_ref.shape[0]
    aim = lax.broadcasted_iota(jnp.int32, (targets, P_SIZE), 0) == dest_ref[...]
    aim = jnp.where(aim, 1.0, 0.0)
    sent = base_ref[...] + jnp.dot(
        aim, late, precision=lax.Precision.HIGHEST, preferred_element_type=f32
    )
    out_ref[...] = jnp.zeros_like(out_ref)
    out_ref[:, 0, :] = sent
    for slot in range(slots):
        out_ref[:, 1 + slot, :] = jnp.broadcast_to(beta_ref[slot : slot + 1, :], (targets, P_SIZE))


def spline(base, slope, distance):
    step = distance * slope
    near = base - step
    outer = jnp.maximum(near, 0.0)
    inner = jnp.maximum(near - step, 0.0)
    return outer * outer - inner * inner


def force_kernel(
    tab_ref,
    a_ref,
    b_ref,
    act_ref,
    cnt_ref,
    nbr_ref,
    acc_out,
    list_ref,
    near_ref,
    own_ref,
    acc_ref,
    names_a,
    names_b,
    sems,
):
    cells = tab_ref.shape[0] - 2 * RIM
    me = own_index()
    odd = me % 2
    base = me * cells - RIM
    slots = act_ref.shape[0]
    copies = [
        pltpu.make_async_copy(ref.at[pl.ds(PLANES * RIM, 8), :], names, sems.at[i])
        for i, (ref, names) in enumerate(((a_ref, names_a), (b_ref, names_b)))
    ]
    for copy in copies:
        copy.start()
    acc_out[...] = jnp.zeros_like(acc_out)
    list_ref[0] = 0
    for copy in copies:
        copy.wait()
    fa = [names_a[0, s].astype(jnp.int32) for s in range(slots)]
    fb = [names_b[0, s].astype(jnp.int32) for s in range(slots)]
    left = [jnp.where(odd == 1, fa[s], fb[s]) for s in range(slots)]
    right = [jnp.where(odd == 1, fb[s], fa[s]) for s in range(slots)]
    left = [jnp.where(v >= cells - RIM, v - (cells - RIM), -1) for v in left]
    right = [jnp.where(jnp.logical_and(v >= 0, v < RIM), v + cells + RIM, -1) for v in right]

    @pl.loop(0, cnt_ref[0])
    def _(slot):
        mine = act_ref[slot] - me * cells
        gather_entries(slot, base, nbr_ref, tab_ref, near_ref)
        own_columns(tab_ref[RIM + mine], (0, 1, 2, 6, 7), own_ref)
        for entry in range(NBR):
            cell = nbr_ref[slot, entry] - base
            found = jnp.int32(-1)
            for s in range(slots):
                found = jnp.where(cell == left[s], s, found)
                found = jnp.where(cell == right[s], slots + s, found)
            at = list_ref[0]
            list_ref[at + 1] = (slot * NBR + entry) * (2 * slots) + found
            list_ref[0] = at + jnp.where(found >= 0, 1, 0)

        @pl.loop(0, P_SIZE // ROWS)
        def _(part):
            rows = pl.ds(pl.multiple_of(part * ROWS, ROWS), ROWS)
            x, y, z, own_base, own_slope = [own_ref[i, rows, :] for i in range(5)]
            total = [jnp.zeros((ROWS, P_SIZE), f32) for _ in range(3)]
            for entry in range(NBR):
                dx = x - near_ref[entry, 0:1, :]
                dy = y - near_ref[entry, 1:2, :]
                dz = z - near_ref[entry, 2:3, :]
                square = jnp.maximum(dx * dx + dy * dy + dz * dz, TINY)
                inverse = lax.rsqrt(square)
                distance = square * inverse
                pull = spline(own_base, own_slope, distance)
                pull = pull + spline(near_ref[entry, 6:7, :], near_ref[entry, 7:8, :], distance)
                pull = pull * inverse * near_ref[entry, 4:5, :]
                total = [total[0] + pull * dx, total[1] + pull * dy, total[2] + pull * dz]
            for axis in range(3):
                acc_ref[axis, rows, :] = total[axis]

        for axis in range(3):
            acc_out[axis, pl.ds(slot, 1), :] = row_sums(acc_ref[axis])


def finish_kernel(
    capacity, tab_ref, part_ref, got_ref, list_ref, nbr_ref, act_ref, acc_out, arrive_ref, off_ref, own_ref
):
    cells = tab_ref.shape[0] - 2 * RIM
    me = own_index()
    slots = act_ref.shape[0]
    targets = got_ref.shape[0]
    acc_out[...] = part_ref[...]
    rows = got_ref[:, 0, :]
    width = targets * capacity
    column = lax.broadcasted_iota(jnp.int32, (P_SIZE, width), 1)
    lane = lax.broadcasted_iota(jnp.int32, (P_SIZE, width), 0)
    spot = lane - column % capacity
    sender = lax.broadcasted_iota(jnp.int32, (targets, width), 1) // capacity
    mask = sender == lax.broadcasted_iota(jnp.int32, (targets, width), 0)
    for index in range(STATE):
        pick = jnp.where(spot == index * capacity, 1.0, 0.0)
        spread = jnp.dot(rows, pick, precision=lax.Precision.HIGHEST, preferred_element_type=f32)
        arrive_ref[index : index + 1, :] = jnp.sum(
            jnp.where(mask, spread, 0.0), axis=0, keepdims=True
        )

    @pl.when(list_ref[0] > 0)
    def _():
        for entry in range(NBR):
            off_ref[entry] = offset_tile(entry)

    @pl.loop(0, list_ref[0])
    def _(item):
        word = list_ref[item + 1]
        found = word % (2 * slots)
        place = word // (2 * slots)
        slot = place // NBR
        entry = place % NBR
        other = jnp.where(found < slots, me - 1, me + 1)
        near = tab_ref[nbr_ref[slot, entry] - (me * cells - RIM)] + off_ref[entry]
        beta = got_ref[other, pl.ds(1 + found % slots, 1), :]
        slope = beta * near[5:6, :]
        own_columns(tab_ref[RIM + act_ref[slot] - me * cells], (0, 1, 2), own_ref)
        dx = own_ref[0] - near[0:1, :]
        dy = own_ref[1] - near[1:2, :]
        dz = own_ref[2] - near[2:3, :]
        square = jnp.maximum(dx * dx + dy * dy + dz * dz, TINY)
        inverse = lax.rsqrt(square)
        pull = spline(beta, slope, square * inverse) * inverse * near[4:5, :]
        for axis, part in enumerate((dx, dy, dz)):
            acc_out[axis, pl.ds(slot, 1), :] += row_sums(pull * part)


def local(
    positions,
    masses,
    smoothing,
    entropy,
    density,
    active_cells,
    active_count,
    neighbours,
    mig_source,
    mig_dest,
):
    cells = masses.shape[0]
    slots = active_cells.shape[0]
    devices = lax.axis_size(AXES)
    mig_rows = mig_source.shape[0]
    capacity = max(2, 2 * mig_rows // devices)
    shape = jax.ShapeDtypeStruct
    rim_shape = shape((PLANES * RIM + 8, P_SIZE), f32)
    tab_shape = shape((cells + 2 * RIM, 8, P_SIZE), f32)
    fields = (positions, masses, smoothing, entropy, density)
    source = mig_source.reshape(1, mig_rows)
    dest = mig_dest.reshape(1, mig_rows)

    send_a, send_b, table = pl.pallas_call(
        pack_kernel,
        out_shape=(rim_shape, rim_shape, tab_shape),
        in_specs=[VMEM] * 5 + [SMEM] * 2,
        out_specs=(VMEM,) * 3,
        scratch_shapes=[pltpu.VMEM((cells, P_SIZE), f32)] * 2,
        compiler_params=PARAMS,
        name="pack",
    )(*fields, active_cells, active_count)

    pairs_a = [(i ^ 1, i) for i in range(devices) if i ^ 1 < devices]
    pairs_b = []
    for i in range(1, devices - 1, 2):
        pairs_b += [(i, i + 1), (i + 1, i)]
    got_b = lax.ppermute(send_b, AXES, pairs_b)
    got_a = lax.ppermute(send_a, AXES, pairs_a)

    base, code, place = pl.pallas_call(
        functools.partial(migrant_kernel, capacity),
        out_shape=(
            shape((devices, P_SIZE), f32),
            shape((mig_rows, P_SIZE), f32),
            shape((mig_rows, P_SIZE), f32),
        ),
        in_specs=[VMEM] * 7 + [SMEM] * 2,
        out_specs=(VMEM,) * 3,
        compiler_params=PARAMS,
        name="migrants",
    )(*fields, source, dest, active_cells, active_count)

    new_density, outgoing, table = pl.pallas_call(
        density_kernel,
        out_shape=(
            shape((cells, P_SIZE), f32),
            shape((devices, 8, P_SIZE), f32),
            tab_shape,
        ),
        in_specs=[VMEM] * 9 + [SMEM] * 3,
        out_specs=(VMEM,) * 3,
        input_output_aliases={4: 2},
        scratch_shapes=[
            pltpu.VMEM((NBR, 8, P_SIZE), f32),
            pltpu.VMEM((4, P_SIZE, P_SIZE), f32),
            pltpu.VMEM((P_SIZE, P_SIZE), f32),
            pltpu.VMEM((8, P_SIZE), f32),
            pltpu.VMEM((8, P_SIZE), f32),
        ],
        compiler_params=PARAMS,
        name="density",
    )(density, entropy, got_a, got_b, table, base, code, place, dest, active_cells, active_count, neighbours)

    incoming = lax.all_to_all(outgoing, AXES, split_axis=0, concat_axis=0, tiled=True)

    todo_len = pl.cdiv(slots * NBR + 2, P_SIZE) * P_SIZE
    partial, todo = pl.pallas_call(
        force_kernel,
        out_shape=(shape((3, slots, P_SIZE), f32), shape((todo_len,), jnp.int32)),
        in_specs=[VMEM] * 3 + [SMEM] * 3,
        out_specs=(VMEM, SMEM),
        scratch_shapes=[
            pltpu.VMEM((NBR, 8, P_SIZE), f32),
            pltpu.VMEM((5, P_SIZE, P_SIZE), f32),
            pltpu.VMEM((3, P_SIZE, P_SIZE), f32),
            pltpu.SMEM((8, P_SIZE), f32),
            pltpu.SMEM((8, P_SIZE), f32),
            pltpu.SemaphoreType.DMA((2,)),
        ],
        compiler_params=PARAMS,
        name="force",
    )(table, got_a, got_b, active_cells, active_count, neighbours)

    acceleration, arrivals = pl.pallas_call(
        functools.partial(finish_kernel, capacity),
        out_shape=(
            shape((3, slots, P_SIZE), f32),
            shape((STATE, devices * capacity), f32),
        ),
        in_specs=[VMEM] * 3 + [SMEM] * 3,
        out_specs=(VMEM, VMEM),
        scratch_shapes=[
            pltpu.VMEM((NBR, 8, P_SIZE), f32),
            pltpu.VMEM((3, P_SIZE, P_SIZE), f32),
        ],
        compiler_params=PARAMS,
        name="finish",
    )(table, partial, incoming, todo, neighbours, active_cells)
    return (new_density, acceleration, arrivals)


def solution(mesh):
    placed = (
        P(None, AXES, None),
        P(AXES, None),
        P(AXES, None),
        P(AXES, None),
        P(AXES, None),
        P(AXES),
        P(AXES),
        P(AXES, None),
        P(AXES),
        P(AXES, None),
    )
    return jax.shard_map(
        local,
        mesh=mesh,
        in_specs=placed,
        out_specs=(P(AXES, None), P(None, AXES, None), P(None, AXES)),
        check_vma=False,
    )
```

```python
import functools
import math

import jax
import jax.numpy as jnp
from jax import lax
from jax.experimental import pallas as pl
from jax.experimental.pallas import tpu as pltpu
from jax.sharding import PartitionSpec as P

P_SIZE = 128
NBR = 27
RIM = 64
STATE = 7
PLANES = 6
GROUP = 2
TINY = 1e-9
AXES = ("gx", "gy")

kernel_norm = 8.0 / math.pi
log_six_norm = math.log(6.0 * kernel_norm)
f32 = jnp.float32
bf16 = jnp.bfloat16
VMEM = pl.BlockSpec(memory_space=pltpu.VMEM)
SMEM = pl.BlockSpec(memory_space=pltpu.SMEM)
HBM = pl.BlockSpec(memory_space=pltpu.HBM)
PARAMS = pltpu.CompilerParams(vmem_limit_bytes=16 << 20)


def in_hbm(value):
    return pltpu.with_memory_space_constraint(value, pltpu.HBM)


def own_index():
    return lax.axis_index("gx") * lax.axis_size("gy") + lax.axis_index("gy")


def beta_of(inverse_len, entropy, density):
    power = 0.5 * (log_six_norm + jnp.log(entropy)) - jnp.log(density) * (1.0 / 6.0)
    return inverse_len * inverse_len * jnp.exp(power)


def row_sums(block):
    return jnp.sum(block.T, axis=0, keepdims=True)


def offset_tile(entry):
    row = lax.broadcasted_iota(jnp.int32, (8, P_SIZE), 0)
    shift = (entry // 9 - 1, entry // 3 % 3 - 1, entry % 3 - 1)
    tile = jnp.zeros((8, P_SIZE), f32)
    for axis in range(3):
        if shift[axis]:
            tile = jnp.where(row == axis, float(shift[axis]), tile)
    return tile


def split(value):
    high = value.astype(bf16).astype(f32)
    rest = value - high
    middle = rest.astype(bf16).astype(f32)
    return high, middle, rest - middle


def start_copies(pairs, sems):
    copies = [pltpu.make_async_copy(src, dst, sems.at[i]) for i, (src, dst) in enumerate(pairs)]
    for copy in copies:
        copy.start()
    return copies


def put(tab_ref, cell, count, row, plane):
    tab_ref[pl.ds(cell * 8 + row, count, stride=8), :] = plane


def tile_of(tab_ref, cell):
    return tab_ref[pl.ds(pl.multiple_of(cell * 8, 8), 8), :]


def put_table(tab_ref, cell, count, x, y, z, mass, inverse_len, beta):
    x, y, z = x - 0.5, y - 0.5, z - 0.5
    planes = (x, y, z, x * x, jnp.ones_like(x), mass, inverse_len, beta)
    for row, plane in enumerate(planes):
        put(tab_ref, cell, count, row, plane)


def pack_kernel(
    pos_hbm,
    mass_hbm,
    len_hbm,
    ent_hbm,
    rho_hbm,
    source_hbm,
    dest_hbm,
    act_hbm,
    cnt_ref,
    b_ref,
    a_ref,
    tab_ref,
    pos_ref,
    mass_ref,
    len_ref,
    ent_ref,
    rho_ref,
    source_ref,
    dest_ref,
    ih_ref,
    beta_ref,
    act_ref,
    sems,
):
    cells = mass_ref.shape[0]
    me = own_index()
    copies = start_copies(
        (
            (len_hbm, len_ref),
            (ent_hbm, ent_ref),
            (rho_hbm, rho_ref),
            (act_hbm, act_ref),
            (pos_hbm, pos_ref),
            (mass_hbm, mass_ref),
            (source_hbm, source_ref),
            (dest_hbm, dest_ref),
        ),
        sems,
    )
    for copy in copies:
        copy.wait()
    inverse_len = 1.0 / len_ref[...]
    ih_ref[...] = inverse_len
    beta_ref[...] = beta_of(inverse_len, ent_ref[...], rho_ref[...])
    lane = lax.broadcasted_iota(jnp.int32, (8, P_SIZE), 1)
    names = jnp.full((8, P_SIZE), -1.0, f32)
    for slot in range(act_ref.shape[0]):
        mine = act_ref[slot] - me * cells
        live = slot < cnt_ref[0]
        names = jnp.where(jnp.logical_and(lane == slot, live), mine.astype(f32), names)

        @pl.when(live)
        def _():
            beta_ref[pl.ds(mine, 1), :] = jnp.zeros((1, P_SIZE), f32)

    odd = me % 2
    start_a = pl.multiple_of((1 - odd) * (cells - RIM), RIM)
    start_b = pl.multiple_of(odd * (cells - RIM), RIM)
    for out_ref, start in ((b_ref, start_b), (a_ref, start_a)):
        rows = pl.ds(start, RIM)
        for axis in range(3):
            out_ref[pl.ds(axis * RIM, RIM), :] = pos_ref[axis, rows, :]
        out_ref[pl.ds(3 * RIM, RIM), :] = mass_ref[rows, :]
        out_ref[pl.ds(4 * RIM, RIM), :] = ih_ref[rows, :]
        out_ref[pl.ds(5 * RIM, RIM), :] = beta_ref[rows, :]
        out_ref[pl.ds(PLANES * RIM, 8), :] = names
    put_table(
        tab_ref,
        RIM,
        cells,
        pos_ref[0],
        pos_ref[1],
        pos_ref[2],
        mass_ref[...],
        ih_ref[...],
        beta_ref[...],
    )


def migrant_kernel(
    capacity,
    pos_ref,
    mass_ref,
    len_ref,
    ent_ref,
    rho_ref,
    source_ref,
    dest_ref,
    act_ref,
    cnt_ref,
    base_ref,
    code_ref,
    place_ref,
):
    cells = mass_ref.shape[0]
    me = own_index()
    targets = base_ref.shape[0]
    source = source_ref[...]
    cell_row = source // P_SIZE
    code_row = jnp.zeros_like(source)
    for slot in range(act_ref.shape[0]):
        mine = act_ref[slot] - me * cells
        named = jnp.logical_and(cell_row == mine, slot < cnt_ref[0])
        code_row = jnp.where(named, slot + 1, code_row)
    row_id = lax.broadcasted_iota(jnp.int32, (8, P_SIZE), 0)
    stack = jnp.zeros((8, P_SIZE), f32)
    for index, part in enumerate((cell_row, source % P_SIZE, dest_ref[...], code_row)):
        stack = jnp.where(row_id == index, part.astype(f32), stack)
    columns = stack.T
    shape = (P_SIZE, P_SIZE)
    cell, lane_of, dest, code = [jnp.broadcast_to(columns[:, i : i + 1], shape) for i in range(4)]
    lane = lax.broadcasted_iota(jnp.int32, shape, 1)
    row = lax.broadcasted_iota(jnp.int32, shape, 0)
    lane_f = lane.astype(f32)
    hit = lane_f == lane_of
    same = jnp.logical_and(dest == dest_ref[...].astype(f32), lane < row)
    rank = jnp.sum(jnp.where(same, 1.0, 0.0), axis=1, keepdims=True)
    wide = lax.broadcasted_iota(jnp.int32, (P_SIZE, cells), 1).astype(f32)
    pick = jnp.where(wide == columns[:, 0:1], 1.0, 0.0)
    spot = lane_f - rank
    sent = jnp.zeros(shape, f32)
    planes = [pos_ref[0], pos_ref[1], pos_ref[2], mass_ref[...], len_ref[...], ent_ref[...], rho_ref[...]]
    for index, plane in enumerate(planes):
        found = jnp.dot(pick, plane, precision=lax.Precision.HIGHEST, preferred_element_type=f32)
        keep = jnp.logical_and(hit, code == 0.0) if index == STATE - 1 else hit
        value = jnp.sum(jnp.where(keep, found, 0.0), axis=1, keepdims=True)
        sent = jnp.where(spot == float(index * capacity), value, sent)
    aim = lax.broadcasted_iota(jnp.int32, (targets, P_SIZE), 0) == dest_ref[...]
    aim = jnp.where(aim, 1.0, 0.0)
    base_ref[...] = jnp.dot(aim, sent, precision=lax.Precision.HIGHEST, preferred_element_type=f32)
    code_ref[...] = jnp.where(hit, code, 0.0)
    place_ref[...] = jnp.where(spot == float((STATE - 1) * capacity), 1.0, 0.0)


def neighbour_tile(tab_ref, cell, entry):
    row = lax.broadcasted_iota(jnp.int32, (8, P_SIZE), 0)
    tile = tile_of(tab_ref, cell) + offset_tile(entry)
    square = tile * tile
    length = square[0:1, :] + square[1:2, :] + square[2:3, :]
    return jnp.where(row == 3, length, tile)


def own_features(tile):
    row = lax.broadcasted_iota(jnp.int32, (8, P_SIZE), 0)
    square = tile * tile
    length = square[0:1, :] + square[1:2, :] + square[2:3, :]
    lead = jnp.where(row < 3, -2.0 * tile, jnp.where(row == 3, 1.0, jnp.where(row == 4, length, 0.0)))
    high, middle, low = split(lead)
    return jnp.concatenate([high, high, middle, middle, high, low], axis=0).T.astype(bf16)


def other_features(tile):
    high, middle, low = split(tile)
    return jnp.concatenate([high, middle, high, middle, low, high], axis=0).astype(bf16)


def groups():
    return [range(first, min(first + GROUP, NBR)) for first in range(0, NBR, GROUP)]


def density_kernel(
    rho_in,
    ent_ref,
    a_ref,
    b_ref,
    tab_in,
    base_ref,
    code_ref,
    place_ref,
    dest_ref,
    act_ref,
    cnt_ref,
    nbr_ref,
    new_ref,
    out_ref,
    tab_ref,
    near_ref,
    made_ref,
    beta_ref,
):
    cells = new_ref.shape[0]
    me = own_index()
    odd = me % 2
    start_of_a = (1 - odd) * (cells + RIM)
    for in_ref, start in ((a_ref, start_of_a), (b_ref, cells + RIM - start_of_a)):
        put_table(tab_ref, start, RIM, *[in_ref[pl.ds(i * RIM, RIM), :] for i in range(PLANES)])
    made_ref[...] = jnp.zeros_like(made_ref)
    beta_ref[...] = jnp.zeros_like(beta_ref)
    base = me * cells - RIM

    @pl.loop(0, cnt_ref[0])
    def _(slot):
        mine = act_ref[slot] - me * cells
        own = tile_of(tab_ref, RIM + mine)
        left = own_features(own)
        scale = jnp.broadcast_to(own.T[:, 6:7], (P_SIZE, P_SIZE))
        total = jnp.zeros((P_SIZE, P_SIZE), f32)
        for group in groups():
            parts = []
            for entry in group:
                tile = neighbour_tile(tab_ref, nbr_ref[slot, entry] - base, entry)
                near_ref[pl.ds(pl.multiple_of((slot * NBR + entry) * 8, 8), 8), :] = tile
                parts.append(other_features(tile))
            squares = jnp.dot(left, jnp.concatenate(parts, axis=1), preferred_element_type=f32)
            for place, entry in enumerate(group):
                square = jnp.maximum(squares[:, place * P_SIZE : (place + 1) * P_SIZE], TINY)
                mass = near_ref[pl.ds((slot * NBR + entry) * 8 + 5, 1), :]
                ratio = square * lax.rsqrt(square) * scale
                outer = jnp.maximum(1.0 - ratio, 0.0)
                inner = jnp.maximum(0.5 - ratio, 0.0)
                weight = outer * outer * outer - 4.0 * (inner * inner * inner)
                total = total + weight * mass
        inverse_len = own[6:7, :]
        made = row_sums(total) * (2.0 * kernel_norm) * inverse_len * inverse_len * inverse_len
        beta = beta_of(inverse_len, ent_ref[pl.ds(mine, 1), :], made)
        new_ref[pl.ds(mine, 1), :] = made
        tab_ref[pl.ds((RIM + mine) * 8 + 7, 1), :] = beta
        made_ref[pl.ds(slot, 1), :] = made
        beta_ref[pl.ds(slot, 1), :] = beta

    code = code_ref[...]
    chosen = jnp.zeros_like(code)
    slots = act_ref.shape[0]
    for slot in range(slots):
        chosen = jnp.where(code == float(slot + 1), made_ref[slot : slot + 1, :], chosen)
    late = place_ref[...] * jnp.sum(chosen, axis=1, keepdims=True)
    targets = base_ref.shape[0]
    aim = lax.broadcasted_iota(jnp.int32, (targets, P_SIZE), 0) == dest_ref[...]
    aim = jnp.where(aim, 1.0, 0.0)
    sent = base_ref[...] + jnp.dot(
        aim, late, precision=lax.Precision.HIGHEST, preferred_element_type=f32
    )
    put(out_ref, 0, targets, 0, sent)
    for row in range(1, 8):
        fill = jnp.zeros((1, P_SIZE), f32) if row > slots else beta_ref[row - 1 : row, :]
        put(out_ref, 0, targets, row, jnp.broadcast_to(fill, (targets, P_SIZE)))


def spline(base, slope, distance):
    step = distance * slope
    near = base - step
    outer = jnp.maximum(near, 0.0)
    inner = jnp.maximum(near - step, 0.0)
    return outer * outer - inner * inner


def force_kernel(
    tab_ref,
    near_ref,
    a_ref,
    b_ref,
    new_ref,
    act_ref,
    cnt_ref,
    nbr_ref,
    acc_out,
    list_ref,
    new_out,
    high_ref,
    low_ref,
    names_a,
    names_b,
    sems,
):
    cells = tab_ref.shape[0] // 8 - 2 * RIM
    me = own_index()
    odd = me % 2
    base = me * cells - RIM
    slots = act_ref.shape[0]
    copies = start_copies(
        [
            (ref.at[pl.ds(PLANES * RIM, 8), :], names)
            for ref, names in ((a_ref, names_a), (b_ref, names_b))
        ]
        + [(new_ref, new_out)],
        sems,
    )
    acc_out[...] = jnp.zeros_like(acc_out)
    list_ref[0] = 0
    for copy in copies[:2]:
        copy.wait()
    fa = [names_a[0, s].astype(jnp.int32) for s in range(slots)]
    fb = [names_b[0, s].astype(jnp.int32) for s in range(slots)]
    left = [jnp.where(odd == 1, fa[s], fb[s]) for s in range(slots)]
    right = [jnp.where(odd == 1, fb[s], fa[s]) for s in range(slots)]
    left = [jnp.where(v >= cells - RIM, v - (cells - RIM), -1) for v in left]
    right = [jnp.where(jnp.logical_and(v >= 0, v < RIM), v + cells + RIM, -1) for v in right]
    row = lax.broadcasted_iota(jnp.int32, (8, P_SIZE), 0)

    @pl.loop(0, cnt_ref[0])
    def _(slot):
        mine = act_ref[slot] - me * cells
        own = tile_of(tab_ref, RIM + mine)
        columns = own.T
        own_base = jnp.broadcast_to(columns[:, 7:8], (P_SIZE, P_SIZE))
        own_slope = own_base * jnp.broadcast_to(columns[:, 6:7], (P_SIZE, P_SIZE))
        left_side = own_features(own)
        parts = []
        for group in groups():
            tiles = [
                near_ref[pl.ds(pl.multiple_of((slot * NBR + entry) * 8, 8), 8), :] for entry in group
            ]
            other = jnp.concatenate([other_features(tile) for tile in tiles], axis=1)
            squares = jnp.dot(left_side, other, preferred_element_type=f32)
            for place, entry in enumerate(group):
                near = tiles[place]
                cell = nbr_ref[slot, entry] - base
                found = jnp.int32(-1)
                for s in range(slots):
                    found = jnp.where(cell == left[s], s, found)
                    found = jnp.where(cell == right[s], slots + s, found)
                at = list_ref[0]
                list_ref[at + 1] = (slot * NBR + entry) * (2 * slots) + found
                list_ref[0] = at + jnp.where(found >= 0, 1, 0)

                beta = tab_ref[pl.ds(cell * 8 + 7, 1), :]
                slope = beta * near[6:7, :]
                square = jnp.maximum(squares[:, place * P_SIZE : (place + 1) * P_SIZE], TINY)
                inverse = lax.rsqrt(square)
                distance = square * inverse
                pull = spline(own_base, own_slope, distance) + spline(beta, slope, distance)
                pull = pull * inverse
                high = pull.astype(bf16)
                high_ref[:, pl.ds(entry * P_SIZE, P_SIZE)] = high
                low_ref[:, pl.ds(entry * P_SIZE, P_SIZE)] = (pull - high.astype(f32)).astype(bf16)
                weighed = jnp.where(row < 3, near, 1.0) * near[5:6, :]
                parts.append(jnp.concatenate(split(weighed), axis=0).astype(bf16))
        right_side = jnp.concatenate(parts, axis=1)
        dims = (((1,), (1,)), ((), ()))
        sums = lax.dot_general(high_ref[...], right_side, dims, preferred_element_type=f32)
        sums = sums + lax.dot_general(low_ref[...], right_side, dims, preferred_element_type=f32)
        flat = sums.T
        flat = flat[0:8, :] + flat[8:16, :] + flat[16:24, :]
        made = own * flat[3:4, :] - flat
        for axis in range(3):
            acc_out[axis, pl.ds(slot, 1), :] = made[axis : axis + 1, :]

    copies[2].wait()


def finish_kernel(
    capacity,
    tab_ref,
    near_ref,
    part_ref,
    got_ref,
    list_ref,
    act_ref,
    acc_out,
    arrive_ref,
):
    cells = tab_ref.shape[0] // 8 - 2 * RIM
    me = own_index()
    slots = act_ref.shape[0]
    targets = got_ref.shape[0] // 8
    acc_out[...] = part_ref[...]
    rows = got_ref[pl.ds(0, targets, stride=8), :]
    width = targets * capacity
    column = lax.broadcasted_iota(jnp.int32, (P_SIZE, width), 1)
    lane = lax.broadcasted_iota(jnp.int32, (P_SIZE, width), 0)
    spot = lane - column % capacity
    sender = lax.broadcasted_iota(jnp.int32, (targets, width), 1) // capacity
    mask = sender == lax.broadcasted_iota(jnp.int32, (targets, width), 0)
    pieces = jnp.concatenate(split(rows), axis=0).astype(bf16)
    for index in range(STATE):
        pick = jnp.where(spot == index * capacity, 1.0, 0.0).astype(bf16)
        spread = jnp.dot(pieces, pick, preferred_element_type=f32)
        spread = spread[0:targets] + spread[targets : 2 * targets] + spread[2 * targets :]
        arrive_ref[index : index + 1, :] = jnp.sum(
            jnp.where(mask, spread, 0.0), axis=0, keepdims=True
        )

    @pl.loop(0, list_ref[0])
    def _(item):
        word = list_ref[item + 1]
        found = word % (2 * slots)
        place = word // (2 * slots)
        slot = place // NBR
        other = jnp.where(found < slots, me - 1, me + 1)
        near = near_ref[pl.ds(pl.multiple_of(place * 8, 8), 8), :]
        beta = got_ref[pl.ds(other * 8 + 1 + found % slots, 1), :]
        slope = beta * near[6:7, :]
        columns = tile_of(tab_ref, RIM + act_ref[slot] - me * cells).T
        apart = [
            jnp.broadcast_to(columns[:, axis : axis + 1], (P_SIZE, P_SIZE)) - near[axis : axis + 1, :]
            for axis in range(3)
        ]
        square = apart[0] * apart[0] + apart[1] * apart[1] + apart[2] * apart[2]
        square = jnp.maximum(square, TINY)
        inverse = lax.rsqrt(square)
        pull = spline(beta, slope, square * inverse) * inverse * near[5:6, :]
        for axis in range(3):
            acc_out[axis, pl.ds(slot, 1), :] += row_sums(pull * apart[axis])


def local(
    positions,
    masses,
    smoothing,
    entropy,
    density,
    active_cells,
    active_count,
    neighbours,
    mig_source,
    mig_dest,
):
    cells = masses.shape[0]
    slots = active_cells.shape[0]
    devices = lax.axis_size(AXES)
    mig_rows = mig_source.shape[0]
    capacity = max(2, 2 * mig_rows // devices)
    shape = jax.ShapeDtypeStruct
    rim_shape = shape((PLANES * RIM + 8, P_SIZE), f32)
    tab_shape = pltpu.VMEM(((cells + 2 * RIM) * 8, P_SIZE), f32)
    near_shape = pltpu.VMEM((slots * NBR * 8, P_SIZE), f32)
    fields = (positions, masses, smoothing, entropy, density)
    rows = (mig_source.reshape(1, mig_rows), mig_dest.reshape(1, mig_rows))

    send_b, send_a, table, *held = pl.pallas_call(
        pack_kernel,
        out_shape=(rim_shape, rim_shape, tab_shape)
        + tuple(pltpu.VMEM(v.shape, v.dtype) for v in fields + rows),
        in_specs=[HBM] * 8 + [SMEM],
        out_specs=(VMEM,) * 10,
        scratch_shapes=[
            pltpu.VMEM((cells, P_SIZE), f32),
            pltpu.VMEM((cells, P_SIZE), f32),
            pltpu.SMEM((slots,), jnp.int32),
            pltpu.SemaphoreType.DMA((8,)),
        ],
        compiler_params=PARAMS,
        name="pack",
    )(*[in_hbm(v) for v in (*fields, *rows, active_cells)], active_count)
    dest = held[6]

    pairs_a = [(i ^ 1, i) for i in range(devices) if i ^ 1 < devices]
    pairs_b = []
    for i in range(1, devices - 1, 2):
        pairs_b += [(i, i + 1), (i + 1, i)]
    got_b = lax.ppermute(send_b, AXES, pairs_b)
    got_a = lax.ppermute(send_a, AXES, pairs_a)

    base, code, place = pl.pallas_call(
        functools.partial(migrant_kernel, capacity),
        out_shape=(
            shape((devices, P_SIZE), f32),
            shape((mig_rows, P_SIZE), f32),
            shape((mig_rows, P_SIZE), f32),
        ),
        in_specs=[VMEM] * 7 + [SMEM] * 2,
        out_specs=(VMEM,) * 3,
        compiler_params=PARAMS,
        name="migrants",
    )(*held, active_cells, active_count)

    made, outgoing, table, near = pl.pallas_call(
        density_kernel,
        out_shape=(
            pltpu.VMEM((cells, P_SIZE), f32),
            shape((devices * 8, P_SIZE), f32),
            tab_shape,
            near_shape,
        ),
        in_specs=[VMEM] * 9 + [SMEM] * 3,
        out_specs=(VMEM,) * 4,
        input_output_aliases={0: 0, 4: 2},
        scratch_shapes=[
            pltpu.VMEM((8, P_SIZE), f32),
            pltpu.VMEM((8, P_SIZE), f32),
        ],
        compiler_params=PARAMS,
        name="density",
    )(held[4], held[3], got_a, got_b, table, base, code, place, dest, active_cells, active_count, neighbours)

    incoming = lax.all_to_all(outgoing, AXES, split_axis=0, concat_axis=0, tiled=True)

    todo_len = pl.cdiv(slots * NBR + 2, P_SIZE) * P_SIZE
    partial, todo, new_density = pl.pallas_call(
        force_kernel,
        out_shape=(
            shape((3, slots, P_SIZE), f32),
            shape((todo_len,), jnp.int32),
            shape((cells, P_SIZE), f32),
        ),
        in_specs=[VMEM] * 5 + [SMEM] * 3,
        out_specs=(VMEM, SMEM, HBM),
        scratch_shapes=[
            pltpu.VMEM((P_SIZE, NBR * P_SIZE), bf16),
            pltpu.VMEM((P_SIZE, NBR * P_SIZE), bf16),
            pltpu.SMEM((8, P_SIZE), f32),
            pltpu.SMEM((8, P_SIZE), f32),
            pltpu.SemaphoreType.DMA((3,)),
        ],
        compiler_params=PARAMS,
        name="force",
    )(table, near, got_a, got_b, made, active_cells, active_count, neighbours)

    acceleration, arrivals = pl.pallas_call(
        functools.partial(finish_kernel, capacity),
        out_shape=(
            shape((3, slots, P_SIZE), f32),
            shape((STATE, devices * capacity), f32),
        ),
        in_specs=[VMEM] * 4 + [SMEM] * 2,
        out_specs=(VMEM, VMEM),
        compiler_params=PARAMS,
        name="finish",
    )(table, near, partial, incoming, todo, active_cells)
    return (new_density, acceleration, arrivals)


def solution(mesh):
    placed = (
        P(None, AXES, None),
        P(AXES, None),
        P(AXES, None),
        P(AXES, None),
        P(AXES, None),
        P(AXES),
        P(AXES),
        P(AXES, None),
        P(AXES),
        P(AXES, None),
    )
    return jax.shard_map(
        local,
        mesh=mesh,
        in_specs=placed,
        out_specs=(P(AXES, None), P(None, AXES, None), P(None, AXES)),
        check_vma=False,
    )
```

```python
import functools
import math

import jax
import jax.numpy as jnp
from jax import lax
from jax.experimental import pallas as pl
from jax.experimental.pallas import tpu as pltpu
from jax.sharding import PartitionSpec as P

P_SIZE = 128
NBR = 27
RIM = 64
STATE = 7
PLANES = 6
SUM_GROUP = 8
TINY = 1e-10
AXES = ("gx", "gy")

kernel_norm = 8.0 / math.pi
log_six_norm = math.log(6.0 * kernel_norm)
f32 = jnp.float32
bf16 = jnp.bfloat16
VMEM = pl.BlockSpec(memory_space=pltpu.VMEM)
SMEM = pl.BlockSpec(memory_space=pltpu.SMEM)
HBM = pl.BlockSpec(memory_space=pltpu.HBM)
PARAMS = pltpu.CompilerParams(vmem_limit_bytes=16 << 20)


def in_hbm(value):
    return pltpu.with_memory_space_constraint(value, pltpu.HBM)


def own_index():
    return lax.axis_index("gx") * lax.axis_size("gy") + lax.axis_index("gy")


def beta_of(inverse_len, entropy, density):
    power = 0.5 * (log_six_norm + jnp.log(entropy)) - jnp.log(density) * (1.0 / 6.0)
    return inverse_len * inverse_len * jnp.exp(power)


def row_sums(block):
    return jnp.sum(block.T, axis=0, keepdims=True)


def offset_tile(entry):
    row = lax.broadcasted_iota(jnp.int32, (8, P_SIZE), 0)
    shift = (entry // 9 - 1, entry // 3 % 3 - 1, entry % 3 - 1)
    tile = jnp.zeros((8, P_SIZE), f32)
    for axis in range(3):
        if shift[axis]:
            tile = jnp.where(row == axis, float(shift[axis]), tile)
    return tile


def split(value):
    high = value.astype(bf16).astype(f32)
    rest = value - high
    middle = rest.astype(bf16).astype(f32)
    return high, middle, rest - middle


def start_copies(pairs, sems):
    copies = [pltpu.make_async_copy(src, dst, sems.at[i]) for i, (src, dst) in enumerate(pairs)]
    for copy in copies:
        copy.start()
    return copies


def put(tab_ref, cell, count, row, plane):
    tab_ref[pl.ds(cell * 8 + row, count, stride=8), :] = plane


def tile_of(tab_ref, cell):
    return tab_ref[pl.ds(pl.multiple_of(cell * 8, 8), 8), :]


def put_table(tab_ref, cell, count, x, y, z, mass, inverse_len, beta):
    cube_root = jnp.exp(jnp.log(mass) * (1.0 / 3.0))
    planes = (x - 0.5, y - 0.5, z - 0.5, mass, cube_root, mass, inverse_len, beta)
    for row, plane in enumerate(planes):
        put(tab_ref, cell, count, row, plane)


def pack_kernel(
    pos_hbm,
    mass_hbm,
    len_hbm,
    ent_hbm,
    rho_hbm,
    source_hbm,
    dest_hbm,
    act_hbm,
    nbr_hbm,
    cnt_ref,
    b_ref,
    a_ref,
    pos_ref,
    mass_ref,
    len_ref,
    ent_ref,
    rho_ref,
    source_ref,
    dest_ref,
    act_ref,
    nbr_ref,
    sems,
):
    cells = mass_ref.shape[0]
    me = own_index()
    copies = start_copies(
        (
            (act_hbm, act_ref),
            (len_hbm, len_ref),
            (ent_hbm, ent_ref),
            (rho_hbm, rho_ref),
            (pos_hbm, pos_ref),
            (mass_hbm, mass_ref),
            (source_hbm, source_ref),
            (dest_hbm, dest_ref),
            (nbr_hbm, nbr_ref),
        ),
        sems,
    )
    for copy in copies[:6]:
        copy.wait()
    odd = me % 2
    start_a = pl.multiple_of((1 - odd) * (cells - RIM), RIM)
    start_b = pl.multiple_of(odd * (cells - RIM), RIM)
    lane = lax.broadcasted_iota(jnp.int32, (8, P_SIZE), 1)
    names = jnp.full((8, P_SIZE), -1.0, f32)
    slots = act_ref.shape[0]
    for slot in range(slots):
        mine = act_ref[slot] - me * cells
        live = slot < cnt_ref[0]
        names = jnp.where(jnp.logical_and(lane == slot, live), mine.astype(f32), names)
    cell = lax.broadcasted_iota(jnp.int32, (RIM, P_SIZE), 0)
    for out_ref, start in ((b_ref, start_b), (a_ref, start_a)):
        rows = pl.ds(start, RIM)
        for axis in range(3):
            out_ref[pl.ds(axis * RIM, RIM), :] = pos_ref[axis, rows, :]
        inverse_len = 1.0 / len_ref[rows, :]
        beta = beta_of(inverse_len, ent_ref[rows, :], rho_ref[rows, :])
        for slot in range(slots):
            mine = jnp.where(slot < cnt_ref[0], act_ref[slot] - me * cells - start, -1)
            beta = jnp.where(cell == mine, 0.0, beta)
        out_ref[pl.ds(3 * RIM, RIM), :] = mass_ref[rows, :]
        out_ref[pl.ds(4 * RIM, RIM), :] = inverse_len
        out_ref[pl.ds(5 * RIM, RIM), :] = beta
        out_ref[pl.ds(PLANES * RIM, 8), :] = names
    for copy in copies[6:]:
        copy.wait()


def migrant_kernel(
    capacity,
    pos_ref,
    mass_ref,
    len_ref,
    ent_ref,
    rho_ref,
    source_ref,
    dest_ref,
    act_ref,
    cnt_ref,
    tab_ref,
    base_ref,
    code_ref,
    place_ref,
    pick_ref,
):
    cells = mass_ref.shape[0]
    me = own_index()
    targets = base_ref.shape[0]
    inverse_len = 1.0 / len_ref[...]
    beta = beta_of(inverse_len, ent_ref[...], rho_ref[...])
    put_table(
        tab_ref, RIM, cells, pos_ref[0], pos_ref[1], pos_ref[2], mass_ref[...], inverse_len, beta
    )
    source = source_ref[...]
    cell_row = source // P_SIZE
    code_row = jnp.zeros_like(source)
    for slot in range(act_ref.shape[0]):
        mine = act_ref[slot] - me * cells
        named = jnp.logical_and(cell_row == mine, slot < cnt_ref[0])
        code_row = jnp.where(named, slot + 1, code_row)
    row_id = lax.broadcasted_iota(jnp.int32, (8, P_SIZE), 0)
    stack = jnp.zeros((8, P_SIZE), f32)
    for index, part in enumerate((cell_row, source % P_SIZE, dest_ref[...], code_row)):
        stack = jnp.where(row_id == index, part.astype(f32), stack)
    columns = stack.T
    shape = (P_SIZE, P_SIZE)
    cell, lane_of, dest, code = [jnp.broadcast_to(columns[:, i : i + 1], shape) for i in range(4)]
    lane = lax.broadcasted_iota(jnp.int32, shape, 1)
    row = lax.broadcasted_iota(jnp.int32, shape, 0)
    lane_f = lane.astype(f32)
    hit = lane_f == lane_of
    same = jnp.logical_and(dest == dest_ref[...].astype(f32), lane < row)
    rank = jnp.sum(jnp.where(same, 1.0, 0.0), axis=1, keepdims=True)
    wide = lax.broadcasted_iota(jnp.int32, (P_SIZE, cells), 1).astype(f32)
    pick = jnp.where(wide == columns[:, 0:1], 1.0, 0.0)
    spot = lane_f - rank
    sent = jnp.zeros(shape, f32)
    planes = [pos_ref[0], pos_ref[1], pos_ref[2], mass_ref[...], len_ref[...], ent_ref[...], rho_ref[...]]
    for index, plane in enumerate(planes):
        found = jnp.dot(pick, plane, precision=lax.Precision.HIGHEST, preferred_element_type=f32)
        keep = jnp.logical_and(hit, code == 0.0) if index == STATE - 1 else hit
        value = jnp.sum(jnp.where(keep, found, 0.0), axis=1, keepdims=True)
        sent = jnp.where(spot == float(index * capacity), value, sent)
    aim = lax.broadcasted_iota(jnp.int32, (targets, P_SIZE), 0) == dest_ref[...]
    aim = jnp.where(aim, 1.0, 0.0)
    base_ref[...] = jnp.dot(aim, sent, precision=lax.Precision.HIGHEST, preferred_element_type=f32)
    code_ref[...] = jnp.where(hit, code, 0.0)
    place_ref[...] = jnp.where(spot == float((STATE - 1) * capacity), 1.0, 0.0)
    width = targets * capacity
    column = lax.broadcasted_iota(jnp.int32, (P_SIZE, width), 1)
    spot_of = lax.broadcasted_iota(jnp.int32, (P_SIZE, width), 0) - column % capacity
    for index in range(STATE):
        hit = jnp.where(spot_of == index * capacity, 1.0, 0.0)
        pick_ref[:, pl.ds(index * width, width)] = hit.astype(bf16)


def squared_length(tile):
    square = tile * tile
    return square[0:1, :] + square[1:2, :] + square[2:3, :]


def row_ids():
    return lax.broadcasted_iota(jnp.int32, (8, P_SIZE), 0)


def own_features(tile, scale):
    row = row_ids()
    lead = jnp.where(row < 3, -2.0 * tile, 1.0)
    lead = jnp.where(row == 4, squared_length(tile), lead)
    lead = jnp.where(row < 5, lead * scale, 0.0)
    high, middle, low = split(lead)
    return jnp.concatenate([high, high, middle, middle, high, low], axis=0).T.astype(bf16)


def other_features(tile):
    high, middle, low = split(tile)
    return jnp.concatenate([high, middle, high, middle, low, high], axis=0).astype(bf16)


def groups(size):
    return [range(first, min(first + size, NBR)) for first in range(0, NBR, size)]


def density_kernel(
    rho_in,
    ent_ref,
    a_ref,
    b_ref,
    tab_in,
    base_ref,
    code_ref,
    place_ref,
    dest_ref,
    act_ref,
    cnt_ref,
    nbr_ref,
    new_ref,
    out_ref,
    tab_ref,
    near_ref,
    names_a,
    names_b,
    made_ref,
    beta_ref,
    sems,
):
    cells = new_ref.shape[0]
    slots = act_ref.shape[0]
    me = own_index()
    odd = me % 2
    copies = start_copies(
        [
            (ref.at[pl.ds(PLANES * RIM, 8), :], names)
            for ref, names in ((a_ref, names_a), (b_ref, names_b))
        ],
        sems,
    )
    start_of_a = (1 - odd) * (cells + RIM)
    for in_ref, start in ((a_ref, start_of_a), (b_ref, cells + RIM - start_of_a)):
        put_table(tab_ref, start, RIM, *[in_ref[pl.ds(i * RIM, RIM), :] for i in range(PLANES)])
    base = me * cells - RIM
    row = row_ids()
    for slot in range(slots):
        mine = act_ref[slot] - me * cells
        own = tile_of(tab_ref, RIM + mine)
        inverse_len = own[6:7, :]
        left = own_features(own, inverse_len * inverse_len)
        outer_sum = jnp.zeros((P_SIZE, P_SIZE), f32)
        inner_sum = jnp.zeros((P_SIZE, P_SIZE), f32)
        for group in groups(2):
            parts = []
            roots = []
            for entry in group:
                tile = tile_of(tab_ref, nbr_ref[slot, entry] - base) + offset_tile(entry)
                tile = jnp.where(row == 3, squared_length(tile), tile)
                root = tile[4:5, :]
                tile_one = jnp.where(row == 4, 1.0, tile)
                near_ref[pl.ds((slot * NBR + entry) * 8, 8), :] = tile_one
                parts.append(other_features(tile_one * (root * root)))
                roots.append(root)
            squares = jnp.dot(left, jnp.concatenate(parts, axis=1), preferred_element_type=f32)
            for place, root in enumerate(roots):
                square = jnp.maximum(squares[:, place * P_SIZE : (place + 1) * P_SIZE], TINY)
                ratio = square * lax.rsqrt(square)
                outer = jnp.maximum(root - ratio, 0.0)
                inner = jnp.maximum(0.5 * root - ratio, 0.0)
                outer_sum = outer_sum + outer * outer * outer
                inner_sum = inner_sum + inner * inner * inner
        total = outer_sum - 4.0 * inner_sum
        made = row_sums(total) * (2.0 * kernel_norm) * inverse_len * inverse_len * inverse_len
        made = jnp.where(slot < cnt_ref[0], made, new_ref[pl.ds(mine, 1), :])
        beta = beta_of(inverse_len, ent_ref[pl.ds(mine, 1), :], made)
        made_ref[slot : slot + 1, :] = made
        beta_ref[slot : slot + 1, :] = beta

    for slot in range(slots):
        mine = act_ref[slot] - me * cells
        new_ref[pl.ds(mine, 1), :] = made_ref[slot : slot + 1, :]
        tab_ref[pl.ds((RIM + mine) * 8 + 7, 1), :] = beta_ref[slot : slot + 1, :]
    code = code_ref[...]
    chosen = jnp.zeros_like(code)
    for slot in range(slots):
        chosen = jnp.where(code == float(slot + 1), made_ref[slot : slot + 1, :], chosen)
    late = place_ref[...] * jnp.sum(chosen, axis=1, keepdims=True)
    targets = base_ref.shape[0]
    aim = lax.broadcasted_iota(jnp.int32, (targets, P_SIZE), 0) == dest_ref[...]
    aim = jnp.where(aim, 1.0, 0.0)
    for line in range(1, 8):
        fill = jnp.zeros((1, P_SIZE), f32) if line > slots else beta_ref[line - 1 : line, :]
        put(out_ref, 0, targets, line, jnp.broadcast_to(fill, (targets, P_SIZE)))
    sent = base_ref[...] + jnp.dot(
        aim, late, precision=lax.Precision.HIGHEST, preferred_element_type=f32
    )
    put(out_ref, 0, targets, 0, sent)
    for copy in copies:
        copy.wait()


def spline(base, slope, distance):
    step = distance * slope
    outer = jnp.maximum(base - step, 0.0)
    least = jnp.minimum(step, outer)
    return least * (outer + (outer - least))


def force_kernel(
    tab_ref,
    near_ref,
    new_ref,
    names_a,
    names_b,
    act_ref,
    cnt_ref,
    nbr_ref,
    acc_out,
    list_ref,
    new_out,
    high_ref,
    low_ref,
    sems,
):
    cells = tab_ref.shape[0] // 8 - 2 * RIM
    me = own_index()
    odd = me % 2
    base = me * cells - RIM
    slots = act_ref.shape[0]
    copies = start_copies([(new_ref, new_out)], sems)
    fa = [names_a[0, s].astype(jnp.int32) for s in range(slots)]
    fb = [names_b[0, s].astype(jnp.int32) for s in range(slots)]
    left = [jnp.where(odd == 1, fa[s], fb[s]) for s in range(slots)]
    right = [jnp.where(odd == 1, fb[s], fa[s]) for s in range(slots)]
    left = [jnp.where(v >= cells - RIM, v - (cells - RIM), -1) for v in left]
    right = [jnp.where(jnp.logical_and(v >= 0, v < RIM), v + cells + RIM, -1) for v in right]
    row = row_ids()
    dims = (((1,), (1,)), ((), ()))
    at = jnp.int32(0)
    for slot in range(slots):
        live = slot < cnt_ref[0]
        mine = act_ref[slot] - me * cells
        own = tile_of(tab_ref, RIM + mine)
        columns = own.T
        own_base = jnp.broadcast_to(columns[:, 7:8], (P_SIZE, P_SIZE))
        own_slope = own_base * jnp.broadcast_to(columns[:, 6:7], (P_SIZE, P_SIZE))
        left_side = own_features(own, 1.0)
        sums = jnp.zeros((P_SIZE, 24), f32)
        for block in groups(SUM_GROUP):
            parts = []
            for first in range(block.start, block.stop, 2):
                group = range(first, min(first + 2, block.stop))
                tiles = [near_ref[pl.ds((slot * NBR + entry) * 8, 8), :] for entry in group]
                other = jnp.concatenate([other_features(tile) for tile in tiles], axis=1)
                squares = jnp.dot(left_side, other, preferred_element_type=f32)
                for place, entry in enumerate(group):
                    near = tiles[place]
                    cell = nbr_ref[slot, entry] - base
                    found = jnp.int32(-1)
                    for s in range(slots):
                        found = jnp.where(cell == left[s], s, found)
                        found = jnp.where(cell == right[s], slots + s, found)
                    list_ref[at + 1] = (slot * NBR + entry) * (2 * slots) + found
                    at = at + jnp.where(jnp.logical_and(found >= 0, live), 1, 0)

                    beta = tab_ref[pl.ds(cell * 8 + 7, 1), :]
                    slope = beta * near[6:7, :]
                    square = jnp.maximum(squares[:, place * P_SIZE : (place + 1) * P_SIZE], TINY)
                    inverse = lax.rsqrt(square)
                    distance = square * inverse
                    pull = spline(own_base, own_slope, distance) + spline(beta, slope, distance)
                    pull = pull * inverse
                    high = pull.astype(bf16)
                    place_of = pl.ds((slot * NBR + entry) * P_SIZE, P_SIZE)
                    high_ref[:, place_of] = high
                    low_ref[:, place_of] = (pull - high.astype(f32)).astype(bf16)
                    weighed = jnp.where(row < 3, near, 1.0) * near[5:6, :]
                    parts.append(jnp.concatenate(split(weighed), axis=0).astype(bf16))
            right_side = jnp.concatenate(parts, axis=1)
            span = pl.ds((slot * NBR + block.start) * P_SIZE, len(block) * P_SIZE)
            for ref in (high_ref, low_ref):
                sums = sums + lax.dot_general(
                    ref[:, span], right_side, dims, preferred_element_type=f32
                )
        flat = sums.T
        flat = flat[0:8, :] + flat[8:16, :] + flat[16:24, :]
        made = jnp.where(live, own * flat[3:4, :] - flat, 0.0)
        for axis in range(3):
            acc_out[axis, slot : slot + 1, :] = made[axis : axis + 1, :]
    list_ref[0] = at
    for copy in copies:
        copy.wait()


def finish_kernel(
    capacity,
    tab_ref,
    near_ref,
    part_ref,
    got_ref,
    pick_ref,
    list_ref,
    act_ref,
    acc_out,
    arrive_ref,
):
    cells = tab_ref.shape[0] // 8 - 2 * RIM
    me = own_index()
    slots = act_ref.shape[0]
    targets = got_ref.shape[0] // 8
    acc_out[...] = part_ref[...]
    rows = got_ref[pl.ds(0, targets, stride=8), :]
    width = targets * capacity
    sender = lax.broadcasted_iota(jnp.int32, (targets, width), 1) // capacity
    mask = sender == lax.broadcasted_iota(jnp.int32, (targets, width), 0)
    pieces = jnp.concatenate(split(rows), axis=0).astype(bf16)
    spread = jnp.dot(pieces, pick_ref[...], preferred_element_type=f32)
    spread = spread[0:targets] + spread[targets : 2 * targets] + spread[2 * targets :]
    for index in range(STATE):
        part = spread[:, index * width : (index + 1) * width]
        arrive_ref[index : index + 1, :] = jnp.sum(jnp.where(mask, part, 0.0), axis=0, keepdims=True)

    @pl.loop(0, list_ref[0])
    def _(item):
        word = list_ref[item + 1]
        found = word % (2 * slots)
        place = word // (2 * slots)
        slot = place // NBR
        other = jnp.where(found < slots, me - 1, me + 1)
        near = near_ref[pl.ds(pl.multiple_of(place * 8, 8), 8), :]
        beta = got_ref[pl.ds(other * 8 + 1 + found % slots, 1), :]
        slope = beta * near[6:7, :]
        columns = tile_of(tab_ref, RIM + act_ref[slot] - me * cells).T
        apart = [
            jnp.broadcast_to(columns[:, axis : axis + 1], (P_SIZE, P_SIZE)) - near[axis : axis + 1, :]
            for axis in range(3)
        ]
        square = apart[0] * apart[0] + apart[1] * apart[1] + apart[2] * apart[2]
        square = jnp.maximum(square, TINY)
        inverse = lax.rsqrt(square)
        pull = spline(beta, slope, square * inverse) * inverse * near[5:6, :]
        for axis in range(3):
            acc_out[axis, pl.ds(slot, 1), :] += row_sums(pull * apart[axis])


def local(
    positions,
    masses,
    smoothing,
    entropy,
    density,
    active_cells,
    active_count,
    neighbours,
    mig_source,
    mig_dest,
):
    cells = masses.shape[0]
    slots = active_cells.shape[0]
    devices = lax.axis_size(AXES)
    mig_rows = mig_source.shape[0]
    capacity = max(2, 2 * mig_rows // devices)
    shape = jax.ShapeDtypeStruct
    rim_shape = shape((PLANES * RIM + 8, P_SIZE), f32)
    tab_shape = pltpu.VMEM(((cells + 2 * RIM) * 8, P_SIZE), f32)
    near_shape = pltpu.VMEM((slots * NBR * 8, P_SIZE), f32)
    name_shape = pltpu.SMEM((8, P_SIZE), f32)
    fields = (positions, masses, smoothing, entropy, density)
    rows = (mig_source.reshape(1, mig_rows), mig_dest.reshape(1, mig_rows))
    lists = (active_cells, neighbours)

    send_b, send_a, *held = pl.pallas_call(
        pack_kernel,
        out_shape=(rim_shape, rim_shape)
        + tuple(pltpu.VMEM(v.shape, v.dtype) for v in fields + rows)
        + tuple(pltpu.SMEM(v.shape, v.dtype) for v in lists),
        in_specs=[HBM] * 9 + [SMEM],
        out_specs=(VMEM,) * 9 + (SMEM,) * 2,
        scratch_shapes=[pltpu.SemaphoreType.DMA((9,))],
        compiler_params=PARAMS,
        name="pack",
    )(*[in_hbm(v) for v in fields + rows + lists], active_count)
    dest, active, near_ids = held[6:]

    pairs_a = [(i ^ 1, i) for i in range(devices) if i ^ 1 < devices]
    pairs_b = []
    for i in range(1, devices - 1, 2):
        pairs_b += [(i, i + 1), (i + 1, i)]
    got_b = lax.ppermute(send_b, AXES, pairs_b)
    got_a = lax.ppermute(send_a, AXES, pairs_a)

    table, base, code, place, pick = pl.pallas_call(
        functools.partial(migrant_kernel, capacity),
        out_shape=(
            tab_shape,
            pltpu.VMEM((devices, P_SIZE), f32),
            pltpu.VMEM((mig_rows, P_SIZE), f32),
            pltpu.VMEM((mig_rows, P_SIZE), f32),
            pltpu.VMEM((P_SIZE, STATE * devices * capacity), bf16),
        ),
        in_specs=[VMEM] * 7 + [SMEM] * 2,
        out_specs=(VMEM,) * 5,
        compiler_params=PARAMS,
        name="migrants",
    )(*held[:7], active, active_count)

    made, outgoing, table, near, names_a, names_b = pl.pallas_call(
        density_kernel,
        out_shape=(
            pltpu.VMEM((cells, P_SIZE), f32),
            shape((devices * 8, P_SIZE), f32),
            tab_shape,
            near_shape,
            name_shape,
            name_shape,
        ),
        in_specs=[VMEM] * 9 + [SMEM] * 3,
        out_specs=(VMEM,) * 4 + (SMEM,) * 2,
        input_output_aliases={0: 0, 4: 2},
        scratch_shapes=[
            pltpu.VMEM((8, P_SIZE), f32),
            pltpu.VMEM((8, P_SIZE), f32),
            pltpu.SemaphoreType.DMA((2,)),
        ],
        compiler_params=PARAMS,
        name="density",
    )(held[4], held[3], got_a, got_b, table, base, code, place, dest, active, active_count, near_ids)

    incoming = lax.all_to_all(outgoing, AXES, split_axis=0, concat_axis=0, tiled=True)

    todo_len = pl.cdiv(slots * NBR + 2, P_SIZE) * P_SIZE
    partial, todo, new_density = pl.pallas_call(
        force_kernel,
        out_shape=(
            shape((3, slots, P_SIZE), f32),
            pltpu.SMEM((todo_len,), jnp.int32),
            shape((cells, P_SIZE), f32),
        ),
        in_specs=[VMEM] * 3 + [SMEM] * 5,
        out_specs=(VMEM, SMEM, HBM),
        scratch_shapes=[
            pltpu.VMEM((P_SIZE, slots * NBR * P_SIZE), bf16),
            pltpu.VMEM((P_SIZE, slots * NBR * P_SIZE), bf16),
            pltpu.SemaphoreType.DMA((1,)),
        ],
        compiler_params=PARAMS,
        name="force",
    )(table, near, made, names_a, names_b, active, active_count, near_ids)

    acceleration, arrivals = pl.pallas_call(
        functools.partial(finish_kernel, capacity),
        out_shape=(
            shape((3, slots, P_SIZE), f32),
            shape((STATE, devices * capacity), f32),
        ),
        in_specs=[VMEM] * 5 + [SMEM] * 2,
        out_specs=(VMEM, VMEM),
        compiler_params=PARAMS,
        name="finish",
    )(table, near, partial, incoming, pick, todo, active)
    return (new_density, acceleration, arrivals)


def solution(mesh):
    placed = (
        P(None, AXES, None),
        P(AXES, None),
        P(AXES, None),
        P(AXES, None),
        P(AXES, None),
        P(AXES),
        P(AXES),
        P(AXES, None),
        P(AXES),
        P(AXES, None),
    )
    return jax.shard_map(
        local,
        mesh=mesh,
        in_specs=placed,
        out_specs=(P(AXES, None), P(None, AXES, None), P(None, AXES)),
        check_vma=False,
    )
```

```python
import functools
import math

import jax
import jax.numpy as jnp
from jax import lax
from jax.experimental import pallas as pl
from jax.experimental.pallas import tpu as pltpu
from jax.sharding import PartitionSpec as P

P_SIZE = 128
NBR = 27
RIM = 64
STATE = 7
PLANES = 6
SUM_GROUP = 8
TINY = 1e-9
AXES = ("gx", "gy")

kernel_norm = 8.0 / math.pi
log_six_norm = math.log(6.0 * kernel_norm)
f32 = jnp.float32
bf16 = jnp.bfloat16
VMEM = pl.BlockSpec(memory_space=pltpu.VMEM)
SMEM = pl.BlockSpec(memory_space=pltpu.SMEM)
HBM = pl.BlockSpec(memory_space=pltpu.HBM)
PARAMS = pltpu.CompilerParams(vmem_limit_bytes=16 << 20)


def in_hbm(value):
    return pltpu.with_memory_space_constraint(value, pltpu.HBM)


def own_index():
    return lax.axis_index("gx") * lax.axis_size("gy") + lax.axis_index("gy")


def beta_of(inverse_len, entropy, density):
    power = 0.5 * (log_six_norm + jnp.log(entropy)) - jnp.log(density) * (1.0 / 6.0)
    return inverse_len * inverse_len * jnp.exp(power)


def row_sums(block):
    return jnp.sum(block.T, axis=0, keepdims=True)


def offset_tile(entry):
    row = lax.broadcasted_iota(jnp.int32, (8, P_SIZE), 0)
    shift = (entry // 9 - 1, entry // 3 % 3 - 1, entry % 3 - 1)
    tile = jnp.zeros((8, P_SIZE), f32)
    for axis in range(3):
        if shift[axis]:
            tile = jnp.where(row == axis, float(shift[axis]), tile)
    return tile


def split(value):
    high = value.astype(bf16).astype(f32)
    rest = value - high
    middle = rest.astype(bf16).astype(f32)
    return high, middle, rest - middle


def start_copies(pairs, sems):
    copies = [pltpu.make_async_copy(src, dst, sems.at[i]) for i, (src, dst) in enumerate(pairs)]
    for copy in copies:
        copy.start()
    return copies


def put(tab_ref, cell, count, row, plane):
    tab_ref[pl.ds(cell * 8 + row, count, stride=8), :] = plane


def tile_of(tab_ref, cell):
    return tab_ref[pl.ds(pl.multiple_of(cell * 8, 8), 8), :]


def put_table(tab_ref, cell, count, x, y, z, mass, inverse_len, beta):
    cube_root = jnp.exp(jnp.log(mass) * (1.0 / 3.0))
    planes = (x - 0.5, y - 0.5, z - 0.5, mass, cube_root, mass, inverse_len, beta)
    for row, plane in enumerate(planes):
        put(tab_ref, cell, count, row, plane)


def pack_kernel(
    pos_hbm,
    mass_hbm,
    len_hbm,
    ent_hbm,
    rho_hbm,
    source_hbm,
    dest_hbm,
    act_hbm,
    nbr_hbm,
    cnt_ref,
    b_ref,
    a_ref,
    pos_ref,
    mass_ref,
    len_ref,
    ent_ref,
    rho_ref,
    source_ref,
    dest_ref,
    act_ref,
    nbr_ref,
    sems,
):
    cells = mass_ref.shape[0]
    me = own_index()
    copies = start_copies(
        (
            (act_hbm, act_ref),
            (len_hbm, len_ref),
            (ent_hbm, ent_ref),
            (rho_hbm, rho_ref),
            (pos_hbm, pos_ref),
            (mass_hbm, mass_ref),
            (source_hbm, source_ref),
            (dest_hbm, dest_ref),
            (nbr_hbm, nbr_ref),
        ),
        sems,
    )
    for copy in copies[:6]:
        copy.wait()
    odd = me % 2
    start_a = pl.multiple_of((1 - odd) * (cells - RIM), RIM)
    start_b = pl.multiple_of(odd * (cells - RIM), RIM)
    lane = lax.broadcasted_iota(jnp.int32, (8, P_SIZE), 1)
    names = jnp.full((8, P_SIZE), -1.0, f32)
    slots = act_ref.shape[0]
    for slot in range(slots):
        mine = act_ref[slot] - me * cells
        live = slot < cnt_ref[0]
        names = jnp.where(jnp.logical_and(lane == slot, live), mine.astype(f32), names)
    cell = lax.broadcasted_iota(jnp.int32, (RIM, P_SIZE), 0)
    for out_ref, start in ((b_ref, start_b), (a_ref, start_a)):
        rows = pl.ds(start, RIM)
        for axis in range(3):
            out_ref[pl.ds(axis * RIM, RIM), :] = pos_ref[axis, rows, :]
        inverse_len = 1.0 / len_ref[rows, :]
        beta = beta_of(inverse_len, ent_ref[rows, :], rho_ref[rows, :])
        for slot in range(slots):
            mine = jnp.where(slot < cnt_ref[0], act_ref[slot] - me * cells - start, -1)
            beta = jnp.where(cell == mine, 0.0, beta)
        out_ref[pl.ds(3 * RIM, RIM), :] = mass_ref[rows, :]
        out_ref[pl.ds(4 * RIM, RIM), :] = inverse_len
        out_ref[pl.ds(5 * RIM, RIM), :] = beta
        out_ref[pl.ds(PLANES * RIM, 8), :] = names
    for copy in copies[6:]:
        copy.wait()


def migrant_kernel(
    capacity,
    pos_ref,
    mass_ref,
    len_ref,
    ent_ref,
    rho_ref,
    source_ref,
    dest_ref,
    act_ref,
    cnt_ref,
    tab_ref,
    base_ref,
    code_ref,
    place_ref,
    pick_ref,
):
    cells = mass_ref.shape[0]
    me = own_index()
    targets = base_ref.shape[0]
    inverse_len = 1.0 / len_ref[...]
    beta = beta_of(inverse_len, ent_ref[...], rho_ref[...])
    put_table(
        tab_ref, RIM, cells, pos_ref[0], pos_ref[1], pos_ref[2], mass_ref[...], inverse_len, beta
    )
    source = source_ref[...]
    cell_row = source // P_SIZE
    code_row = jnp.zeros_like(source)
    for slot in range(act_ref.shape[0]):
        mine = act_ref[slot] - me * cells
        named = jnp.logical_and(cell_row == mine, slot < cnt_ref[0])
        code_row = jnp.where(named, slot + 1, code_row)
    row_id = lax.broadcasted_iota(jnp.int32, (8, P_SIZE), 0)
    stack = jnp.zeros((8, P_SIZE), f32)
    for index, part in enumerate((cell_row, source % P_SIZE, dest_ref[...], code_row)):
        stack = jnp.where(row_id == index, part.astype(f32), stack)
    columns = stack.T
    shape = (P_SIZE, P_SIZE)
    cell, lane_of, dest, code = [jnp.broadcast_to(columns[:, i : i + 1], shape) for i in range(4)]
    lane = lax.broadcasted_iota(jnp.int32, shape, 1)
    row = lax.broadcasted_iota(jnp.int32, shape, 0)
    lane_f = lane.astype(f32)
    hit = lane_f == lane_of
    same = jnp.logical_and(dest == dest_ref[...].astype(f32), lane < row)
    rank = jnp.sum(jnp.where(same, 1.0, 0.0), axis=1, keepdims=True)
    wide = lax.broadcasted_iota(jnp.int32, (P_SIZE, cells), 1).astype(f32)
    pick = jnp.where(wide == columns[:, 0:1], 1.0, 0.0)
    spot = lane_f - rank
    sent = jnp.zeros(shape, f32)
    planes = [pos_ref[0], pos_ref[1], pos_ref[2], mass_ref[...], len_ref[...], ent_ref[...], rho_ref[...]]
    for index, plane in enumerate(planes):
        found = jnp.dot(pick, plane, precision=lax.Precision.HIGHEST, preferred_element_type=f32)
        keep = jnp.logical_and(hit, code == 0.0) if index == STATE - 1 else hit
        value = jnp.sum(jnp.where(keep, found, 0.0), axis=1, keepdims=True)
        sent = jnp.where(spot == float(index * capacity), value, sent)
    aim = lax.broadcasted_iota(jnp.int32, (targets, P_SIZE), 0) == dest_ref[...]
    aim = jnp.where(aim, 1.0, 0.0)
    base_ref[...] = jnp.dot(aim, sent, precision=lax.Precision.HIGHEST, preferred_element_type=f32)
    code_ref[...] = jnp.where(hit, code, 0.0)
    place_ref[...] = jnp.where(spot == float((STATE - 1) * capacity), 1.0, 0.0)
    width = targets * capacity
    column = lax.broadcasted_iota(jnp.int32, (P_SIZE, width), 1)
    spot_of = lax.broadcasted_iota(jnp.int32, (P_SIZE, width), 0) - column % capacity
    for index in range(STATE):
        hit = jnp.where(spot_of == index * capacity, 1.0, 0.0)
        pick_ref[:, pl.ds(index * width, width)] = hit.astype(bf16)


def squared_length(tile):
    square = tile * tile
    return square[0:1, :] + square[1:2, :] + square[2:3, :]


def row_ids():
    return lax.broadcasted_iota(jnp.int32, (8, P_SIZE), 0)


def own_features(tile, scale):
    row = row_ids()
    lead = jnp.where(row < 3, -2.0 * tile, 1.0)
    lead = jnp.where(row == 4, squared_length(tile), lead)
    lead = jnp.where(row < 5, lead * scale, 0.0)
    high, middle, low = split(lead)
    return jnp.concatenate([high, high, middle, middle, high, low], axis=0).T.astype(bf16)


def other_features(tile):
    high, middle, low = split(tile)
    return jnp.concatenate([high, middle, high, middle, low, high], axis=0).astype(bf16)


def groups(size):
    return [range(first, min(first + size, NBR)) for first in range(0, NBR, size)]


def density_kernel(
    rho_in,
    ent_ref,
    a_ref,
    b_ref,
    tab_in,
    base_ref,
    code_ref,
    place_ref,
    dest_ref,
    act_ref,
    cnt_ref,
    nbr_ref,
    new_ref,
    out_ref,
    tab_ref,
    near_ref,
    names_a,
    names_b,
    made_ref,
    beta_ref,
    sems,
):
    cells = new_ref.shape[0]
    slots = act_ref.shape[0]
    me = own_index()
    odd = me % 2
    copies = start_copies(
        [
            (ref.at[pl.ds(PLANES * RIM, 8), :], names)
            for ref, names in ((a_ref, names_a), (b_ref, names_b))
        ],
        sems,
    )
    start_of_a = (1 - odd) * (cells + RIM)
    for in_ref, start in ((a_ref, start_of_a), (b_ref, cells + RIM - start_of_a)):
        put_table(tab_ref, start, RIM, *[in_ref[pl.ds(i * RIM, RIM), :] for i in range(PLANES)])
    base = me * cells - RIM
    row = row_ids()
    for slot in range(slots):
        mine = act_ref[slot] - me * cells
        own = tile_of(tab_ref, RIM + mine)
        inverse_len = own[6:7, :]
        left = own_features(own, inverse_len * inverse_len)
        outer_sum = jnp.zeros((P_SIZE, P_SIZE), f32)
        inner_sum = jnp.zeros((P_SIZE, P_SIZE), f32)
        for group in groups(2):
            parts = []
            roots = []
            for entry in group:
                tile = tile_of(tab_ref, nbr_ref[slot, entry] - base) + offset_tile(entry)
                tile = jnp.where(row == 3, squared_length(tile), tile)
                root = tile[4:5, :]
                tile_one = jnp.where(row == 4, 1.0, tile)
                near_ref[pl.ds((slot * NBR + entry) * 8, 8), :] = tile_one
                parts.append(other_features(tile_one * (root * root)))
                roots.append(root)
            squares = jnp.dot(left, jnp.concatenate(parts, axis=1), preferred_element_type=f32)
            for place, root in enumerate(roots):
                square = squares[:, place * P_SIZE : (place + 1) * P_SIZE]
                square = jnp.maximum(square, root * TINY)
                ratio = square * lax.rsqrt(square)
                outer = jnp.maximum(root - ratio, 0.0)
                inner = jnp.maximum(0.5 * root - ratio, 0.0)
                outer_sum = outer_sum + outer * outer * outer
                inner_sum = inner_sum + inner * inner * inner
        total = outer_sum - 4.0 * inner_sum
        made = row_sums(total) * (2.0 * kernel_norm) * inverse_len * inverse_len * inverse_len
        made = jnp.where(slot < cnt_ref[0], made, new_ref[pl.ds(mine, 1), :])
        beta = beta_of(inverse_len, ent_ref[pl.ds(mine, 1), :], made)
        made_ref[slot : slot + 1, :] = made
        beta_ref[slot : slot + 1, :] = beta

    for slot in range(slots):
        mine = act_ref[slot] - me * cells
        new_ref[pl.ds(mine, 1), :] = made_ref[slot : slot + 1, :]
        tab_ref[pl.ds((RIM + mine) * 8 + 7, 1), :] = beta_ref[slot : slot + 1, :]
    code = code_ref[...]
    chosen = jnp.zeros_like(code)
    for slot in range(slots):
        chosen = jnp.where(code == float(slot + 1), made_ref[slot : slot + 1, :], chosen)
    late = place_ref[...] * jnp.sum(chosen, axis=1, keepdims=True)
    targets = base_ref.shape[0]
    aim = lax.broadcasted_iota(jnp.int32, (targets, P_SIZE), 0) == dest_ref[...]
    aim = jnp.where(aim, 1.0, 0.0)
    for line in range(1, 8):
        fill = jnp.zeros((1, P_SIZE), f32) if line > slots else beta_ref[line - 1 : line, :]
        put(out_ref, 0, targets, line, jnp.broadcast_to(fill, (targets, P_SIZE)))
    sent = base_ref[...] + jnp.dot(
        aim, late, precision=lax.Precision.HIGHEST, preferred_element_type=f32
    )
    put(out_ref, 0, targets, 0, sent)
    for copy in copies:
        copy.wait()


def spline(base, slope, distance):
    step = distance * slope
    outer = jnp.maximum(base - step, 0.0)
    least = jnp.minimum(step, outer)
    return least * (outer + (outer - least))


def force_kernel(
    tab_ref,
    near_ref,
    new_ref,
    names_a,
    names_b,
    act_ref,
    cnt_ref,
    nbr_ref,
    acc_out,
    list_ref,
    new_out,
    sems,
):
    cells = tab_ref.shape[0] // 8 - 2 * RIM
    me = own_index()
    odd = me % 2
    base = me * cells - RIM
    slots = act_ref.shape[0]
    copies = start_copies([(new_ref, new_out)], sems)
    fa = [names_a[0, s].astype(jnp.int32) for s in range(slots)]
    fb = [names_b[0, s].astype(jnp.int32) for s in range(slots)]
    left = [jnp.where(odd == 1, fa[s], fb[s]) for s in range(slots)]
    right = [jnp.where(odd == 1, fb[s], fa[s]) for s in range(slots)]
    left = [jnp.where(v >= cells - RIM, v - (cells - RIM), -1) for v in left]
    right = [jnp.where(jnp.logical_and(v >= 0, v < RIM), v + cells + RIM, -1) for v in right]
    row = row_ids()
    dims = (((1,), (1,)), ((), ()))
    at = jnp.int32(0)
    for slot in range(slots):
        live = slot < cnt_ref[0]
        mine = act_ref[slot] - me * cells
        own = tile_of(tab_ref, RIM + mine)
        columns = own.T
        own_base = jnp.broadcast_to(columns[:, 7:8], (P_SIZE, P_SIZE))
        own_slope = own_base * jnp.broadcast_to(columns[:, 6:7], (P_SIZE, P_SIZE))
        left_side = own_features(own, 1.0)
        sums = jnp.zeros((P_SIZE, 24), f32)
        for block in groups(SUM_GROUP):
            parts, highs, lows = [], [], []
            for first in range(block.start, block.stop, 2):
                group = range(first, min(first + 2, block.stop))
                tiles = [near_ref[pl.ds((slot * NBR + entry) * 8, 8), :] for entry in group]
                other = jnp.concatenate([other_features(tile) for tile in tiles], axis=1)
                squares = jnp.dot(left_side, other, preferred_element_type=f32)
                for place, entry in enumerate(group):
                    near = tiles[place]
                    cell = nbr_ref[slot, entry] - base
                    found = jnp.int32(-1)
                    for s in range(slots):
                        found = jnp.where(cell == left[s], s, found)
                        found = jnp.where(cell == right[s], slots + s, found)
                    list_ref[at + 1] = (slot * NBR + entry) * (2 * slots) + found
                    at = at + jnp.where(jnp.logical_and(found >= 0, live), 1, 0)

                    beta = tab_ref[pl.ds(cell * 8 + 7, 1), :]
                    slope = beta * near[6:7, :]
                    square = jnp.maximum(squares[:, place * P_SIZE : (place + 1) * P_SIZE], near[6:7, :] * TINY)
                    inverse = lax.rsqrt(square)
                    distance = square * inverse
                    pull = spline(own_base, own_slope, distance) + spline(beta, slope, distance)
                    pull = pull * inverse
                    high = pull.astype(bf16)
                    highs.append(high)
                    lows.append((pull - high.astype(f32)).astype(bf16))
                    weighed = jnp.where(row < 3, near, 1.0) * near[5:6, :]
                    parts.append(jnp.concatenate(split(weighed), axis=0).astype(bf16))
            sums = sums + lax.dot_general(
                jnp.concatenate(highs + lows, axis=1),
                jnp.concatenate(parts + parts, axis=1),
                dims,
                preferred_element_type=f32,
            )
        flat = sums.T
        flat = flat[0:8, :] + flat[8:16, :] + flat[16:24, :]
        made = jnp.where(live, own * flat[3:4, :] - flat, 0.0)
        for axis in range(3):
            acc_out[axis, slot : slot + 1, :] = made[axis : axis + 1, :]
    list_ref[0] = at
    for copy in copies:
        copy.wait()


def finish_kernel(
    capacity,
    tab_ref,
    near_ref,
    part_ref,
    got_ref,
    pick_ref,
    list_ref,
    act_ref,
    acc_out,
    arrive_ref,
):
    cells = tab_ref.shape[0] // 8 - 2 * RIM
    me = own_index()
    slots = act_ref.shape[0]
    targets = got_ref.shape[0] // 8
    acc_out[...] = part_ref[...]
    rows = got_ref[pl.ds(0, targets, stride=8), :]
    width = targets * capacity
    sender = lax.broadcasted_iota(jnp.int32, (targets, width), 1) // capacity
    mask = sender == lax.broadcasted_iota(jnp.int32, (targets, width), 0)
    pieces = jnp.concatenate(split(rows), axis=0).astype(bf16)
    spread = jnp.dot(pieces, pick_ref[...], preferred_element_type=f32)
    spread = spread[0:targets] + spread[targets : 2 * targets] + spread[2 * targets :]
    for index in range(STATE):
        part = spread[:, index * width : (index + 1) * width]
        arrive_ref[index : index + 1, :] = jnp.sum(jnp.where(mask, part, 0.0), axis=0, keepdims=True)

    @pl.loop(0, list_ref[0])
    def _(item):
        word = list_ref[item + 1]
        found = word % (2 * slots)
        place = word // (2 * slots)
        slot = place // NBR
        other = jnp.where(found < slots, me - 1, me + 1)
        near = near_ref[pl.ds(pl.multiple_of(place * 8, 8), 8), :]
        beta = got_ref[pl.ds(other * 8 + 1 + found % slots, 1), :]
        slope = beta * near[6:7, :]
        columns = tile_of(tab_ref, RIM + act_ref[slot] - me * cells).T
        apart = [
            jnp.broadcast_to(columns[:, axis : axis + 1], (P_SIZE, P_SIZE)) - near[axis : axis + 1, :]
            for axis in range(3)
        ]
        square = apart[0] * apart[0] + apart[1] * apart[1] + apart[2] * apart[2]
        square = jnp.maximum(square, TINY)
        inverse = lax.rsqrt(square)
        pull = spline(beta, slope, square * inverse) * inverse * near[5:6, :]
        for axis in range(3):
            acc_out[axis, pl.ds(slot, 1), :] += row_sums(pull * apart[axis])


def local(
    positions,
    masses,
    smoothing,
    entropy,
    density,
    active_cells,
    active_count,
    neighbours,
    mig_source,
    mig_dest,
):
    cells = masses.shape[0]
    slots = active_cells.shape[0]
    devices = lax.axis_size(AXES)
    mig_rows = mig_source.shape[0]
    capacity = max(2, 2 * mig_rows // devices)
    shape = jax.ShapeDtypeStruct
    rim_shape = shape((PLANES * RIM + 8, P_SIZE), f32)
    tab_shape = pltpu.VMEM(((cells + 2 * RIM) * 8, P_SIZE), f32)
    near_shape = pltpu.VMEM((slots * NBR * 8, P_SIZE), f32)
    name_shape = pltpu.SMEM((8, P_SIZE), f32)
    fields = (positions, masses, smoothing, entropy, density)
    rows = (mig_source.reshape(1, mig_rows), mig_dest.reshape(1, mig_rows))
    lists = (active_cells, neighbours)

    send_b, send_a, *held = pl.pallas_call(
        pack_kernel,
        out_shape=(rim_shape, rim_shape)
        + tuple(pltpu.VMEM(v.shape, v.dtype) for v in fields + rows)
        + tuple(pltpu.SMEM(v.shape, v.dtype) for v in lists),
        in_specs=[HBM] * 9 + [SMEM],
        out_specs=(VMEM,) * 9 + (SMEM,) * 2,
        scratch_shapes=[pltpu.SemaphoreType.DMA((9,))],
        compiler_params=PARAMS,
        name="pack",
    )(*[in_hbm(v) for v in fields + rows + lists], active_count)
    dest, active, near_ids = held[6:]

    pairs_a = [(i ^ 1, i) for i in range(devices) if i ^ 1 < devices]
    pairs_b = []
    for i in range(1, devices - 1, 2):
        pairs_b += [(i, i + 1), (i + 1, i)]
    got_b = lax.ppermute(send_b, AXES, pairs_b)
    got_a = lax.ppermute(send_a, AXES, pairs_a)

    table, base, code, place, pick = pl.pallas_call(
        functools.partial(migrant_kernel, capacity),
        out_shape=(
            tab_shape,
            pltpu.VMEM((devices, P_SIZE), f32),
            pltpu.VMEM((mig_rows, P_SIZE), f32),
            pltpu.VMEM((mig_rows, P_SIZE), f32),
            pltpu.VMEM((P_SIZE, STATE * devices * capacity), bf16),
        ),
        in_specs=[VMEM] * 7 + [SMEM] * 2,
        out_specs=(VMEM,) * 5,
        compiler_params=PARAMS,
        name="migrants",
    )(*held[:7], active, active_count)

    made, outgoing, table, near, names_a, names_b = pl.pallas_call(
        density_kernel,
        out_shape=(
            pltpu.VMEM((cells, P_SIZE), f32),
            shape((devices * 8, P_SIZE), f32),
            tab_shape,
            near_shape,
            name_shape,
            name_shape,
        ),
        in_specs=[VMEM] * 9 + [SMEM] * 3,
        out_specs=(VMEM,) * 4 + (SMEM,) * 2,
        input_output_aliases={0: 0, 4: 2},
        scratch_shapes=[
            pltpu.VMEM((8, P_SIZE), f32),
            pltpu.VMEM((8, P_SIZE), f32),
            pltpu.SemaphoreType.DMA((2,)),
        ],
        compiler_params=PARAMS,
        name="density",
    )(held[4], held[3], got_a, got_b, table, base, code, place, dest, active, active_count, near_ids)

    incoming = lax.all_to_all(outgoing, AXES, split_axis=0, concat_axis=0, tiled=True)

    todo_len = pl.cdiv(slots * NBR + 2, P_SIZE) * P_SIZE
    partial, todo, new_density = pl.pallas_call(
        force_kernel,
        out_shape=(
            shape((3, slots, P_SIZE), f32),
            pltpu.SMEM((todo_len,), jnp.int32),
            shape((cells, P_SIZE), f32),
        ),
        in_specs=[VMEM] * 3 + [SMEM] * 5,
        out_specs=(VMEM, SMEM, HBM),
        scratch_shapes=[
            pltpu.SemaphoreType.DMA((1,)),
        ],
        compiler_params=PARAMS,
        name="force",
    )(table, near, made, names_a, names_b, active, active_count, near_ids)

    acceleration, arrivals = pl.pallas_call(
        functools.partial(finish_kernel, capacity),
        out_shape=(
            shape((3, slots, P_SIZE), f32),
            shape((STATE, devices * capacity), f32),
        ),
        in_specs=[VMEM] * 5 + [SMEM] * 2,
        out_specs=(VMEM, VMEM),
        compiler_params=PARAMS,
        name="finish",
    )(table, near, partial, incoming, pick, todo, active)
    return (new_density, acceleration, arrivals)


def solution(mesh):
    placed = (
        P(None, AXES, None),
        P(AXES, None),
        P(AXES, None),
        P(AXES, None),
        P(AXES, None),
        P(AXES),
        P(AXES),
        P(AXES, None),
        P(AXES),
        P(AXES, None),
    )
    return jax.shard_map(
        local,
        mesh=mesh,
        in_specs=placed,
        out_specs=(P(AXES, None), P(None, AXES, None), P(None, AXES)),
        check_vma=False,
    )
```

```python
import functools
import math

import jax
import jax.numpy as jnp
from jax import lax
from jax.experimental import pallas as pl
from jax.experimental.pallas import tpu as pltpu
from jax.sharding import PartitionSpec as P

P_SIZE = 128
NBR = 27
RIM = 64
STATE = 7
PLANES = 6
SUM_GROUP = 8
EARLY_FIRST = 5
EARLY = 11
TINY = 1e-9
AXES = ("gx", "gy")

kernel_norm = 8.0 / math.pi
log_six_norm = math.log(6.0 * kernel_norm)
f32 = jnp.float32
bf16 = jnp.bfloat16
VMEM = pl.BlockSpec(memory_space=pltpu.VMEM)
SMEM = pl.BlockSpec(memory_space=pltpu.SMEM)
HBM = pl.BlockSpec(memory_space=pltpu.HBM)
PARAMS = pltpu.CompilerParams(vmem_limit_bytes=16 << 20)


def in_hbm(value):
    return pltpu.with_memory_space_constraint(value, pltpu.HBM)


def own_index():
    return lax.axis_index("gx") * lax.axis_size("gy") + lax.axis_index("gy")


def beta_of(inverse_len, entropy, density):
    power = 0.5 * (log_six_norm + jnp.log(entropy)) - jnp.log(density) * (1.0 / 6.0)
    return inverse_len * inverse_len * jnp.exp(power)


def row_sums(block):
    return jnp.sum(block.T, axis=0, keepdims=True)


def offset_tile(entry):
    row = lax.broadcasted_iota(jnp.int32, (8, P_SIZE), 0)
    shift = (entry // 9 - 1, entry // 3 % 3 - 1, entry % 3 - 1)
    tile = jnp.zeros((8, P_SIZE), f32)
    for axis in range(3):
        if shift[axis]:
            tile = jnp.where(row == axis, float(shift[axis]), tile)
    return tile


def split(value):
    high = value.astype(bf16).astype(f32)
    rest = value - high
    middle = rest.astype(bf16).astype(f32)
    return high, middle, rest - middle


def start_copies(pairs, sems):
    copies = [pltpu.make_async_copy(src, dst, sems.at[i]) for i, (src, dst) in enumerate(pairs)]
    for copy in copies:
        copy.start()
    return copies


def put(tab_ref, cell, count, row, plane):
    tab_ref[pl.ds(cell * 8 + row, count, stride=8), :] = plane


def tile_of(tab_ref, cell):
    return tab_ref[pl.ds(pl.multiple_of(cell * 8, 8), 8), :]


def put_table(tab_ref, cell, count, x, y, z, mass, inverse_len, beta):
    cube_root = jnp.exp(jnp.log(mass) * (1.0 / 3.0))
    planes = (x - 0.5, y - 0.5, z - 0.5, mass, cube_root, mass, inverse_len, beta)
    for row, plane in enumerate(planes):
        put(tab_ref, cell, count, row, plane)


def pack_kernel(
    pos_hbm,
    mass_hbm,
    len_hbm,
    ent_hbm,
    rho_hbm,
    source_hbm,
    dest_hbm,
    act_hbm,
    nbr_hbm,
    cnt_ref,
    b_ref,
    a_ref,
    pos_ref,
    mass_ref,
    len_ref,
    ent_ref,
    rho_ref,
    source_ref,
    dest_ref,
    act_ref,
    nbr_ref,
    sems,
):
    cells = mass_ref.shape[0]
    me = own_index()
    copies = start_copies(
        (
            (act_hbm, act_ref),
            (len_hbm, len_ref),
            (ent_hbm, ent_ref),
            (rho_hbm, rho_ref),
            (pos_hbm, pos_ref),
            (mass_hbm, mass_ref),
            (source_hbm, source_ref),
            (dest_hbm, dest_ref),
            (nbr_hbm, nbr_ref),
        ),
        sems,
    )
    for copy in copies[:6]:
        copy.wait()
    odd = me % 2
    start_a = pl.multiple_of((1 - odd) * (cells - RIM), RIM)
    start_b = pl.multiple_of(odd * (cells - RIM), RIM)
    lane = lax.broadcasted_iota(jnp.int32, (8, P_SIZE), 1)
    names = jnp.full((8, P_SIZE), -1.0, f32)
    slots = act_ref.shape[0]
    for slot in range(slots):
        mine = act_ref[slot] - me * cells
        live = slot < cnt_ref[0]
        names = jnp.where(jnp.logical_and(lane == slot, live), mine.astype(f32), names)
    cell = lax.broadcasted_iota(jnp.int32, (RIM, P_SIZE), 0)
    for out_ref, start in ((b_ref, start_b), (a_ref, start_a)):
        rows = pl.ds(start, RIM)
        for axis in range(3):
            out_ref[pl.ds(axis * RIM, RIM), :] = pos_ref[axis, rows, :]
        inverse_len = 1.0 / len_ref[rows, :]
        beta = beta_of(inverse_len, ent_ref[rows, :], rho_ref[rows, :])
        for slot in range(slots):
            mine = jnp.where(slot < cnt_ref[0], act_ref[slot] - me * cells - start, -1)
            beta = jnp.where(cell == mine, 0.0, beta)
        out_ref[pl.ds(3 * RIM, RIM), :] = mass_ref[rows, :]
        out_ref[pl.ds(4 * RIM, RIM), :] = inverse_len
        out_ref[pl.ds(5 * RIM, RIM), :] = beta
        out_ref[pl.ds(PLANES * RIM, 8), :] = names
    for copy in copies[6:]:
        copy.wait()


def squared_length(tile):
    square = tile * tile
    return square[0:1, :] + square[1:2, :] + square[2:3, :]


def row_ids():
    return lax.broadcasted_iota(jnp.int32, (8, P_SIZE), 0)


def own_features(tile, scale):
    row = row_ids()
    lead = jnp.where(row < 3, -2.0 * tile, 1.0)
    lead = jnp.where(row == 4, squared_length(tile), lead)
    lead = jnp.where(row < 5, lead * scale, 0.0)
    high, middle, low = split(lead)
    return jnp.concatenate([high, high, middle, middle, high, low], axis=0).T.astype(bf16)


def other_features(tile):
    high, middle, low = split(tile)
    return jnp.concatenate([high, middle, high, middle, low, high], axis=0).astype(bf16)


def groups(size):
    return [range(first, min(first + size, NBR)) for first in range(0, NBR, size)]


def early(slot):
    return EARLY if slot else EARLY_FIRST


def stencil_tile(tab_ref, off_ref, cell, offset):
    tile = tile_of(tab_ref, cell) + tile_of(off_ref, offset)
    return jnp.where(row_ids() == 3, squared_length(tile), tile)


def density_terms(left, tiles, weights):
    row = row_ids()
    parts, roots, kept = [], [], []
    for tile, weight in zip(tiles, weights):
        root = tile[4:5, :] if weight is None else tile[4:5, :] * weight
        one = jnp.where(row == 4, 1.0, tile)
        parts.append(other_features(one * (root * root)))
        roots.append(root)
        kept.append(one)
    squares = jnp.dot(left, jnp.concatenate(parts, axis=1), preferred_element_type=f32)
    outer_sum = inner_sum = None
    for place, root in enumerate(roots):
        square = squares[:, place * P_SIZE : (place + 1) * P_SIZE]
        square = jnp.maximum(square, kept[place][6:7, :] * TINY)
        ratio = square * lax.rsqrt(square)
        outer = jnp.maximum(root - ratio, 0.0)
        inner = jnp.maximum(0.5 * root - ratio, 0.0)
        outer, inner = outer * outer * outer, inner * inner * inner
        outer_sum = outer if outer_sum is None else outer_sum + outer
        inner_sum = inner if inner_sum is None else inner_sum + inner
    return outer_sum, inner_sum, kept


def place_of(slot, position):
    return slot * NBR + position


def migrant_kernel(
    capacity,
    pos_ref,
    mass_ref,
    len_ref,
    ent_ref,
    rho_ref,
    source_ref,
    dest_ref,
    act_ref,
    cnt_ref,
    nbr_ref,
    tab_ref,
    base_ref,
    code_ref,
    place_ref,
    pick_ref,
    near_ref,
    left_ref,
    total_ref,
    off_ref,
    cell_ref,
    offset_ref,
    own_ref,
):
    cells = mass_ref.shape[0]
    me = own_index()
    targets = base_ref.shape[0]
    inverse_len = 1.0 / len_ref[...]
    beta = beta_of(inverse_len, ent_ref[...], rho_ref[...])
    put_table(
        tab_ref, RIM, cells, pos_ref[0], pos_ref[1], pos_ref[2], mass_ref[...], inverse_len, beta
    )
    for entry in range(NBR):
        off_ref[pl.ds(entry * 8, 8), :] = offset_tile(entry)
    slots = act_ref.shape[0]
    base = me * cells - RIM
    for slot in range(slots):
        mine = jnp.int32(0)
        for entry in range(NBR):
            cell = nbr_ref[slot, entry] - base
            near_by = jnp.logical_and(cell >= RIM, cell < RIM + cells)
            at = jnp.where(near_by, mine, NBR - 1 - entry + mine)
            cell_ref[place_of(slot, at)] = cell
            offset_ref[place_of(slot, at)] = entry
            mine = mine + jnp.where(near_by, 1, 0)
        own_ref[slot] = mine
    for slot in range(slots):
        home = act_ref[slot] - base
        own = tile_of(tab_ref, home)
        inverse_len = own[6:7, :]
        left = own_features(own, inverse_len * inverse_len)
        left_ref[pl.ds(slot * P_SIZE, P_SIZE), :] = left
        outer_sum = jnp.zeros((P_SIZE, P_SIZE), f32)
        inner_sum = jnp.zeros((P_SIZE, P_SIZE), f32)
        for first in range(0, early(slot), 2):
            tiles, weights = [], []
            positions = range(first, min(first + 2, early(slot)))
            for position in positions:
                valid = position < own_ref[slot]
                cell = jnp.where(valid, cell_ref[place_of(slot, position)], home)
                offset = jnp.where(valid, offset_ref[place_of(slot, position)], 0)
                tiles.append(stencil_tile(tab_ref, off_ref, cell, offset))
                weights.append(jnp.where(valid, 1.0, 0.0))
            outer, inner, kept = density_terms(left, tiles, weights)
            outer_sum, inner_sum = outer_sum + outer, inner_sum + inner
            for position, tile in zip(positions, kept):
                near_ref[pl.ds(place_of(slot, position) * 8, 8), :] = tile
        total_ref[pl.ds(slot * P_SIZE, P_SIZE), :] = outer_sum - 4.0 * inner_sum
    source = source_ref[...]
    cell_row = source // P_SIZE
    code_row = jnp.zeros_like(source)
    for slot in range(act_ref.shape[0]):
        mine = act_ref[slot] - me * cells
        named = jnp.logical_and(cell_row == mine, slot < cnt_ref[0])
        code_row = jnp.where(named, slot + 1, code_row)
    row_id = lax.broadcasted_iota(jnp.int32, (8, P_SIZE), 0)
    stack = jnp.zeros((8, P_SIZE), f32)
    for index, part in enumerate((cell_row, source % P_SIZE, dest_ref[...], code_row)):
        stack = jnp.where(row_id == index, part.astype(f32), stack)
    columns = stack.T
    shape = (P_SIZE, P_SIZE)
    cell, lane_of, dest, code = [jnp.broadcast_to(columns[:, i : i + 1], shape) for i in range(4)]
    lane = lax.broadcasted_iota(jnp.int32, shape, 1)
    row = lax.broadcasted_iota(jnp.int32, shape, 0)
    lane_f = lane.astype(f32)
    hit = lane_f == lane_of
    same = jnp.logical_and(dest == dest_ref[...].astype(f32), lane < row)
    rank = jnp.sum(jnp.where(same, 1.0, 0.0), axis=1, keepdims=True)
    wide = lax.broadcasted_iota(jnp.int32, (P_SIZE, cells), 1).astype(f32)
    pick = jnp.where(wide == columns[:, 0:1], 1.0, 0.0)
    spot = lane_f - rank
    sent = jnp.zeros(shape, f32)
    planes = [pos_ref[0], pos_ref[1], pos_ref[2], mass_ref[...], len_ref[...], ent_ref[...], rho_ref[...]]
    for index, plane in enumerate(planes):
        found = jnp.dot(pick, plane, precision=lax.Precision.HIGHEST, preferred_element_type=f32)
        keep = jnp.logical_and(hit, code == 0.0) if index == STATE - 1 else hit
        value = jnp.sum(jnp.where(keep, found, 0.0), axis=1, keepdims=True)
        sent = jnp.where(spot == float(index * capacity), value, sent)
    aim = lax.broadcasted_iota(jnp.int32, (targets, P_SIZE), 0) == dest_ref[...]
    aim = jnp.where(aim, 1.0, 0.0)
    base_ref[...] = jnp.dot(aim, sent, precision=lax.Precision.HIGHEST, preferred_element_type=f32)
    code_ref[...] = jnp.where(hit, code, 0.0)
    place_ref[...] = jnp.where(spot == float((STATE - 1) * capacity), 1.0, 0.0)
    width = targets * capacity
    column = lax.broadcasted_iota(jnp.int32, (P_SIZE, width), 1)
    spot_of = lax.broadcasted_iota(jnp.int32, (P_SIZE, width), 0) - column % capacity
    for index in range(STATE):
        hit = jnp.where(spot_of == index * capacity, 1.0, 0.0)
        pick_ref[:, pl.ds(index * width, width)] = hit.astype(bf16)


def density_kernel(
    rho_in,
    ent_ref,
    a_ref,
    b_ref,
    tab_in,
    near_in,
    base_ref,
    code_ref,
    place_ref,
    dest_ref,
    left_ref,
    total_in,
    off_ref,
    act_ref,
    cnt_ref,
    cell_ref,
    offset_ref,
    own_ref,
    new_ref,
    out_ref,
    tab_ref,
    near_ref,
    total_ref,
    names_a,
    names_b,
    made_ref,
    beta_ref,
    sems,
):
    cells = new_ref.shape[0]
    slots = act_ref.shape[0]
    me = own_index()
    odd = me % 2
    copies = start_copies(
        [
            (ref.at[pl.ds(PLANES * RIM, 8), :], names)
            for ref, names in ((a_ref, names_a), (b_ref, names_b))
        ],
        sems,
    )
    start_of_a = (1 - odd) * (cells + RIM)
    for in_ref, start in ((a_ref, start_of_a), (b_ref, cells + RIM - start_of_a)):
        put_table(tab_ref, start, RIM, *[in_ref[pl.ds(i * RIM, RIM), :] for i in range(PLANES)])

    for slot in range(slots):

        @pl.loop(own_ref[slot], early(slot))
        def _(position):
            place = place_of(slot, position)
            tile = stencil_tile(tab_ref, off_ref, cell_ref[place], offset_ref[place])
            span = pl.ds(slot * P_SIZE, P_SIZE)
            outer, inner, kept = density_terms(left_ref[span, :], [tile], [None])
            total_ref[span, :] = total_ref[span, :] + (outer - 4.0 * inner)
            near_ref[pl.ds(pl.multiple_of(place * 8, 8), 8), :] = kept[0]

    for slot in range(slots):
        mine = act_ref[slot] - me * cells
        inverse_len = tile_of(tab_ref, RIM + mine)[6:7, :]
        span = pl.ds(slot * P_SIZE, P_SIZE)
        left = left_ref[span, :]
        outer_sum = total_ref[span, :]
        inner_sum = jnp.zeros((P_SIZE, P_SIZE), f32)
        for first in range(early(slot), NBR, 2):
            positions = range(first, min(first + 2, NBR))
            tiles = []
            for position in positions:
                place = place_of(slot, position)
                tiles.append(stencil_tile(tab_ref, off_ref, cell_ref[place], offset_ref[place]))
            outer, inner, kept = density_terms(left, tiles, [None] * len(tiles))
            outer_sum, inner_sum = outer_sum + outer, inner_sum + inner
            for position, tile in zip(positions, kept):
                near_ref[pl.ds(place_of(slot, position) * 8, 8), :] = tile
        total = outer_sum - 4.0 * inner_sum
        made = row_sums(total) * (2.0 * kernel_norm) * inverse_len * inverse_len * inverse_len
        made = jnp.where(slot < cnt_ref[0], made, new_ref[pl.ds(mine, 1), :])
        beta = beta_of(inverse_len, ent_ref[pl.ds(mine, 1), :], made)
        made_ref[slot : slot + 1, :] = made
        beta_ref[slot : slot + 1, :] = beta

    for slot in range(slots):
        mine = act_ref[slot] - me * cells
        new_ref[pl.ds(mine, 1), :] = made_ref[slot : slot + 1, :]
        tab_ref[pl.ds((RIM + mine) * 8 + 7, 1), :] = beta_ref[slot : slot + 1, :]
    code = code_ref[...]
    chosen = jnp.zeros_like(code)
    for slot in range(slots):
        chosen = jnp.where(code == float(slot + 1), made_ref[slot : slot + 1, :], chosen)
    late = place_ref[...] * jnp.sum(chosen, axis=1, keepdims=True)
    targets = base_ref.shape[0]
    aim = lax.broadcasted_iota(jnp.int32, (targets, P_SIZE), 0) == dest_ref[...]
    aim = jnp.where(aim, 1.0, 0.0)
    for line in range(1, 8):
        fill = jnp.zeros((1, P_SIZE), f32) if line > slots else beta_ref[line - 1 : line, :]
        put(out_ref, 0, targets, line, jnp.broadcast_to(fill, (targets, P_SIZE)))
    sent = base_ref[...] + jnp.dot(
        aim, late, precision=lax.Precision.HIGHEST, preferred_element_type=f32
    )
    put(out_ref, 0, targets, 0, sent)
    for copy in copies:
        copy.wait()


def spline(base, slope, distance):
    step = distance * slope
    outer = jnp.maximum(base - step, 0.0)
    least = jnp.minimum(step, outer)
    return least * (outer + (outer - least))


def force_kernel(
    tab_ref,
    near_ref,
    new_ref,
    names_a,
    names_b,
    act_ref,
    cnt_ref,
    cell_ref,
    acc_out,
    list_ref,
    new_out,
    sems,
):
    cells = tab_ref.shape[0] // 8 - 2 * RIM
    me = own_index()
    odd = me % 2
    slots = act_ref.shape[0]
    copies = start_copies([(new_ref, new_out)], sems)
    fa = [names_a[0, s].astype(jnp.int32) for s in range(slots)]
    fb = [names_b[0, s].astype(jnp.int32) for s in range(slots)]
    left = [jnp.where(odd == 1, fa[s], fb[s]) for s in range(slots)]
    right = [jnp.where(odd == 1, fb[s], fa[s]) for s in range(slots)]
    left = [jnp.where(v >= cells - RIM, v - (cells - RIM), -1) for v in left]
    right = [jnp.where(jnp.logical_and(v >= 0, v < RIM), v + cells + RIM, -1) for v in right]
    row = row_ids()
    dims = (((1,), (1,)), ((), ()))
    at = jnp.int32(0)
    for slot in range(slots):
        live = slot < cnt_ref[0]
        mine = act_ref[slot] - me * cells
        own = tile_of(tab_ref, RIM + mine)
        columns = own.T
        own_base = jnp.broadcast_to(columns[:, 7:8], (P_SIZE, P_SIZE))
        own_slope = own_base * jnp.broadcast_to(columns[:, 6:7], (P_SIZE, P_SIZE))
        left_side = own_features(own, 1.0)
        sums = jnp.zeros((P_SIZE, 24), f32)
        for block in groups(SUM_GROUP):
            parts, highs, lows = [], [], []
            for first in range(block.start, block.stop, 2):
                group = range(first, min(first + 2, block.stop))
                tiles = [near_ref[pl.ds((slot * NBR + entry) * 8, 8), :] for entry in group]
                other = jnp.concatenate([other_features(tile) for tile in tiles], axis=1)
                squares = jnp.dot(left_side, other, preferred_element_type=f32)
                for place, entry in enumerate(group):
                    near = tiles[place]
                    cell = cell_ref[place_of(slot, entry)]
                    found = jnp.int32(-1)
                    for s in range(slots):
                        found = jnp.where(cell == left[s], s, found)
                        found = jnp.where(cell == right[s], slots + s, found)
                    list_ref[at + 1] = (slot * NBR + entry) * (2 * slots) + found
                    at = at + jnp.where(jnp.logical_and(found >= 0, live), 1, 0)

                    beta = tab_ref[pl.ds(cell * 8 + 7, 1), :]
                    slope = beta * near[6:7, :]
                    square = jnp.maximum(squares[:, place * P_SIZE : (place + 1) * P_SIZE], near[6:7, :] * TINY)
                    inverse = lax.rsqrt(square)
                    distance = square * inverse
                    pull = spline(own_base, own_slope, distance) + spline(beta, slope, distance)
                    pull = pull * inverse
                    high = pull.astype(bf16)
                    highs.append(high)
                    lows.append((pull - high.astype(f32)).astype(bf16))
                    weighed = jnp.where(row < 3, near, 1.0) * near[5:6, :]
                    parts.append(jnp.concatenate(split(weighed), axis=0).astype(bf16))
            sums = sums + lax.dot_general(
                jnp.concatenate(highs + lows, axis=1),
                jnp.concatenate(parts + parts, axis=1),
                dims,
                preferred_element_type=f32,
            )
        flat = sums.T
        flat = flat[0:8, :] + flat[8:16, :] + flat[16:24, :]
        made = jnp.where(live, own * flat[3:4, :] - flat, 0.0)
        for axis in range(3):
            acc_out[axis, slot : slot + 1, :] = made[axis : axis + 1, :]
    list_ref[0] = at
    for copy in copies:
        copy.wait()


def finish_kernel(
    capacity,
    tab_ref,
    near_ref,
    part_ref,
    got_ref,
    pick_ref,
    list_ref,
    act_ref,
    acc_out,
    arrive_ref,
):
    cells = tab_ref.shape[0] // 8 - 2 * RIM
    me = own_index()
    slots = act_ref.shape[0]
    targets = got_ref.shape[0] // 8
    acc_out[...] = part_ref[...]
    rows = got_ref[pl.ds(0, targets, stride=8), :]
    width = targets * capacity
    sender = lax.broadcasted_iota(jnp.int32, (targets, width), 1) // capacity
    mask = sender == lax.broadcasted_iota(jnp.int32, (targets, width), 0)
    pieces = jnp.concatenate(split(rows), axis=0).astype(bf16)
    spread = jnp.dot(pieces, pick_ref[...], preferred_element_type=f32)
    spread = spread[0:targets] + spread[targets : 2 * targets] + spread[2 * targets :]
    for index in range(STATE):
        part = spread[:, index * width : (index + 1) * width]
        arrive_ref[index : index + 1, :] = jnp.sum(jnp.where(mask, part, 0.0), axis=0, keepdims=True)

    @pl.loop(0, list_ref[0])
    def _(item):
        word = list_ref[item + 1]
        found = word % (2 * slots)
        place = word // (2 * slots)
        slot = place // NBR
        other = jnp.where(found < slots, me - 1, me + 1)
        near = near_ref[pl.ds(pl.multiple_of(place * 8, 8), 8), :]
        beta = got_ref[pl.ds(other * 8 + 1 + found % slots, 1), :]
        slope = beta * near[6:7, :]
        columns = tile_of(tab_ref, RIM + act_ref[slot] - me * cells).T
        apart = [
            jnp.broadcast_to(columns[:, axis : axis + 1], (P_SIZE, P_SIZE)) - near[axis : axis + 1, :]
            for axis in range(3)
        ]
        square = apart[0] * apart[0] + apart[1] * apart[1] + apart[2] * apart[2]
        square = jnp.maximum(square, TINY)
        inverse = lax.rsqrt(square)
        pull = spline(beta, slope, square * inverse) * inverse * near[5:6, :]
        for axis in range(3):
            acc_out[axis, pl.ds(slot, 1), :] += row_sums(pull * apart[axis])


def local(
    positions,
    masses,
    smoothing,
    entropy,
    density,
    active_cells,
    active_count,
    neighbours,
    mig_source,
    mig_dest,
):
    cells = masses.shape[0]
    slots = active_cells.shape[0]
    devices = lax.axis_size(AXES)
    mig_rows = mig_source.shape[0]
    capacity = max(2, 2 * mig_rows // devices)
    shape = jax.ShapeDtypeStruct
    rim_shape = shape((PLANES * RIM + 8, P_SIZE), f32)
    tab_shape = pltpu.VMEM(((cells + 2 * RIM) * 8, P_SIZE), f32)
    near_shape = pltpu.VMEM((slots * NBR * 8, P_SIZE), f32)
    name_shape = pltpu.SMEM((8, P_SIZE), f32)
    fields = (positions, masses, smoothing, entropy, density)
    rows = (mig_source.reshape(1, mig_rows), mig_dest.reshape(1, mig_rows))
    lists = (active_cells, neighbours)

    send_b, send_a, *held = pl.pallas_call(
        pack_kernel,
        out_shape=(rim_shape, rim_shape)
        + tuple(pltpu.VMEM(v.shape, v.dtype) for v in fields + rows)
        + tuple(pltpu.SMEM(v.shape, v.dtype) for v in lists),
        in_specs=[HBM] * 9 + [SMEM],
        out_specs=(VMEM,) * 9 + (SMEM,) * 2,
        scratch_shapes=[pltpu.SemaphoreType.DMA((9,))],
        compiler_params=PARAMS,
        name="pack",
    )(*[in_hbm(v) for v in fields + rows + lists], active_count)
    dest, active, near_ids = held[6:]

    pairs_a = [(i ^ 1, i) for i in range(devices) if i ^ 1 < devices]
    pairs_b = []
    for i in range(1, devices - 1, 2):
        pairs_b += [(i, i + 1), (i + 1, i)]
    got_b = lax.ppermute(send_b, AXES, pairs_b)
    got_a = lax.ppermute(send_a, AXES, pairs_a)

    table, base, code, place, pick, near, left, total, offsets, cell_list, offset_list, owned = pl.pallas_call(
        functools.partial(migrant_kernel, capacity),
        out_shape=(
            tab_shape,
            pltpu.VMEM((devices, P_SIZE), f32),
            pltpu.VMEM((mig_rows, P_SIZE), f32),
            pltpu.VMEM((mig_rows, P_SIZE), f32),
            pltpu.VMEM((P_SIZE, STATE * devices * capacity), bf16),
            near_shape,
            pltpu.VMEM((slots * P_SIZE, 48), bf16),
            pltpu.VMEM((slots * P_SIZE, P_SIZE), f32),
            pltpu.VMEM((NBR * 8, P_SIZE), f32),
            pltpu.SMEM((slots * NBR,), jnp.int32),
            pltpu.SMEM((slots * NBR,), jnp.int32),
            pltpu.SMEM((slots,), jnp.int32),
        ),
        in_specs=[VMEM] * 7 + [SMEM] * 3,
        out_specs=(VMEM,) * 9 + (SMEM,) * 3,
        compiler_params=PARAMS,
        name="migrants",
    )(*held[:7], active, active_count, near_ids)

    made, outgoing, table, near, _, names_a, names_b = pl.pallas_call(
        density_kernel,
        out_shape=(
            pltpu.VMEM((cells, P_SIZE), f32),
            shape((devices * 8, P_SIZE), f32),
            tab_shape,
            near_shape,
            pltpu.VMEM((slots * P_SIZE, P_SIZE), f32),
            name_shape,
            name_shape,
        ),
        in_specs=[VMEM] * 13 + [SMEM] * 5,
        out_specs=(VMEM,) * 5 + (SMEM,) * 2,
        input_output_aliases={0: 0, 4: 2, 5: 3, 11: 4},
        scratch_shapes=[
            pltpu.VMEM((8, P_SIZE), f32),
            pltpu.VMEM((8, P_SIZE), f32),
            pltpu.SemaphoreType.DMA((2,)),
        ],
        compiler_params=PARAMS,
        name="density",
    )(
        held[4],
        held[3],
        got_a,
        got_b,
        table,
        near,
        base,
        code,
        place,
        dest,
        left,
        total,
        offsets,
        active,
        active_count,
        cell_list,
        offset_list,
        owned,
    )

    incoming = lax.all_to_all(outgoing, AXES, split_axis=0, concat_axis=0, tiled=True)

    todo_len = pl.cdiv(slots * NBR + 2, P_SIZE) * P_SIZE
    partial, todo, new_density = pl.pallas_call(
        force_kernel,
        out_shape=(
            shape((3, slots, P_SIZE), f32),
            pltpu.SMEM((todo_len,), jnp.int32),
            shape((cells, P_SIZE), f32),
        ),
        in_specs=[VMEM] * 3 + [SMEM] * 5,
        out_specs=(VMEM, SMEM, HBM),
        scratch_shapes=[
            pltpu.SemaphoreType.DMA((1,)),
        ],
        compiler_params=PARAMS,
        name="force",
    )(table, near, made, names_a, names_b, active, active_count, cell_list)

    acceleration, arrivals = pl.pallas_call(
        functools.partial(finish_kernel, capacity),
        out_shape=(
            shape((3, slots, P_SIZE), f32),
            shape((STATE, devices * capacity), f32),
        ),
        in_specs=[VMEM] * 5 + [SMEM] * 2,
        out_specs=(VMEM, VMEM),
        compiler_params=PARAMS,
        name="finish",
    )(table, near, partial, incoming, pick, todo, active)
    return (new_density, acceleration, arrivals)


def solution(mesh):
    placed = (
        P(None, AXES, None),
        P(AXES, None),
        P(AXES, None),
        P(AXES, None),
        P(AXES, None),
        P(AXES),
        P(AXES),
        P(AXES, None),
        P(AXES),
        P(AXES, None),
    )
    return jax.shard_map(
        local,
        mesh=mesh,
        in_specs=placed,
        out_specs=(P(AXES, None), P(None, AXES, None), P(None, AXES)),
        check_vma=False,
    )
```

```python
import functools
import math

import jax
import jax.numpy as jnp
from jax import lax
from jax.experimental import pallas as pl
from jax.experimental.pallas import tpu as pltpu
from jax.sharding import PartitionSpec as P

P_SIZE = 128
NBR = 27
RIM = 64
STATE = 7
PLANES = 6
SUM_GROUP = 8
EARLY_FIRST = 5
EARLY = 11
ITEMS = 4
TINY = 1e-9
AXES = ("gx", "gy")

kernel_norm = 8.0 / math.pi
log_six_norm = math.log(6.0 * kernel_norm)
f32 = jnp.float32
bf16 = jnp.bfloat16
VMEM = pl.BlockSpec(memory_space=pltpu.VMEM)
SMEM = pl.BlockSpec(memory_space=pltpu.SMEM)
HBM = pl.BlockSpec(memory_space=pltpu.HBM)
PARAMS = pltpu.CompilerParams(vmem_limit_bytes=16 << 20)


def in_hbm(value):
    return pltpu.with_memory_space_constraint(value, pltpu.HBM)


def own_index():
    return lax.axis_index("gx") * lax.axis_size("gy") + lax.axis_index("gy")


def beta_of(inverse_len, entropy, density):
    power = 0.5 * (log_six_norm + jnp.log(entropy)) - jnp.log(density) * (1.0 / 6.0)
    return inverse_len * inverse_len * jnp.exp(power)


def row_sums(block):
    return jnp.sum(block.T, axis=0, keepdims=True)


def offset_tile(entry):
    row = lax.broadcasted_iota(jnp.int32, (8, P_SIZE), 0)
    shift = (entry // 9 - 1, entry // 3 % 3 - 1, entry % 3 - 1)
    tile = jnp.zeros((8, P_SIZE), f32)
    for axis in range(3):
        if shift[axis]:
            tile = jnp.where(row == axis, float(shift[axis]), tile)
    return tile


def split(value):
    high = value.astype(bf16).astype(f32)
    rest = value - high
    middle = rest.astype(bf16).astype(f32)
    return high, middle, rest - middle


def start_copies(pairs, sems):
    copies = [pltpu.make_async_copy(src, dst, sems.at[i]) for i, (src, dst) in enumerate(pairs)]
    for copy in copies:
        copy.start()
    return copies


def put(tab_ref, cell, count, row, plane):
    tab_ref[pl.ds(cell * 8 + row, count, stride=8), :] = plane


def tile_of(tab_ref, cell):
    return tab_ref[pl.ds(pl.multiple_of(cell * 8, 8), 8), :]


def put_table(tab_ref, cell, count, x, y, z, mass, inverse_len, beta):
    cube_root = jnp.exp(jnp.log(mass) * (1.0 / 3.0))
    planes = (x - 0.5, y - 0.5, z - 0.5, None, cube_root, mass, inverse_len, beta)
    for row, plane in enumerate(planes):
        if plane is not None:
            put(tab_ref, cell, count, row, plane)


def pack_kernel(
    pos_hbm,
    mass_hbm,
    len_hbm,
    ent_hbm,
    rho_hbm,
    act_hbm,
    nbr_hbm,
    cnt_ref,
    b_ref,
    a_ref,
    act_ref,
    nbr_ref,
    rim_ref,
    sems,
):
    cells = mass_hbm.shape[0]
    me = own_index()
    odd = me % 2
    start_a = pl.multiple_of((1 - odd) * (cells - RIM), RIM)
    start_b = pl.multiple_of(odd * (cells - RIM), RIM)
    sides = ((b_ref, start_b), (a_ref, start_a))
    pairs = [(act_hbm, act_ref)]
    for side, (out_ref, start) in enumerate(sides):
        rows = pl.ds(start, RIM)
        for index, ref in enumerate((len_hbm, ent_hbm, rho_hbm)):
            pairs.append((ref.at[rows, :], rim_ref.at[side, index]))
    first = len(pairs)
    for out_ref, start in sides:
        rows = pl.ds(start, RIM)
        for axis in range(3):
            pairs.append((pos_hbm.at[axis, rows, :], out_ref.at[pl.ds(axis * RIM, RIM), :]))
        pairs.append((mass_hbm.at[rows, :], out_ref.at[pl.ds(3 * RIM, RIM), :]))
    pairs.append((nbr_hbm, nbr_ref))
    copies = start_copies(pairs, sems)
    for copy in copies[:first]:
        copy.wait()
    lane = lax.broadcasted_iota(jnp.int32, (8, P_SIZE), 1)
    names = jnp.full((8, P_SIZE), -1.0, f32)
    slots = act_ref.shape[0]
    for slot in range(slots):
        mine = act_ref[slot] - me * cells
        live = slot < cnt_ref[0]
        names = jnp.where(jnp.logical_and(lane == slot, live), mine.astype(f32), names)
    cell = lax.broadcasted_iota(jnp.int32, (RIM, P_SIZE), 0)
    for side, (out_ref, start) in enumerate(sides):
        inverse_len = 1.0 / rim_ref[side, 0]
        beta = beta_of(inverse_len, rim_ref[side, 1], rim_ref[side, 2])
        for slot in range(slots):
            mine = jnp.where(slot < cnt_ref[0], act_ref[slot] - me * cells - start, -1)
            beta = jnp.where(cell == mine, 0.0, beta)
        out_ref[pl.ds(4 * RIM, RIM), :] = inverse_len
        out_ref[pl.ds(5 * RIM, RIM), :] = beta
        out_ref[pl.ds(PLANES * RIM, 8), :] = names
    for copy in copies[first:]:
        copy.wait()


def squared_length(tile):
    square = tile * tile
    return square[0:1, :] + square[1:2, :] + square[2:3, :]


def row_ids():
    return lax.broadcasted_iota(jnp.int32, (8, P_SIZE), 0)


def own_features(tile, scale):
    row = row_ids()
    lead = jnp.where(row < 3, -2.0 * tile, 1.0)
    lead = jnp.where(row == 4, squared_length(tile), lead)
    lead = jnp.where(row < 5, lead * scale, 0.0)
    high, middle, low = split(lead)
    return jnp.concatenate([high, high, middle, middle, high, low], axis=0).T.astype(bf16)


def other_features(tile):
    high, middle, low = split(tile)
    return jnp.concatenate([high, middle, high, middle, low, high], axis=0).astype(bf16)


def groups(size):
    return [range(first, min(first + size, NBR)) for first in range(0, NBR, size)]


def early(slot):
    return EARLY if slot else EARLY_FIRST


def stencil_tile(tab_ref, off_ref, cell, offset):
    tile = tile_of(tab_ref, cell) + tile_of(off_ref, offset)
    return jnp.where(row_ids() == 3, squared_length(tile), tile)


def density_terms(left, tiles, weights):
    row = row_ids()
    parts, roots, kept = [], [], []
    for tile, weight in zip(tiles, weights):
        root = tile[4:5, :] if weight is None else tile[4:5, :] * weight
        one = jnp.where(row == 4, 1.0, tile)
        parts.append(other_features(one * (root * root)))
        roots.append(root)
        kept.append(one)
    squares = jnp.dot(left, jnp.concatenate(parts, axis=1), preferred_element_type=f32)
    outer_sum = inner_sum = None
    for place, root in enumerate(roots):
        square = squares[:, place * P_SIZE : (place + 1) * P_SIZE]
        square = jnp.maximum(square, kept[place][6:7, :] * TINY)
        ratio = square * lax.rsqrt(square)
        outer = jnp.maximum(root - ratio, 0.0)
        inner = jnp.maximum(0.5 * root - ratio, 0.0)
        outer, inner = outer * outer * outer, inner * inner * inner
        outer_sum = outer if outer_sum is None else outer_sum + outer
        inner_sum = inner if inner_sum is None else inner_sum + inner
    return outer_sum, inner_sum, kept


def place_of(slot, position):
    return slot * NBR + position


def migrant_kernel(
    capacity,
    pos_hbm,
    mass_hbm,
    len_hbm,
    ent_hbm,
    rho_hbm,
    source_hbm,
    dest_hbm,
    act_ref,
    cnt_ref,
    nbr_ref,
    ent_ref,
    rho_ref,
    dest_ref,
    tab_ref,
    base_ref,
    code_ref,
    place_ref,
    pick_ref,
    near_ref,
    left_ref,
    total_ref,
    off_ref,
    cell_ref,
    offset_ref,
    own_ref,
    pos_ref,
    mass_ref,
    len_ref,
    source_ref,
    sems,
):
    cells = mass_hbm.shape[0]
    me = own_index()
    targets = base_ref.shape[0]
    slots = act_ref.shape[0]
    base = me * cells - RIM
    copies = start_copies(
        (
            (len_hbm, len_ref),
            (ent_hbm, ent_ref),
            (rho_hbm, rho_ref),
            (pos_hbm, pos_ref),
            (mass_hbm, mass_ref),
            (source_hbm, source_ref),
            (dest_hbm, dest_ref),
        ),
        sems,
    )
    for entry in range(NBR):
        off_ref[pl.ds(entry * 8, 8), :] = offset_tile(entry)
    for slot in range(slots):
        mine = jnp.int32(0)
        for entry in range(NBR):
            cell = nbr_ref[slot, entry] - base
            near_by = jnp.logical_and(cell >= RIM, cell < RIM + cells)
            at = jnp.where(near_by, mine, NBR - 1 - entry + mine)
            cell_ref[place_of(slot, at)] = cell
            offset_ref[place_of(slot, at)] = entry
            mine = mine + jnp.where(near_by, 1, 0)
        own_ref[slot] = mine
    width = targets * capacity
    column = lax.broadcasted_iota(jnp.int32, (P_SIZE, width), 1)
    spot_of = lax.broadcasted_iota(jnp.int32, (P_SIZE, width), 0) - column % capacity
    for index in range(STATE):
        hit = jnp.where(spot_of == index * capacity, 1.0, 0.0)
        pick_ref[:, pl.ds(index * width, width)] = hit.astype(bf16)
    for copy in copies:
        copy.wait()
    inverse_len = 1.0 / len_ref[...]
    beta = beta_of(inverse_len, ent_ref[...], rho_ref[...])
    put_table(
        tab_ref, RIM, cells, pos_ref[0], pos_ref[1], pos_ref[2], mass_ref[...], inverse_len, beta
    )
    for slot in range(slots):
        home = act_ref[slot] - base
        own = tile_of(tab_ref, home)
        inverse_len = own[6:7, :]
        left = own_features(own, inverse_len * inverse_len)
        left_ref[pl.ds(slot * P_SIZE, P_SIZE), :] = left
        outer_sum = jnp.zeros((P_SIZE, P_SIZE), f32)
        inner_sum = jnp.zeros((P_SIZE, P_SIZE), f32)
        for first in range(0, early(slot), 2):
            tiles, weights = [], []
            positions = range(first, min(first + 2, early(slot)))
            for position in positions:
                valid = position < own_ref[slot]
                cell = jnp.where(valid, cell_ref[place_of(slot, position)], home)
                offset = jnp.where(valid, offset_ref[place_of(slot, position)], 0)
                tiles.append(stencil_tile(tab_ref, off_ref, cell, offset))
                weights.append(jnp.where(valid, 1.0, 0.0))
            outer, inner, kept = density_terms(left, tiles, weights)
            outer_sum, inner_sum = outer_sum + outer, inner_sum + inner
            for position, tile in zip(positions, kept):
                near_ref[pl.ds(place_of(slot, position) * 8, 8), :] = tile
        total_ref[pl.ds(slot * P_SIZE, P_SIZE), :] = outer_sum - 4.0 * inner_sum
    source = source_ref[...]
    cell_row = source // P_SIZE
    code_row = jnp.zeros_like(source)
    for slot in range(act_ref.shape[0]):
        mine = act_ref[slot] - me * cells
        named = jnp.logical_and(cell_row == mine, slot < cnt_ref[0])
        code_row = jnp.where(named, slot + 1, code_row)
    row_id = lax.broadcasted_iota(jnp.int32, (8, P_SIZE), 0)
    stack = jnp.zeros((8, P_SIZE), f32)
    for index, part in enumerate((cell_row, source % P_SIZE, dest_ref[...], code_row)):
        stack = jnp.where(row_id == index, part.astype(f32), stack)
    columns = stack.T
    shape = (P_SIZE, P_SIZE)
    cell, lane_of, dest, code = [jnp.broadcast_to(columns[:, i : i + 1], shape) for i in range(4)]
    lane = lax.broadcasted_iota(jnp.int32, shape, 1)
    row = lax.broadcasted_iota(jnp.int32, shape, 0)
    lane_f = lane.astype(f32)
    hit = lane_f == lane_of
    same = jnp.logical_and(dest == dest_ref[...].astype(f32), lane < row)
    rank = jnp.sum(jnp.where(same, 1.0, 0.0), axis=1, keepdims=True)
    wide = lax.broadcasted_iota(jnp.int32, (P_SIZE, cells), 1).astype(f32)
    pick = jnp.where(wide == columns[:, 0:1], 1.0, 0.0).astype(bf16)
    spot = lane_f - rank
    sent = jnp.zeros(shape, f32)
    planes = [pos_ref[0], pos_ref[1], pos_ref[2], mass_ref[...], len_ref[...], ent_ref[...], rho_ref[...]]
    for index, plane in enumerate(planes):
        found = sum(
            jnp.dot(pick, piece.astype(bf16), preferred_element_type=f32) for piece in split(plane)
        )
        keep = jnp.logical_and(hit, code == 0.0) if index == STATE - 1 else hit
        value = jnp.sum(jnp.where(keep, found, 0.0), axis=1, keepdims=True)
        sent = jnp.where(spot == float(index * capacity), value, sent)
    aim = lax.broadcasted_iota(jnp.int32, (targets, P_SIZE), 0) == dest_ref[...]
    aim = jnp.where(aim, 1.0, 0.0)
    base_ref[...] = jnp.dot(aim, sent, precision=lax.Precision.HIGHEST, preferred_element_type=f32)
    code_ref[...] = jnp.where(hit, code, 0.0)
    place_ref[...] = jnp.where(spot == float((STATE - 1) * capacity), 1.0, 0.0)


def density_kernel(
    rho_in,
    ent_ref,
    a_ref,
    b_ref,
    tab_in,
    near_in,
    base_ref,
    code_ref,
    place_ref,
    dest_ref,
    left_ref,
    total_in,
    off_ref,
    act_ref,
    cnt_ref,
    cell_ref,
    offset_ref,
    own_ref,
    new_ref,
    out_ref,
    tab_ref,
    near_ref,
    total_ref,
    names_a,
    names_b,
    made_ref,
    beta_ref,
    sems,
):
    cells = new_ref.shape[0]
    slots = act_ref.shape[0]
    me = own_index()
    odd = me % 2
    copies = start_copies(
        [
            (ref.at[pl.ds(PLANES * RIM, 8), :], names)
            for ref, names in ((a_ref, names_a), (b_ref, names_b))
        ],
        sems,
    )
    start_of_a = (1 - odd) * (cells + RIM)
    for in_ref, start in ((a_ref, start_of_a), (b_ref, cells + RIM - start_of_a)):
        put_table(tab_ref, start, RIM, *[in_ref[pl.ds(i * RIM, RIM), :] for i in range(PLANES)])

    for slot in range(slots):

        @pl.loop(own_ref[slot], early(slot))
        def _(position):
            place = place_of(slot, position)
            tile = stencil_tile(tab_ref, off_ref, cell_ref[place], offset_ref[place])
            span = pl.ds(slot * P_SIZE, P_SIZE)
            outer, inner, kept = density_terms(left_ref[span, :], [tile], [None])
            total_ref[span, :] = total_ref[span, :] + (outer - 4.0 * inner)
            near_ref[pl.ds(pl.multiple_of(place * 8, 8), 8), :] = kept[0]

    for slot in range(slots):
        mine = act_ref[slot] - me * cells
        inverse_len = tile_of(tab_ref, RIM + mine)[6:7, :]
        span = pl.ds(slot * P_SIZE, P_SIZE)
        left = left_ref[span, :]
        outer_sum = total_ref[span, :]
        inner_sum = jnp.zeros((P_SIZE, P_SIZE), f32)
        for first in range(early(slot), NBR, 2):
            positions = range(first, min(first + 2, NBR))
            tiles = []
            for position in positions:
                place = place_of(slot, position)
                tiles.append(stencil_tile(tab_ref, off_ref, cell_ref[place], offset_ref[place]))
            outer, inner, kept = density_terms(left, tiles, [None] * len(tiles))
            outer_sum, inner_sum = outer_sum + outer, inner_sum + inner
            for position, tile in zip(positions, kept):
                near_ref[pl.ds(place_of(slot, position) * 8, 8), :] = tile
        total = outer_sum - 4.0 * inner_sum
        made = row_sums(total) * (2.0 * kernel_norm) * inverse_len * inverse_len * inverse_len
        made = jnp.where(slot < cnt_ref[0], made, new_ref[pl.ds(mine, 1), :])
        beta = beta_of(inverse_len, ent_ref[pl.ds(mine, 1), :], made)
        made_ref[slot : slot + 1, :] = made
        beta_ref[slot : slot + 1, :] = beta

    for slot in range(slots):
        mine = act_ref[slot] - me * cells
        new_ref[pl.ds(mine, 1), :] = made_ref[slot : slot + 1, :]
        tab_ref[pl.ds((RIM + mine) * 8 + 7, 1), :] = beta_ref[slot : slot + 1, :]
    code = code_ref[...]
    chosen = jnp.zeros_like(code)
    for slot in range(slots):
        chosen = jnp.where(code == float(slot + 1), made_ref[slot : slot + 1, :], chosen)
    late = place_ref[...] * jnp.sum(chosen, axis=1, keepdims=True)
    targets = base_ref.shape[0]
    aim = lax.broadcasted_iota(jnp.int32, (targets, P_SIZE), 0) == dest_ref[...]
    aim = jnp.where(aim, 1.0, 0.0)
    for line in range(1, 8):
        fill = jnp.zeros((1, P_SIZE), f32) if line > slots else beta_ref[line - 1 : line, :]
        put(out_ref, 0, targets, line, jnp.broadcast_to(fill, (targets, P_SIZE)))
    sent = base_ref[...] + jnp.dot(
        aim, late, precision=lax.Precision.HIGHEST, preferred_element_type=f32
    )
    put(out_ref, 0, targets, 0, sent)
    for copy in copies:
        copy.wait()


def spline(base, slope, distance):
    step = distance * slope
    outer = jnp.maximum(base - step, 0.0)
    least = jnp.minimum(step, outer)
    return least * (outer + (outer - least))


def pull_sums(pulls, nears):
    row = row_ids()
    highs = [pull.astype(bf16) for pull in pulls]
    lows = [(pull - high.astype(f32)).astype(bf16) for pull, high in zip(pulls, highs)]
    sides = []
    for near in nears:
        weighed = jnp.where(row < 3, near, 1.0) * near[5:6, :]
        sides.append(jnp.concatenate(split(weighed), axis=0).astype(bf16))
    return lax.dot_general(
        jnp.concatenate(highs + lows, axis=1),
        jnp.concatenate(sides + sides, axis=1),
        (((1,), (1,)), ((), ())),
        preferred_element_type=f32,
    )


def force_kernel(
    tab_ref,
    near_ref,
    new_ref,
    names_a,
    names_b,
    act_ref,
    cnt_ref,
    cell_ref,
    acc_out,
    list_ref,
    new_out,
    left_ref,
    sems,
):
    cells = tab_ref.shape[0] // 8 - 2 * RIM
    me = own_index()
    odd = me % 2
    slots = act_ref.shape[0]
    copies = start_copies([(new_ref, new_out)], sems)
    fa = [names_a[0, s].astype(jnp.int32) for s in range(slots)]
    fb = [names_b[0, s].astype(jnp.int32) for s in range(slots)]
    left = [jnp.where(odd == 1, fa[s], fb[s]) for s in range(slots)]
    right = [jnp.where(odd == 1, fb[s], fa[s]) for s in range(slots)]
    left = [jnp.where(v >= cells - RIM, v - (cells - RIM), -1) for v in left]
    right = [jnp.where(jnp.logical_and(v >= 0, v < RIM), v + cells + RIM, -1) for v in right]
    at = jnp.int32(0)
    for slot in range(slots):
        live = slot < cnt_ref[0]
        mine = act_ref[slot] - me * cells
        own = tile_of(tab_ref, RIM + mine)
        columns = own.T
        own_base = jnp.broadcast_to(columns[:, 7:8], (P_SIZE, P_SIZE))
        own_slope = own_base * jnp.broadcast_to(columns[:, 6:7], (P_SIZE, P_SIZE))
        left_side = own_features(own, 1.0)
        left_ref[pl.ds(slot * P_SIZE, P_SIZE), :] = left_side
        sums = jnp.zeros((P_SIZE, 24), f32)
        for block in groups(SUM_GROUP):
            pulls, nears = [], []
            for first in range(block.start, block.stop, 2):
                group = range(first, min(first + 2, block.stop))
                tiles = [near_ref[pl.ds((slot * NBR + entry) * 8, 8), :] for entry in group]
                other = jnp.concatenate([other_features(tile) for tile in tiles], axis=1)
                squares = jnp.dot(left_side, other, preferred_element_type=f32)
                for place, entry in enumerate(group):
                    near = tiles[place]
                    cell = cell_ref[place_of(slot, entry)]
                    found = jnp.int32(-1)
                    for s in range(slots):
                        found = jnp.where(cell == left[s], s, found)
                        found = jnp.where(cell == right[s], slots + s, found)
                    list_ref[at + 1] = (slot * NBR + entry) * (2 * slots) + found
                    at = at + jnp.where(jnp.logical_and(found >= 0, live), 1, 0)

                    beta = tab_ref[pl.ds(cell * 8 + 7, 1), :]
                    slope = beta * near[6:7, :]
                    square = jnp.maximum(squares[:, place * P_SIZE : (place + 1) * P_SIZE], near[6:7, :] * TINY)
                    inverse = lax.rsqrt(square)
                    distance = square * inverse
                    pull = spline(own_base, own_slope, distance) + spline(beta, slope, distance)
                    pull = pull * inverse
                    pulls.append(pull)
                    nears.append(near)
            sums = sums + pull_sums(pulls, nears)
        flat = sums.T
        flat = flat[0:8, :] + flat[8:16, :] + flat[16:24, :]
        made = jnp.where(live, own * flat[3:4, :] - flat, 0.0)
        for axis in range(3):
            acc_out[axis, slot : slot + 1, :] = made[axis : axis + 1, :]
    list_ref[0] = at
    for copy in copies:
        copy.wait()


def finish_kernel(
    capacity,
    tab_ref,
    near_ref,
    part_ref,
    got_ref,
    pick_ref,
    left_ref,
    list_ref,
    act_ref,
    acc_out,
    arrive_ref,
    late_ref,
):
    cells = tab_ref.shape[0] // 8 - 2 * RIM
    me = own_index()
    slots = act_ref.shape[0]
    targets = got_ref.shape[0] // 8
    acc_out[...] = part_ref[...]
    rows = got_ref[pl.ds(0, targets, stride=8), :]
    width = targets * capacity
    sender = lax.broadcasted_iota(jnp.int32, (targets, width), 1) // capacity
    mask = sender == lax.broadcasted_iota(jnp.int32, (targets, width), 0)
    pieces = jnp.concatenate(split(rows), axis=0).astype(bf16)
    spread = jnp.dot(pieces, pick_ref[...], preferred_element_type=f32)
    spread = spread[0:targets] + spread[targets : 2 * targets] + spread[2 * targets :]
    for index in range(STATE):
        part = spread[:, index * width : (index + 1) * width]
        arrive_ref[index : index + 1, :] = jnp.sum(jnp.where(mask, part, 0.0), axis=0, keepdims=True)

    count = list_ref[0]

    @pl.when(count > 0)
    def _():
        late_ref[...] = jnp.zeros_like(late_ref)

        @pl.loop(0, (count + ITEMS - 1) // ITEMS)
        def _(block):
            made = []
            for step in range(ITEMS):
                item = block * ITEMS + step
                word = list_ref[jnp.minimum(item, count - 1) + 1]
                found = word % (2 * slots)
                place = word // (2 * slots)
                slot = place // NBR
                span = pl.ds(pl.multiple_of(slot * P_SIZE, P_SIZE), P_SIZE)
                other = jnp.where(found < slots, me - 1, me + 1)
                near = near_ref[pl.ds(pl.multiple_of(place * 8, 8), 8), :]
                beta = got_ref[pl.ds(other * 8 + 1 + found % slots, 1), :]
                beta = beta * jnp.where(item < count, 1.0, 0.0)
                square = jnp.dot(
                    left_ref[span, :], other_features(near), preferred_element_type=f32
                )
                square = jnp.maximum(square, near[6:7, :] * TINY)
                inverse = lax.rsqrt(square)
                pull = spline(beta, beta * near[6:7, :], square * inverse) * inverse
                made.append((span, pull_sums([pull], [near])))
            for span, sums in made:
                late_ref[span, :] = late_ref[span, :] + sums

        for slot in range(slots):
            own = tile_of(tab_ref, RIM + act_ref[slot] - me * cells)
            flat = late_ref[pl.ds(slot * P_SIZE, P_SIZE), :].T
            flat = flat[0:8, :] + flat[8:16, :] + flat[16:24, :]
            made = own * flat[3:4, :] - flat
            for axis in range(3):
                acc_out[axis, slot : slot + 1, :] += made[axis : axis + 1, :]


def local(
    positions,
    masses,
    smoothing,
    entropy,
    density,
    active_cells,
    active_count,
    neighbours,
    mig_source,
    mig_dest,
):
    cells = masses.shape[0]
    slots = active_cells.shape[0]
    devices = lax.axis_size(AXES)
    mig_rows = mig_source.shape[0]
    capacity = max(2, 2 * mig_rows // devices)
    shape = jax.ShapeDtypeStruct
    rim_shape = shape((PLANES * RIM + 8, P_SIZE), f32)
    tab_shape = pltpu.VMEM(((cells + 2 * RIM) * 8, P_SIZE), f32)
    near_shape = pltpu.VMEM((slots * NBR * 8, P_SIZE), f32)
    name_shape = pltpu.SMEM((8, P_SIZE), f32)
    fields = (positions, masses, smoothing, entropy, density)
    rows = (mig_source.reshape(1, mig_rows), mig_dest.reshape(1, mig_rows))
    lists = (active_cells, neighbours)

    raw = [in_hbm(v) for v in fields]
    send_b, send_a, active, near_ids = pl.pallas_call(
        pack_kernel,
        out_shape=(rim_shape, rim_shape) + tuple(pltpu.SMEM(v.shape, v.dtype) for v in lists),
        in_specs=[HBM] * 7 + [SMEM],
        out_specs=(VMEM,) * 2 + (SMEM,) * 2,
        scratch_shapes=[
            pltpu.VMEM((2, 3, RIM, P_SIZE), f32),
            pltpu.SemaphoreType.DMA((16,)),
        ],
        compiler_params=PARAMS,
        name="pack",
    )(*raw, *[in_hbm(v) for v in lists], active_count)

    pairs_a = [(i ^ 1, i) for i in range(devices) if i ^ 1 < devices]
    pairs_b = []
    for i in range(1, devices - 1, 2):
        pairs_b += [(i, i + 1), (i + 1, i)]
    got_b = lax.ppermute(send_b, AXES, pairs_b)
    got_a = lax.ppermute(send_a, AXES, pairs_a)

    ent, rho, dest, table, base, code, place, pick, near, left, total, offsets, *found = pl.pallas_call(
        functools.partial(migrant_kernel, capacity),
        out_shape=(
            pltpu.VMEM((cells, P_SIZE), f32),
            pltpu.VMEM((cells, P_SIZE), f32),
            pltpu.VMEM((1, mig_rows), jnp.int32),
            tab_shape,
            pltpu.VMEM((devices, P_SIZE), f32),
            pltpu.VMEM((mig_rows, P_SIZE), f32),
            pltpu.VMEM((mig_rows, P_SIZE), f32),
            pltpu.VMEM((P_SIZE, STATE * devices * capacity), bf16),
            near_shape,
            pltpu.VMEM((slots * P_SIZE, 48), bf16),
            pltpu.VMEM((slots * P_SIZE, P_SIZE), f32),
            pltpu.VMEM((NBR * 8, P_SIZE), f32),
            pltpu.SMEM((slots * NBR,), jnp.int32),
            pltpu.SMEM((slots * NBR,), jnp.int32),
            pltpu.SMEM((slots,), jnp.int32),
        ),
        in_specs=[HBM] * 7 + [SMEM] * 3,
        out_specs=(VMEM,) * 12 + (SMEM,) * 3,
        scratch_shapes=[
            pltpu.VMEM((3, cells, P_SIZE), f32),
            pltpu.VMEM((cells, P_SIZE), f32),
            pltpu.VMEM((cells, P_SIZE), f32),
            pltpu.VMEM((1, mig_rows), jnp.int32),
            pltpu.SemaphoreType.DMA((7,)),
        ],
        compiler_params=PARAMS,
        name="migrants",
    )(*raw, *[in_hbm(v) for v in rows], active, active_count, near_ids)

    made, outgoing, table, near, _, names_a, names_b = pl.pallas_call(
        density_kernel,
        out_shape=(
            pltpu.VMEM((cells, P_SIZE), f32),
            shape((devices * 8, P_SIZE), f32),
            tab_shape,
            near_shape,
            pltpu.VMEM((slots * P_SIZE, P_SIZE), f32),
            name_shape,
            name_shape,
        ),
        in_specs=[VMEM] * 13 + [SMEM] * 5,
        out_specs=(VMEM,) * 5 + (SMEM,) * 2,
        input_output_aliases={0: 0, 4: 2, 5: 3, 11: 4},
        scratch_shapes=[
            pltpu.VMEM((8, P_SIZE), f32),
            pltpu.VMEM((8, P_SIZE), f32),
            pltpu.SemaphoreType.DMA((2,)),
        ],
        compiler_params=PARAMS,
        name="density",
    )(
        rho,
        ent,
        got_a,
        got_b,
        table,
        near,
        base,
        code,
        place,
        dest,
        left,
        total,
        offsets,
        active,
        active_count,
        *found,
    )

    incoming = lax.all_to_all(outgoing, AXES, split_axis=0, concat_axis=0, tiled=True)

    todo_len = pl.cdiv(slots * NBR + 2, P_SIZE) * P_SIZE
    partial, todo, new_density, left = pl.pallas_call(
        force_kernel,
        out_shape=(
            shape((3, slots, P_SIZE), f32),
            pltpu.SMEM((todo_len,), jnp.int32),
            shape((cells, P_SIZE), f32),
            pltpu.VMEM((slots * P_SIZE, 48), bf16),
        ),
        in_specs=[VMEM] * 3 + [SMEM] * 5,
        out_specs=(VMEM, SMEM, HBM, VMEM),
        scratch_shapes=[
            pltpu.SemaphoreType.DMA((1,)),
        ],
        compiler_params=PARAMS,
        name="force",
    )(table, near, made, names_a, names_b, active, active_count, found[0])

    acceleration, arrivals = pl.pallas_call(
        functools.partial(finish_kernel, capacity),
        out_shape=(
            shape((3, slots, P_SIZE), f32),
            shape((STATE, devices * capacity), f32),
        ),
        in_specs=[VMEM] * 6 + [SMEM] * 2,
        out_specs=(VMEM, VMEM),
        scratch_shapes=[pltpu.VMEM((slots * P_SIZE, 24), f32)],
        compiler_params=PARAMS,
        name="finish",
    )(table, near, partial, incoming, pick, left, todo, active)
    return (new_density, acceleration, arrivals)


def solution(mesh):
    placed = (
        P(None, AXES, None),
        P(AXES, None),
        P(AXES, None),
        P(AXES, None),
        P(AXES, None),
        P(AXES),
        P(AXES),
        P(AXES, None),
        P(AXES),
        P(AXES, None),
    )
    return jax.shard_map(
        local,
        mesh=mesh,
        in_specs=placed,
        out_specs=(P(AXES, None), P(None, AXES, None), P(None, AXES)),
        check_vma=False,
    )
```

```python
import functools
import math

import jax
import jax.numpy as jnp
from jax import lax
from jax.experimental import pallas as pl
from jax.experimental.pallas import tpu as pltpu
from jax.sharding import PartitionSpec as P

P_SIZE = 128
NBR = 27
RIM = 64
STATE = 7
PLANES = 6
SUM_GROUP = 8
EARLY_FIRST = 6
EARLY = 13
JOBS = 10
ITEMS = 4
TINY = 1e-9
AXES = ("gx", "gy")

kernel_norm = 8.0 / math.pi
log_six_norm = math.log(6.0 * kernel_norm)
f32 = jnp.float32
bf16 = jnp.bfloat16
VMEM = pl.BlockSpec(memory_space=pltpu.VMEM)
SMEM = pl.BlockSpec(memory_space=pltpu.SMEM)
HBM = pl.BlockSpec(memory_space=pltpu.HBM)
PARAMS = pltpu.CompilerParams(vmem_limit_bytes=16 << 20)


def in_hbm(value):
    return pltpu.with_memory_space_constraint(value, pltpu.HBM)


def own_index():
    return lax.axis_index("gx") * lax.axis_size("gy") + lax.axis_index("gy")


def beta_of(inverse_len, entropy, density):
    power = 0.5 * (log_six_norm + jnp.log(entropy)) - jnp.log(density) * (1.0 / 6.0)
    return inverse_len * inverse_len * jnp.exp(power)


def row_sums(block):
    return jnp.sum(block.T, axis=0, keepdims=True)


def offset_tile(entry):
    row = lax.broadcasted_iota(jnp.int32, (8, P_SIZE), 0)
    shift = (entry // 9 - 1, entry // 3 % 3 - 1, entry % 3 - 1)
    tile = jnp.zeros((8, P_SIZE), f32)
    for axis in range(3):
        if shift[axis]:
            tile = jnp.where(row == axis, float(shift[axis]), tile)
    return tile


def split(value):
    high = value.astype(bf16).astype(f32)
    rest = value - high
    middle = rest.astype(bf16).astype(f32)
    return high, middle, rest - middle


def start_copies(pairs, sems):
    copies = [pltpu.make_async_copy(src, dst, sems.at[i]) for i, (src, dst) in enumerate(pairs)]
    for copy in copies:
        copy.start()
    return copies


def put(tab_ref, cell, count, row, plane):
    tab_ref[pl.ds(cell * 8 + row, count, stride=8), :] = plane


def tile_of(tab_ref, cell):
    return tab_ref[pl.ds(pl.multiple_of(cell * 8, 8), 8), :]


def put_table(tab_ref, cell, count, x, y, z, mass, inverse_len, beta):
    cube_root = jnp.exp(jnp.log(mass) * (1.0 / 3.0))
    planes = (x - 0.5, y - 0.5, z - 0.5, None, cube_root, mass, inverse_len, beta)
    for row, plane in enumerate(planes):
        if plane is not None:
            put(tab_ref, cell, count, row, plane)


def pack_kernel(
    pos_hbm,
    mass_hbm,
    len_hbm,
    ent_hbm,
    rho_hbm,
    act_hbm,
    nbr_hbm,
    cnt_ref,
    b_ref,
    a_ref,
    act_ref,
    nbr_ref,
    rim_ref,
    sems,
):
    cells = mass_hbm.shape[0]
    me = own_index()
    odd = me % 2
    start_a = pl.multiple_of((1 - odd) * (cells - RIM), RIM)
    start_b = pl.multiple_of(odd * (cells - RIM), RIM)
    sides = ((b_ref, start_b), (a_ref, start_a))
    pairs = [(act_hbm, act_ref)]
    for side, (out_ref, start) in enumerate(sides):
        rows = pl.ds(start, RIM)
        for index, ref in enumerate((len_hbm, ent_hbm, rho_hbm)):
            pairs.append((ref.at[rows, :], rim_ref.at[side, index]))
    first = len(pairs)
    for out_ref, start in sides:
        rows = pl.ds(start, RIM)
        for axis in range(3):
            pairs.append((pos_hbm.at[axis, rows, :], out_ref.at[pl.ds(axis * RIM, RIM), :]))
        pairs.append((mass_hbm.at[rows, :], out_ref.at[pl.ds(3 * RIM, RIM), :]))
    pairs.append((nbr_hbm, nbr_ref))
    copies = start_copies(pairs, sems)
    for copy in copies[:first]:
        copy.wait()
    lane = lax.broadcasted_iota(jnp.int32, (8, P_SIZE), 1)
    names = jnp.full((8, P_SIZE), -1.0, f32)
    slots = act_ref.shape[0]
    for slot in range(slots):
        mine = act_ref[slot] - me * cells
        live = slot < cnt_ref[0]
        names = jnp.where(jnp.logical_and(lane == slot, live), mine.astype(f32), names)
    cell = lax.broadcasted_iota(jnp.int32, (RIM, P_SIZE), 0)
    for side, (out_ref, start) in enumerate(sides):
        inverse_len = 1.0 / rim_ref[side, 0]
        beta = beta_of(inverse_len, rim_ref[side, 1], rim_ref[side, 2])
        for slot in range(slots):
            mine = jnp.where(slot < cnt_ref[0], act_ref[slot] - me * cells - start, -1)
            beta = jnp.where(cell == mine, 0.0, beta)
        out_ref[pl.ds(4 * RIM, RIM), :] = inverse_len
        out_ref[pl.ds(5 * RIM, RIM), :] = beta
        out_ref[pl.ds(PLANES * RIM, 8), :] = names
    for copy in copies[first:]:
        copy.wait()


def squared_length(tile):
    square = tile * tile
    return square[0:1, :] + square[1:2, :] + square[2:3, :]


def row_ids():
    return lax.broadcasted_iota(jnp.int32, (8, P_SIZE), 0)


def own_features(tile, scale):
    row = row_ids()
    lead = jnp.where(row < 3, -2.0 * tile, 1.0)
    lead = jnp.where(row == 4, squared_length(tile), lead)
    lead = jnp.where(row < 5, lead * scale, 0.0)
    high, middle, low = split(lead)
    return jnp.concatenate([high, high, middle, middle, high, low], axis=0).T.astype(bf16)


def other_features(tile):
    high, middle, low = split(tile)
    return jnp.concatenate([high, middle, high, middle, low, high], axis=0).astype(bf16)


def groups(size):
    return [range(first, min(first + size, NBR)) for first in range(0, NBR, size)]


def early(slot):
    return EARLY if slot else EARLY_FIRST


def stencil_tile(tab_ref, off_ref, cell, offset):
    tile = tile_of(tab_ref, cell) + tile_of(off_ref, offset)
    return jnp.where(row_ids() == 3, squared_length(tile), tile)


def density_terms(left, tiles, weights):
    row = row_ids()
    parts, roots, kept = [], [], []
    for tile, weight in zip(tiles, weights):
        root = tile[4:5, :] if weight is None else tile[4:5, :] * weight
        one = jnp.where(row == 4, 1.0, tile)
        parts.append(other_features(one * (root * root)))
        roots.append(root)
        kept.append(one)
    squares = jnp.dot(left, jnp.concatenate(parts, axis=1), preferred_element_type=f32)
    outer_sum = inner_sum = None
    for place, root in enumerate(roots):
        square = squares[:, place * P_SIZE : (place + 1) * P_SIZE]
        square = jnp.maximum(square, kept[place][6:7, :] * TINY)
        ratio = square * lax.rsqrt(square)
        outer = jnp.maximum(root - ratio, 0.0)
        inner = jnp.maximum(0.5 * root - ratio, 0.0)
        outer, inner = outer * outer * outer, inner * inner * inner
        outer_sum = outer if outer_sum is None else outer_sum + outer
        inner_sum = inner if inner_sum is None else inner_sum + inner
    return outer_sum, inner_sum, kept


def place_of(slot, position):
    return slot * NBR + position


def migrant_kernel(
    capacity,
    pos_hbm,
    mass_hbm,
    len_hbm,
    ent_hbm,
    rho_hbm,
    source_hbm,
    dest_hbm,
    act_ref,
    cnt_ref,
    nbr_ref,
    ent_ref,
    rho_ref,
    dest_ref,
    tab_ref,
    base_ref,
    code_ref,
    place_ref,
    pick_ref,
    near_ref,
    left_ref,
    total_ref,
    off_ref,
    cell_ref,
    offset_ref,
    job_ref,
    span_ref,
    pos_ref,
    mass_ref,
    len_ref,
    source_ref,
    sems,
):
    cells = mass_hbm.shape[0]
    me = own_index()
    targets = base_ref.shape[0]
    slots = act_ref.shape[0]
    base = me * cells - RIM
    copies = start_copies(
        (
            (len_hbm, len_ref),
            (ent_hbm, ent_ref),
            (rho_hbm, rho_ref),
            (pos_hbm, pos_ref),
            (mass_hbm, mass_ref),
            (source_hbm, source_ref),
            (dest_hbm, dest_ref),
        ),
        sems,
    )
    for entry in range(NBR):
        off_ref[pl.ds(entry * 8, 8), :] = offset_tile(entry)
    owned = []
    for slot in range(slots):
        mine = jnp.int32(0)
        for entry in range(NBR):
            cell = nbr_ref[slot, entry] - base
            near_by = jnp.logical_and(cell >= RIM, cell < RIM + cells)
            at = jnp.where(near_by, mine, NBR - 1 - entry + mine)
            cell_ref[place_of(slot, at)] = cell
            offset_ref[place_of(slot, at)] = entry
            mine = mine + jnp.where(near_by, 1, 0)
        owned.append(mine)
    at = jnp.int32(0)
    for slot in range(slots):
        for position in range(early(slot)):
            job_ref[at + 1] = place_of(slot, position)
            span_ref[at] = slot * P_SIZE
            at = at + jnp.where(position >= owned[slot], 1, 0)
    job_ref[0] = at
    width = targets * capacity
    column = lax.broadcasted_iota(jnp.int32, (P_SIZE, width), 1)
    spot_of = lax.broadcasted_iota(jnp.int32, (P_SIZE, width), 0) - column % capacity
    for index in range(STATE):
        hit = jnp.where(spot_of == index * capacity, 1.0, 0.0)
        pick_ref[:, pl.ds(index * width, width)] = hit.astype(bf16)
    for copy in copies:
        copy.wait()
    inverse_len = 1.0 / len_ref[...]
    beta = beta_of(inverse_len, ent_ref[...], rho_ref[...])
    put_table(
        tab_ref, RIM, cells, pos_ref[0], pos_ref[1], pos_ref[2], mass_ref[...], inverse_len, beta
    )
    for slot in range(slots):
        home = act_ref[slot] - base
        own = tile_of(tab_ref, home)
        inverse_len = own[6:7, :]
        left = own_features(own, inverse_len * inverse_len)
        left_ref[pl.ds(slot * P_SIZE, P_SIZE), :] = left
        outer_sum = jnp.zeros((P_SIZE, P_SIZE), f32)
        inner_sum = jnp.zeros((P_SIZE, P_SIZE), f32)
        for first in range(0, early(slot), 2):
            tiles, weights = [], []
            positions = range(first, min(first + 2, early(slot)))
            for position in positions:
                valid = position < owned[slot]
                cell = jnp.where(valid, cell_ref[place_of(slot, position)], home)
                offset = jnp.where(valid, offset_ref[place_of(slot, position)], 0)
                tiles.append(stencil_tile(tab_ref, off_ref, cell, offset))
                weights.append(jnp.where(valid, 1.0, 0.0))
            outer, inner, kept = density_terms(left, tiles, weights)
            outer_sum, inner_sum = outer_sum + outer, inner_sum + inner
            for position, tile in zip(positions, kept):
                near_ref[pl.ds(place_of(slot, position) * 8, 8), :] = tile
        total_ref[pl.ds(slot * P_SIZE, P_SIZE), :] = outer_sum - 4.0 * inner_sum
    source = source_ref[...]
    cell_row = source // P_SIZE
    code_row = jnp.zeros_like(source)
    for slot in range(act_ref.shape[0]):
        mine = act_ref[slot] - me * cells
        named = jnp.logical_and(cell_row == mine, slot < cnt_ref[0])
        code_row = jnp.where(named, slot + 1, code_row)
    row_id = lax.broadcasted_iota(jnp.int32, (8, P_SIZE), 0)
    stack = jnp.zeros((8, P_SIZE), f32)
    for index, part in enumerate((cell_row, source % P_SIZE, dest_ref[...], code_row)):
        stack = jnp.where(row_id == index, part.astype(f32), stack)
    columns = stack.T
    shape = (P_SIZE, P_SIZE)
    cell, lane_of, dest, code = [jnp.broadcast_to(columns[:, i : i + 1], shape) for i in range(4)]
    lane = lax.broadcasted_iota(jnp.int32, shape, 1)
    row = lax.broadcasted_iota(jnp.int32, shape, 0)
    lane_f = lane.astype(f32)
    hit = lane_f == lane_of
    same = jnp.logical_and(dest == dest_ref[...].astype(f32), lane < row)
    rank = jnp.sum(jnp.where(same, 1.0, 0.0), axis=1, keepdims=True)
    wide = lax.broadcasted_iota(jnp.int32, (P_SIZE, cells), 1).astype(f32)
    pick = jnp.where(wide == columns[:, 0:1], 1.0, 0.0).astype(bf16)
    spot = lane_f - rank
    sent = jnp.zeros(shape, f32)
    planes = [pos_ref[0], pos_ref[1], pos_ref[2], mass_ref[...], len_ref[...], ent_ref[...], rho_ref[...]]
    for index, plane in enumerate(planes):
        found = sum(
            jnp.dot(pick, piece.astype(bf16), preferred_element_type=f32) for piece in split(plane)
        )
        keep = jnp.logical_and(hit, code == 0.0) if index == STATE - 1 else hit
        value = jnp.sum(jnp.where(keep, found, 0.0), axis=1, keepdims=True)
        sent = jnp.where(spot == float(index * capacity), value, sent)
    aim = lax.broadcasted_iota(jnp.int32, (targets, P_SIZE), 0) == dest_ref[...]
    aim = jnp.where(aim, 1.0, 0.0)
    base_ref[...] = jnp.dot(aim, sent, precision=lax.Precision.HIGHEST, preferred_element_type=f32)
    code_ref[...] = jnp.where(hit, code, 0.0)
    place_ref[...] = jnp.where(spot == float((STATE - 1) * capacity), 1.0, 0.0)


def density_kernel(
    rho_in,
    ent_ref,
    a_ref,
    b_ref,
    tab_in,
    near_in,
    base_ref,
    code_ref,
    place_ref,
    dest_ref,
    left_ref,
    total_in,
    off_ref,
    act_ref,
    cnt_ref,
    cell_ref,
    offset_ref,
    job_ref,
    span_ref,
    new_ref,
    out_ref,
    tab_ref,
    near_ref,
    total_ref,
    names_a,
    names_b,
    made_ref,
    beta_ref,
    sems,
):
    cells = new_ref.shape[0]
    slots = act_ref.shape[0]
    me = own_index()
    odd = me % 2
    copies = start_copies(
        [
            (ref.at[pl.ds(PLANES * RIM, 8), :], names)
            for ref, names in ((a_ref, names_a), (b_ref, names_b))
        ],
        sems,
    )
    start_of_a = (1 - odd) * (cells + RIM)
    for in_ref, start in ((a_ref, start_of_a), (b_ref, cells + RIM - start_of_a)):
        put_table(tab_ref, start, RIM, *[in_ref[pl.ds(i * RIM, RIM), :] for i in range(PLANES)])

    jobs = job_ref[0]

    def late_entry(job, place, weight):
        tile = stencil_tile(tab_ref, off_ref, cell_ref[place], offset_ref[place])
        span = pl.ds(pl.multiple_of(span_ref[job], P_SIZE), P_SIZE)
        outer, inner, kept = density_terms(left_ref[span, :], [tile], [weight])
        total_ref[span, :] = total_ref[span, :] + (outer - 4.0 * inner)
        return kept[0]

    @pl.loop(JOBS, jobs)
    def _(job):
        place = job_ref[job + 1]
        near_ref[pl.ds(pl.multiple_of(place * 8, 8), 8), :] = late_entry(job, place, None)

    for turn in range(JOBS):
        valid = turn < jobs
        job = jnp.where(valid, turn, 0)
        place = jnp.where(valid, job_ref[turn + 1], 0)
        kept = late_entry(job, place, jnp.where(valid, 1.0, 0.0))
        target = jnp.where(valid, place, slots * NBR)
        near_ref[pl.ds(pl.multiple_of(target * 8, 8), 8), :] = kept

    for slot in range(slots):
        mine = act_ref[slot] - me * cells
        inverse_len = tile_of(tab_ref, RIM + mine)[6:7, :]
        span = pl.ds(slot * P_SIZE, P_SIZE)
        left = left_ref[span, :]
        outer_sum = jnp.zeros((P_SIZE, P_SIZE), f32)
        inner_sum = jnp.zeros((P_SIZE, P_SIZE), f32)
        for first in range(early(slot), NBR, 2):
            positions = range(first, min(first + 2, NBR))
            tiles = []
            for position in positions:
                place = place_of(slot, position)
                tiles.append(stencil_tile(tab_ref, off_ref, cell_ref[place], offset_ref[place]))
            outer, inner, kept = density_terms(left, tiles, [None] * len(tiles))
            outer_sum, inner_sum = outer_sum + outer, inner_sum + inner
            for position, tile in zip(positions, kept):
                near_ref[pl.ds(place_of(slot, position) * 8, 8), :] = tile
        total = total_ref[span, :] + (outer_sum - 4.0 * inner_sum)
        made = row_sums(total) * (2.0 * kernel_norm) * inverse_len * inverse_len * inverse_len
        made = jnp.where(slot < cnt_ref[0], made, new_ref[pl.ds(mine, 1), :])
        beta = beta_of(inverse_len, ent_ref[pl.ds(mine, 1), :], made)
        made_ref[slot : slot + 1, :] = made
        beta_ref[slot : slot + 1, :] = beta

    for slot in range(slots):
        mine = act_ref[slot] - me * cells
        new_ref[pl.ds(mine, 1), :] = made_ref[slot : slot + 1, :]
        tab_ref[pl.ds((RIM + mine) * 8 + 7, 1), :] = beta_ref[slot : slot + 1, :]
    code = code_ref[...]
    chosen = jnp.zeros_like(code)
    for slot in range(slots):
        chosen = jnp.where(code == float(slot + 1), made_ref[slot : slot + 1, :], chosen)
    late = place_ref[...] * jnp.sum(chosen, axis=1, keepdims=True)
    targets = base_ref.shape[0]
    aim = lax.broadcasted_iota(jnp.int32, (targets, P_SIZE), 0) == dest_ref[...]
    aim = jnp.where(aim, 1.0, 0.0)
    for line in range(1, 8):
        fill = jnp.zeros((1, P_SIZE), f32) if line > slots else beta_ref[line - 1 : line, :]
        put(out_ref, 0, targets, line, jnp.broadcast_to(fill, (targets, P_SIZE)))
    sent = base_ref[...] + jnp.dot(
        aim, late, precision=lax.Precision.HIGHEST, preferred_element_type=f32
    )
    put(out_ref, 0, targets, 0, sent)
    for copy in copies:
        copy.wait()


def spline(base, slope, distance):
    step = distance * slope
    outer = jnp.maximum(base - step, 0.0)
    least = jnp.minimum(step, outer)
    return least * (outer + (outer - least))


def pull_sums(pulls, nears):
    row = row_ids()
    highs = [pull.astype(bf16) for pull in pulls]
    lows = [(pull - high.astype(f32)).astype(bf16) for pull, high in zip(pulls, highs)]
    sides = []
    for near in nears:
        weighed = jnp.where(row < 3, near, 1.0) * near[5:6, :]
        sides.append(jnp.concatenate(split(weighed), axis=0).astype(bf16))
    return lax.dot_general(
        jnp.concatenate(highs + lows, axis=1),
        jnp.concatenate(sides + sides, axis=1),
        (((1,), (1,)), ((), ())),
        preferred_element_type=f32,
    )


def force_kernel(
    tab_ref,
    near_ref,
    new_ref,
    names_a,
    names_b,
    act_ref,
    cnt_ref,
    cell_ref,
    acc_out,
    list_ref,
    new_out,
    left_ref,
    sems,
):
    cells = tab_ref.shape[0] // 8 - 2 * RIM
    me = own_index()
    odd = me % 2
    slots = act_ref.shape[0]
    copies = start_copies([(new_ref, new_out)], sems)
    fa = [names_a[0, s].astype(jnp.int32) for s in range(slots)]
    fb = [names_b[0, s].astype(jnp.int32) for s in range(slots)]
    left = [jnp.where(odd == 1, fa[s], fb[s]) for s in range(slots)]
    right = [jnp.where(odd == 1, fb[s], fa[s]) for s in range(slots)]
    left = [jnp.where(v >= cells - RIM, v - (cells - RIM), -1) for v in left]
    right = [jnp.where(jnp.logical_and(v >= 0, v < RIM), v + cells + RIM, -1) for v in right]
    at = jnp.int32(0)
    for slot in range(slots):
        live = slot < cnt_ref[0]
        mine = act_ref[slot] - me * cells
        own = tile_of(tab_ref, RIM + mine)
        columns = own.T
        own_base = jnp.broadcast_to(columns[:, 7:8], (P_SIZE, P_SIZE))
        own_slope = own_base * jnp.broadcast_to(columns[:, 6:7], (P_SIZE, P_SIZE))
        left_side = own_features(own, 1.0)
        left_ref[pl.ds(slot * P_SIZE, P_SIZE), :] = left_side
        sums = jnp.zeros((P_SIZE, 24), f32)
        for block in groups(SUM_GROUP):
            pulls, nears = [], []
            for first in range(block.start, block.stop, 2):
                group = range(first, min(first + 2, block.stop))
                tiles = [near_ref[pl.ds((slot * NBR + entry) * 8, 8), :] for entry in group]
                other = jnp.concatenate([other_features(tile) for tile in tiles], axis=1)
                squares = jnp.dot(left_side, other, preferred_element_type=f32)
                for place, entry in enumerate(group):
                    near = tiles[place]
                    cell = cell_ref[place_of(slot, entry)]
                    found = jnp.int32(-1)
                    for s in range(slots):
                        found = jnp.where(cell == left[s], s, found)
                        found = jnp.where(cell == right[s], slots + s, found)
                    list_ref[at + 1] = (slot * NBR + entry) * (2 * slots) + found
                    at = at + jnp.where(jnp.logical_and(found >= 0, live), 1, 0)

                    beta = tab_ref[pl.ds(cell * 8 + 7, 1), :]
                    slope = beta * near[6:7, :]
                    square = jnp.maximum(squares[:, place * P_SIZE : (place + 1) * P_SIZE], near[6:7, :] * TINY)
                    inverse = lax.rsqrt(square)
                    distance = square * inverse
                    pull = spline(own_base, own_slope, distance) + spline(beta, slope, distance)
                    pull = pull * inverse
                    pulls.append(pull)
                    nears.append(near)
            sums = sums + pull_sums(pulls, nears)
        flat = sums.T
        flat = flat[0:8, :] + flat[8:16, :] + flat[16:24, :]
        made = jnp.where(live, own * flat[3:4, :] - flat, 0.0)
        for axis in range(3):
            acc_out[axis, slot : slot + 1, :] = made[axis : axis + 1, :]
    list_ref[0] = at
    for copy in copies:
        copy.wait()


def finish_kernel(
    capacity,
    tab_ref,
    near_ref,
    part_ref,
    got_ref,
    pick_ref,
    left_ref,
    list_ref,
    act_ref,
    acc_out,
    arrive_ref,
    late_ref,
):
    cells = tab_ref.shape[0] // 8 - 2 * RIM
    me = own_index()
    slots = act_ref.shape[0]
    targets = got_ref.shape[0] // 8
    acc_out[...] = part_ref[...]
    rows = got_ref[pl.ds(0, targets, stride=8), :]
    width = targets * capacity
    sender = lax.broadcasted_iota(jnp.int32, (targets, width), 1) // capacity
    mask = sender == lax.broadcasted_iota(jnp.int32, (targets, width), 0)
    pieces = jnp.concatenate(split(rows), axis=0).astype(bf16)
    spread = jnp.dot(pieces, pick_ref[...], preferred_element_type=f32)
    spread = spread[0:targets] + spread[targets : 2 * targets] + spread[2 * targets :]
    for index in range(STATE):
        part = spread[:, index * width : (index + 1) * width]
        arrive_ref[index : index + 1, :] = jnp.sum(jnp.where(mask, part, 0.0), axis=0, keepdims=True)

    count = list_ref[0]

    @pl.when(count > 0)
    def _():
        late_ref[...] = jnp.zeros_like(late_ref)

        @pl.loop(0, (count + ITEMS - 1) // ITEMS)
        def _(block):
            made = []
            for step in range(ITEMS):
                item = block * ITEMS + step
                word = list_ref[jnp.minimum(item, count - 1) + 1]
                found = word % (2 * slots)
                place = word // (2 * slots)
                slot = place // NBR
                span = pl.ds(pl.multiple_of(slot * P_SIZE, P_SIZE), P_SIZE)
                other = jnp.where(found < slots, me - 1, me + 1)
                near = near_ref[pl.ds(pl.multiple_of(place * 8, 8), 8), :]
                beta = got_ref[pl.ds(other * 8 + 1 + found % slots, 1), :]
                beta = beta * jnp.where(item < count, 1.0, 0.0)
                square = jnp.dot(
                    left_ref[span, :], other_features(near), preferred_element_type=f32
                )
                square = jnp.maximum(square, near[6:7, :] * TINY)
                inverse = lax.rsqrt(square)
                pull = spline(beta, beta * near[6:7, :], square * inverse) * inverse
                made.append((span, pull_sums([pull], [near])))
            for span, sums in made:
                late_ref[span, :] = late_ref[span, :] + sums

        for slot in range(slots):
            own = tile_of(tab_ref, RIM + act_ref[slot] - me * cells)
            flat = late_ref[pl.ds(slot * P_SIZE, P_SIZE), :].T
            flat = flat[0:8, :] + flat[8:16, :] + flat[16:24, :]
            made = own * flat[3:4, :] - flat
            for axis in range(3):
                acc_out[axis, slot : slot + 1, :] += made[axis : axis + 1, :]


def local(
    positions,
    masses,
    smoothing,
    entropy,
    density,
    active_cells,
    active_count,
    neighbours,
    mig_source,
    mig_dest,
):
    cells = masses.shape[0]
    slots = active_cells.shape[0]
    devices = lax.axis_size(AXES)
    mig_rows = mig_source.shape[0]
    capacity = max(2, 2 * mig_rows // devices)
    shape = jax.ShapeDtypeStruct
    rim_shape = shape((PLANES * RIM + 8, P_SIZE), f32)
    tab_shape = pltpu.VMEM(((cells + 2 * RIM) * 8, P_SIZE), f32)
    near_shape = pltpu.VMEM(((slots * NBR + 1) * 8, P_SIZE), f32)
    name_shape = pltpu.SMEM((8, P_SIZE), f32)
    fields = (positions, masses, smoothing, entropy, density)
    rows = (mig_source.reshape(1, mig_rows), mig_dest.reshape(1, mig_rows))
    lists = (active_cells, neighbours)

    raw = [in_hbm(v) for v in fields]
    send_b, send_a, active, near_ids = pl.pallas_call(
        pack_kernel,
        out_shape=(rim_shape, rim_shape) + tuple(pltpu.SMEM(v.shape, v.dtype) for v in lists),
        in_specs=[HBM] * 7 + [SMEM],
        out_specs=(VMEM,) * 2 + (SMEM,) * 2,
        scratch_shapes=[
            pltpu.VMEM((2, 3, RIM, P_SIZE), f32),
            pltpu.SemaphoreType.DMA((16,)),
        ],
        compiler_params=PARAMS,
        name="pack",
    )(*raw, *[in_hbm(v) for v in lists], active_count)

    pairs_a = [(i ^ 1, i) for i in range(devices) if i ^ 1 < devices]
    pairs_b = []
    for i in range(1, devices - 1, 2):
        pairs_b += [(i, i + 1), (i + 1, i)]
    got_b = lax.ppermute(send_b, AXES, pairs_b)
    got_a = lax.ppermute(send_a, AXES, pairs_a)

    ent, rho, dest, table, base, code, place, pick, near, left, total, offsets, *found = pl.pallas_call(
        functools.partial(migrant_kernel, capacity),
        out_shape=(
            pltpu.VMEM((cells, P_SIZE), f32),
            pltpu.VMEM((cells, P_SIZE), f32),
            pltpu.VMEM((1, mig_rows), jnp.int32),
            tab_shape,
            pltpu.VMEM((devices, P_SIZE), f32),
            pltpu.VMEM((mig_rows, P_SIZE), f32),
            pltpu.VMEM((mig_rows, P_SIZE), f32),
            pltpu.VMEM((P_SIZE, STATE * devices * capacity), bf16),
            near_shape,
            pltpu.VMEM((slots * P_SIZE, 48), bf16),
            pltpu.VMEM((slots * P_SIZE, P_SIZE), f32),
            pltpu.VMEM((NBR * 8, P_SIZE), f32),
            pltpu.SMEM((slots * NBR,), jnp.int32),
            pltpu.SMEM((slots * NBR,), jnp.int32),
            pltpu.SMEM((slots * NBR + 2,), jnp.int32),
            pltpu.SMEM((slots * NBR + 1,), jnp.int32),
        ),
        in_specs=[HBM] * 7 + [SMEM] * 3,
        out_specs=(VMEM,) * 12 + (SMEM,) * 4,
        scratch_shapes=[
            pltpu.VMEM((3, cells, P_SIZE), f32),
            pltpu.VMEM((cells, P_SIZE), f32),
            pltpu.VMEM((cells, P_SIZE), f32),
            pltpu.VMEM((1, mig_rows), jnp.int32),
            pltpu.SemaphoreType.DMA((7,)),
        ],
        compiler_params=PARAMS,
        name="migrants",
    )(*raw, *[in_hbm(v) for v in rows], active, active_count, near_ids)

    made, outgoing, table, near, _, names_a, names_b = pl.pallas_call(
        density_kernel,
        out_shape=(
            pltpu.VMEM((cells, P_SIZE), f32),
            shape((devices * 8, P_SIZE), f32),
            tab_shape,
            near_shape,
            pltpu.VMEM((slots * P_SIZE, P_SIZE), f32),
            name_shape,
            name_shape,
        ),
        in_specs=[VMEM] * 13 + [SMEM] * 6,
        out_specs=(VMEM,) * 5 + (SMEM,) * 2,
        input_output_aliases={0: 0, 4: 2, 5: 3, 11: 4},
        scratch_shapes=[
            pltpu.VMEM((8, P_SIZE), f32),
            pltpu.VMEM((8, P_SIZE), f32),
            pltpu.SemaphoreType.DMA((2,)),
        ],
        compiler_params=PARAMS,
        name="density",
    )(
        rho,
        ent,
        got_a,
        got_b,
        table,
        near,
        base,
        code,
        place,
        dest,
        left,
        total,
        offsets,
        active,
        active_count,
        *found,
    )

    incoming = lax.all_to_all(outgoing, AXES, split_axis=0, concat_axis=0, tiled=True)

    todo_len = pl.cdiv(slots * NBR + 2, P_SIZE) * P_SIZE
    partial, todo, new_density, left = pl.pallas_call(
        force_kernel,
        out_shape=(
            shape((3, slots, P_SIZE), f32),
            pltpu.SMEM((todo_len,), jnp.int32),
            shape((cells, P_SIZE), f32),
            pltpu.VMEM((slots * P_SIZE, 48), bf16),
        ),
        in_specs=[VMEM] * 3 + [SMEM] * 5,
        out_specs=(VMEM, SMEM, HBM, VMEM),
        scratch_shapes=[
            pltpu.SemaphoreType.DMA((1,)),
        ],
        compiler_params=PARAMS,
        name="force",
    )(table, near, made, names_a, names_b, active, active_count, found[0])

    acceleration, arrivals = pl.pallas_call(
        functools.partial(finish_kernel, capacity),
        out_shape=(
            shape((3, slots, P_SIZE), f32),
            shape((STATE, devices * capacity), f32),
        ),
        in_specs=[VMEM] * 6 + [SMEM] * 2,
        out_specs=(VMEM, VMEM),
        scratch_shapes=[pltpu.VMEM((slots * P_SIZE, 24), f32)],
        compiler_params=PARAMS,
        name="finish",
    )(table, near, partial, incoming, pick, left, todo, active)
    return (new_density, acceleration, arrivals)


def solution(mesh):
    placed = (
        P(None, AXES, None),
        P(AXES, None),
        P(AXES, None),
        P(AXES, None),
        P(AXES, None),
        P(AXES),
        P(AXES),
        P(AXES, None),
        P(AXES),
        P(AXES, None),
    )
    return jax.shard_map(
        local,
        mesh=mesh,
        in_specs=placed,
        out_specs=(P(AXES, None), P(None, AXES, None), P(None, AXES)),
        check_vma=False,
    )
```

```python
import functools
import math

import jax
import jax.numpy as jnp
from jax import lax
from jax.experimental import pallas as pl
from jax.experimental.pallas import tpu as pltpu
from jax.sharding import PartitionSpec as P

P_SIZE = 128
NBR = 27
RIM = 64
STATE = 7
PLANES = 6
SUM_GROUP = 8
EARLY_FIRST = 6
EARLY = 13
JOBS = 10
ITEMS = 4
TINY = 1e-9
AXES = ("gx", "gy")

kernel_norm = 8.0 / math.pi
log_six_norm = math.log(6.0 * kernel_norm)
f32 = jnp.float32
bf16 = jnp.bfloat16
VMEM = pl.BlockSpec(memory_space=pltpu.VMEM)
SMEM = pl.BlockSpec(memory_space=pltpu.SMEM)
HBM = pl.BlockSpec(memory_space=pltpu.HBM)
PARAMS = pltpu.CompilerParams(vmem_limit_bytes=16 << 20)


def in_hbm(value):
    return pltpu.with_memory_space_constraint(value, pltpu.HBM)


def own_index():
    return lax.axis_index("gx") * lax.axis_size("gy") + lax.axis_index("gy")


def beta_of(inverse_len, entropy, density):
    power = 0.5 * (log_six_norm + jnp.log(entropy)) - jnp.log(density) * (1.0 / 6.0)
    return inverse_len * inverse_len * jnp.exp(power)


def row_sums(block):
    return jnp.sum(block.T, axis=0, keepdims=True)


def offset_tile(entry):
    row = lax.broadcasted_iota(jnp.int32, (8, P_SIZE), 0)
    shift = (entry // 9 - 1, entry // 3 % 3 - 1, entry % 3 - 1)
    tile = jnp.zeros((8, P_SIZE), f32)
    for axis in range(3):
        if shift[axis]:
            tile = jnp.where(row == axis, float(shift[axis]), tile)
    return tile


def split(value):
    high = value.astype(bf16).astype(f32)
    rest = value - high
    middle = rest.astype(bf16).astype(f32)
    return high, middle, rest - middle


def start_copies(pairs, sems):
    copies = [pltpu.make_async_copy(src, dst, sems.at[i]) for i, (src, dst) in enumerate(pairs)]
    for copy in copies:
        copy.start()
    return copies


def put(tab_ref, cell, count, row, plane):
    tab_ref[pl.ds(cell * 8 + row, count, stride=8), :] = plane


def tile_of(tab_ref, cell):
    return tab_ref[pl.ds(pl.multiple_of(cell * 8, 8), 8), :]


def put_table(tab_ref, cell, count, x, y, z, mass, inverse_len, beta):
    cube_root = jnp.exp(jnp.log(mass) * (1.0 / 3.0))
    planes = (x - 0.5, y - 0.5, z - 0.5, None, cube_root, mass, inverse_len, beta)
    for row, plane in enumerate(planes):
        if plane is not None:
            put(tab_ref, cell, count, row, plane)


def pack_kernel(
    pos_hbm,
    mass_hbm,
    len_hbm,
    ent_hbm,
    rho_hbm,
    act_hbm,
    nbr_hbm,
    b_ref,
    a_ref,
    act_ref,
    nbr_ref,
    rim_ref,
    sems,
):
    cells = mass_hbm.shape[0]
    me = own_index()
    odd = me % 2
    start_a = pl.multiple_of((1 - odd) * (cells - RIM), RIM)
    start_b = pl.multiple_of(odd * (cells - RIM), RIM)
    sides = ((b_ref, start_b), (a_ref, start_a))
    pairs = [(act_hbm, act_ref)]
    for side, (out_ref, start) in enumerate(sides):
        rows = pl.ds(start, RIM)
        for index, ref in enumerate((len_hbm, ent_hbm, rho_hbm)):
            pairs.append((ref.at[rows, :], rim_ref.at[side, index]))
    first = len(pairs)
    for out_ref, start in sides:
        rows = pl.ds(start, RIM)
        for axis in range(3):
            pairs.append((pos_hbm.at[axis, rows, :], out_ref.at[pl.ds(axis * RIM, RIM), :]))
        pairs.append((mass_hbm.at[rows, :], out_ref.at[pl.ds(3 * RIM, RIM), :]))
    pairs.append((nbr_hbm, nbr_ref))
    copies = start_copies(pairs, sems)
    for copy in copies[:first]:
        copy.wait()
    lane = lax.broadcasted_iota(jnp.int32, (8, P_SIZE), 1)
    names = jnp.full((8, P_SIZE), -1.0, f32)
    slots = act_ref.shape[0]
    for slot in range(slots):
        mine = act_ref[slot] - me * cells
        names = jnp.where(lane == slot, mine.astype(f32), names)
    cell = lax.broadcasted_iota(jnp.int32, (RIM, P_SIZE), 0)
    for side, (out_ref, start) in enumerate(sides):
        inverse_len = 1.0 / rim_ref[side, 0]
        beta = beta_of(inverse_len, rim_ref[side, 1], rim_ref[side, 2])
        for slot in range(slots):
            beta = jnp.where(cell == act_ref[slot] - me * cells - start, 0.0, beta)
        out_ref[pl.ds(4 * RIM, RIM), :] = inverse_len
        out_ref[pl.ds(5 * RIM, RIM), :] = beta
        out_ref[pl.ds(PLANES * RIM, 8), :] = names
    for copy in copies[first:]:
        copy.wait()


def squared_length(tile):
    square = tile * tile
    return square[0:1, :] + square[1:2, :] + square[2:3, :]


def row_ids():
    return lax.broadcasted_iota(jnp.int32, (8, P_SIZE), 0)


def own_features(tile, scale):
    row = row_ids()
    lead = jnp.where(row < 3, -2.0 * tile, 1.0)
    lead = jnp.where(row == 4, squared_length(tile), lead)
    lead = jnp.where(row < 5, lead * scale, 0.0)
    high, middle, low = split(lead)
    return jnp.concatenate([high, high, middle, middle, high, low], axis=0).T.astype(bf16)


def other_features(tile):
    high, middle, low = split(tile)
    return jnp.concatenate([high, middle, high, middle, low, high], axis=0).astype(bf16)


def groups(size):
    return [range(first, min(first + size, NBR)) for first in range(0, NBR, size)]


def early(slot):
    return EARLY if slot else EARLY_FIRST


def stencil_tile(tab_ref, off_ref, cell, offset):
    tile = tile_of(tab_ref, cell) + tile_of(off_ref, offset)
    return jnp.where(row_ids() == 3, squared_length(tile), tile)


def density_terms(left, tiles, weights):
    row = row_ids()
    parts, roots, kept = [], [], []
    for tile, weight in zip(tiles, weights):
        root = tile[4:5, :] if weight is None else tile[4:5, :] * weight
        one = jnp.where(row == 4, 1.0, tile)
        parts.append(other_features(one * (root * root)))
        roots.append(root)
        kept.append(one)
    squares = jnp.dot(left, jnp.concatenate(parts, axis=1), preferred_element_type=f32)
    outer_sum = inner_sum = None
    for place, root in enumerate(roots):
        square = squares[:, place * P_SIZE : (place + 1) * P_SIZE]
        square = jnp.maximum(square, kept[place][6:7, :] * TINY)
        ratio = square * lax.rsqrt(square)
        outer = jnp.maximum(root - ratio, 0.0)
        inner = jnp.maximum(0.5 * root - ratio, 0.0)
        outer, inner = outer * outer * outer, inner * inner * inner
        outer_sum = outer if outer_sum is None else outer_sum + outer
        inner_sum = inner if inner_sum is None else inner_sum + inner
    return outer_sum, inner_sum, kept


def place_of(slot, position):
    return slot * NBR + position


def migrant_kernel(
    capacity,
    pos_hbm,
    mass_hbm,
    len_hbm,
    ent_hbm,
    rho_hbm,
    source_hbm,
    dest_hbm,
    act_ref,
    cnt_ref,
    nbr_ref,
    ent_ref,
    rho_ref,
    dest_ref,
    tab_ref,
    base_ref,
    code_ref,
    place_ref,
    pick_ref,
    near_ref,
    left_ref,
    total_ref,
    off_ref,
    cell_ref,
    offset_ref,
    job_ref,
    span_ref,
    pos_ref,
    mass_ref,
    len_ref,
    source_ref,
    sems,
):
    cells = mass_hbm.shape[0]
    me = own_index()
    targets = base_ref.shape[0]
    slots = act_ref.shape[0]
    base = me * cells - RIM
    copies = start_copies(
        (
            (len_hbm, len_ref),
            (ent_hbm, ent_ref),
            (rho_hbm, rho_ref),
            (pos_hbm, pos_ref),
            (mass_hbm, mass_ref),
            (source_hbm, source_ref),
            (dest_hbm, dest_ref),
        ),
        sems,
    )
    for entry in range(NBR):
        off_ref[pl.ds(entry * 8, 8), :] = offset_tile(entry)
    owned = []
    for slot in range(slots):
        mine = jnp.int32(0)
        for entry in range(NBR):
            cell = nbr_ref[slot, entry] - base
            near_by = jnp.logical_and(cell >= RIM, cell < RIM + cells)
            at = jnp.where(near_by, mine, NBR - 1 - entry + mine)
            cell_ref[place_of(slot, at)] = cell
            offset_ref[place_of(slot, at)] = entry
            mine = mine + jnp.where(near_by, 1, 0)
        owned.append(mine)
    at = jnp.int32(0)
    for slot in range(slots):
        for position in range(early(slot)):
            job_ref[at + 1] = place_of(slot, position)
            span_ref[at] = slot * P_SIZE
            at = at + jnp.where(position >= owned[slot], 1, 0)
    job_ref[0] = at
    width = targets * capacity
    column = lax.broadcasted_iota(jnp.int32, (P_SIZE, width), 1)
    spot_of = lax.broadcasted_iota(jnp.int32, (P_SIZE, width), 0) - column % capacity
    for index in range(STATE):
        hit = jnp.where(spot_of == index * capacity, 1.0, 0.0)
        pick_ref[:, pl.ds(index * width, width)] = hit.astype(bf16)
    for copy in copies:
        copy.wait()
    inverse_len = 1.0 / len_ref[...]
    beta = beta_of(inverse_len, ent_ref[...], rho_ref[...])
    put_table(
        tab_ref, RIM, cells, pos_ref[0], pos_ref[1], pos_ref[2], mass_ref[...], inverse_len, beta
    )
    for slot in range(slots):
        home = act_ref[slot] - base
        own = tile_of(tab_ref, home)
        inverse_len = own[6:7, :]
        left = own_features(own, inverse_len * inverse_len)
        left_ref[pl.ds(slot * P_SIZE, P_SIZE), :] = left
        outer_sum = jnp.zeros((P_SIZE, P_SIZE), f32)
        inner_sum = jnp.zeros((P_SIZE, P_SIZE), f32)
        for first in range(0, early(slot), 2):
            tiles, weights = [], []
            positions = range(first, min(first + 2, early(slot)))
            for position in positions:
                valid = position < owned[slot]
                cell = jnp.where(valid, cell_ref[place_of(slot, position)], home)
                offset = jnp.where(valid, offset_ref[place_of(slot, position)], 0)
                tiles.append(stencil_tile(tab_ref, off_ref, cell, offset))
                weights.append(jnp.where(valid, 1.0, 0.0))
            outer, inner, kept = density_terms(left, tiles, weights)
            outer_sum, inner_sum = outer_sum + outer, inner_sum + inner
            for position, tile in zip(positions, kept):
                near_ref[pl.ds(place_of(slot, position) * 8, 8), :] = tile
        total_ref[pl.ds(slot * P_SIZE, P_SIZE), :] = outer_sum - 4.0 * inner_sum
    source = source_ref[...]
    cell_row = source // P_SIZE
    code_row = jnp.zeros_like(source)
    for slot in range(act_ref.shape[0]):
        mine = act_ref[slot] - me * cells
        named = jnp.logical_and(cell_row == mine, slot < cnt_ref[0])
        code_row = jnp.where(named, slot + 1, code_row)
    row_id = lax.broadcasted_iota(jnp.int32, (8, P_SIZE), 0)
    stack = jnp.zeros((8, P_SIZE), f32)
    for index, part in enumerate((cell_row, source % P_SIZE, dest_ref[...], code_row)):
        stack = jnp.where(row_id == index, part.astype(f32), stack)
    columns = stack.T
    shape = (P_SIZE, P_SIZE)
    cell, lane_of, dest, code = [jnp.broadcast_to(columns[:, i : i + 1], shape) for i in range(4)]
    lane = lax.broadcasted_iota(jnp.int32, shape, 1)
    row = lax.broadcasted_iota(jnp.int32, shape, 0)
    lane_f = lane.astype(f32)
    hit = lane_f == lane_of
    same = jnp.logical_and(dest == dest_ref[...].astype(f32), lane < row)
    rank = jnp.sum(jnp.where(same, 1.0, 0.0), axis=1, keepdims=True)
    wide = lax.broadcasted_iota(jnp.int32, (P_SIZE, cells), 1).astype(f32)
    pick = jnp.where(wide == columns[:, 0:1], 1.0, 0.0).astype(bf16)
    spot = lane_f - rank
    sent = jnp.zeros(shape, f32)
    planes = [pos_ref[0], pos_ref[1], pos_ref[2], mass_ref[...], len_ref[...], ent_ref[...], rho_ref[...]]
    for index, plane in enumerate(planes):
        found = sum(
            jnp.dot(pick, piece.astype(bf16), preferred_element_type=f32) for piece in split(plane)
        )
        keep = jnp.logical_and(hit, code == 0.0) if index == STATE - 1 else hit
        value = jnp.sum(jnp.where(keep, found, 0.0), axis=1, keepdims=True)
        sent = jnp.where(spot == float(index * capacity), value, sent)
    aim = lax.broadcasted_iota(jnp.int32, (targets, P_SIZE), 0) == dest_ref[...]
    aim = jnp.where(aim, 1.0, 0.0)
    base_ref[...] = jnp.dot(aim, sent, precision=lax.Precision.HIGHEST, preferred_element_type=f32)
    code_ref[...] = jnp.where(hit, code, 0.0)
    place_ref[...] = jnp.where(spot == float((STATE - 1) * capacity), 1.0, 0.0)


def density_kernel(
    rho_in,
    ent_ref,
    a_ref,
    b_ref,
    tab_in,
    near_in,
    base_ref,
    code_ref,
    place_ref,
    dest_ref,
    left_ref,
    total_in,
    off_ref,
    act_ref,
    cnt_ref,
    cell_ref,
    offset_ref,
    job_ref,
    span_ref,
    new_ref,
    out_ref,
    tab_ref,
    near_ref,
    total_ref,
    names_a,
    names_b,
    made_ref,
    beta_ref,
    sems,
):
    cells = new_ref.shape[0]
    slots = act_ref.shape[0]
    me = own_index()
    odd = me % 2
    copies = start_copies(
        [
            (ref.at[pl.ds(PLANES * RIM, 8), :], names)
            for ref, names in ((a_ref, names_a), (b_ref, names_b))
        ],
        sems,
    )
    start_of_a = (1 - odd) * (cells + RIM)
    for in_ref, start in ((a_ref, start_of_a), (b_ref, cells + RIM - start_of_a)):
        put_table(tab_ref, start, RIM, *[in_ref[pl.ds(i * RIM, RIM), :] for i in range(PLANES)])

    jobs = job_ref[0]

    def late_entry(job, place, weight):
        tile = stencil_tile(tab_ref, off_ref, cell_ref[place], offset_ref[place])
        span = pl.ds(pl.multiple_of(span_ref[job], P_SIZE), P_SIZE)
        outer, inner, kept = density_terms(left_ref[span, :], [tile], [weight])
        total_ref[span, :] = total_ref[span, :] + (outer - 4.0 * inner)
        return kept[0]

    @pl.loop(JOBS, jobs)
    def _(job):
        place = job_ref[job + 1]
        near_ref[pl.ds(pl.multiple_of(place * 8, 8), 8), :] = late_entry(job, place, None)

    for turn in range(JOBS):
        valid = turn < jobs
        job = jnp.where(valid, turn, 0)
        place = jnp.where(valid, job_ref[turn + 1], 0)
        kept = late_entry(job, place, jnp.where(valid, 1.0, 0.0))
        target = jnp.where(valid, place, slots * NBR)
        near_ref[pl.ds(pl.multiple_of(target * 8, 8), 8), :] = kept

    for slot in range(slots):
        mine = act_ref[slot] - me * cells
        inverse_len = tile_of(tab_ref, RIM + mine)[6:7, :]
        span = pl.ds(slot * P_SIZE, P_SIZE)
        left = left_ref[span, :]
        outer_sum = jnp.zeros((P_SIZE, P_SIZE), f32)
        inner_sum = jnp.zeros((P_SIZE, P_SIZE), f32)
        for first in range(early(slot), NBR, 2):
            positions = range(first, min(first + 2, NBR))
            tiles = []
            for position in positions:
                place = place_of(slot, position)
                tiles.append(stencil_tile(tab_ref, off_ref, cell_ref[place], offset_ref[place]))
            outer, inner, kept = density_terms(left, tiles, [None] * len(tiles))
            outer_sum, inner_sum = outer_sum + outer, inner_sum + inner
            for position, tile in zip(positions, kept):
                near_ref[pl.ds(place_of(slot, position) * 8, 8), :] = tile
        total = total_ref[span, :] + (outer_sum - 4.0 * inner_sum)
        made = row_sums(total) * (2.0 * kernel_norm) * inverse_len * inverse_len * inverse_len
        made = jnp.where(slot < cnt_ref[0], made, new_ref[pl.ds(mine, 1), :])
        beta = beta_of(inverse_len, ent_ref[pl.ds(mine, 1), :], made)
        made_ref[slot : slot + 1, :] = made
        beta_ref[slot : slot + 1, :] = beta

    for slot in range(slots):
        mine = act_ref[slot] - me * cells
        new_ref[pl.ds(mine, 1), :] = made_ref[slot : slot + 1, :]
        tab_ref[pl.ds((RIM + mine) * 8 + 7, 1), :] = beta_ref[slot : slot + 1, :]
    code = code_ref[...]
    chosen = jnp.zeros_like(code)
    for slot in range(slots):
        chosen = jnp.where(code == float(slot + 1), made_ref[slot : slot + 1, :], chosen)
    late = place_ref[...] * jnp.sum(chosen, axis=1, keepdims=True)
    targets = base_ref.shape[0]
    aim = lax.broadcasted_iota(jnp.int32, (targets, P_SIZE), 0) == dest_ref[...]
    aim = jnp.where(aim, 1.0, 0.0)
    for line in range(1, 8):
        fill = jnp.zeros((1, P_SIZE), f32) if line > slots else beta_ref[line - 1 : line, :]
        put(out_ref, 0, targets, line, jnp.broadcast_to(fill, (targets, P_SIZE)))
    sent = base_ref[...] + jnp.dot(
        aim, late, precision=lax.Precision.HIGHEST, preferred_element_type=f32
    )
    put(out_ref, 0, targets, 0, sent)
    for copy in copies:
        copy.wait()


def spline(base, slope, distance):
    step = distance * slope
    outer = jnp.maximum(base - step, 0.0)
    least = jnp.minimum(step, outer)
    return least * (outer + (outer - least))


def pull_sums(pulls, nears):
    row = row_ids()
    highs = [pull.astype(bf16) for pull in pulls]
    lows = [(pull - high.astype(f32)).astype(bf16) for pull, high in zip(pulls, highs)]
    sides = []
    for near in nears:
        weighed = jnp.where(row < 3, near, 1.0) * near[5:6, :]
        sides.append(jnp.concatenate(split(weighed), axis=0).astype(bf16))
    return lax.dot_general(
        jnp.concatenate(highs + lows, axis=1),
        jnp.concatenate(sides + sides, axis=1),
        (((1,), (1,)), ((), ())),
        preferred_element_type=f32,
    )


def force_kernel(
    tab_ref,
    near_ref,
    new_ref,
    names_a,
    names_b,
    act_ref,
    cnt_ref,
    cell_ref,
    acc_out,
    list_ref,
    new_out,
    left_ref,
    sems,
):
    cells = tab_ref.shape[0] // 8 - 2 * RIM
    me = own_index()
    odd = me % 2
    slots = act_ref.shape[0]
    copies = start_copies([(new_ref, new_out)], sems)
    fa = [names_a[0, s].astype(jnp.int32) for s in range(slots)]
    fb = [names_b[0, s].astype(jnp.int32) for s in range(slots)]
    left = [jnp.where(odd == 1, fa[s], fb[s]) for s in range(slots)]
    right = [jnp.where(odd == 1, fb[s], fa[s]) for s in range(slots)]
    left = [jnp.where(v >= cells - RIM, v - (cells - RIM), -1) for v in left]
    right = [jnp.where(jnp.logical_and(v >= 0, v < RIM), v + cells + RIM, -1) for v in right]
    at = jnp.int32(0)
    for slot in range(slots):
        live = slot < cnt_ref[0]
        mine = act_ref[slot] - me * cells
        own = tile_of(tab_ref, RIM + mine)
        columns = own.T
        own_base = jnp.broadcast_to(columns[:, 7:8], (P_SIZE, P_SIZE))
        own_slope = own_base * jnp.broadcast_to(columns[:, 6:7], (P_SIZE, P_SIZE))
        left_side = own_features(own, 1.0)
        left_ref[pl.ds(slot * P_SIZE, P_SIZE), :] = left_side
        sums = jnp.zeros((P_SIZE, 24), f32)
        for block in groups(SUM_GROUP):
            pulls, nears = [], []
            for first in range(block.start, block.stop, 2):
                group = range(first, min(first + 2, block.stop))
                tiles = [near_ref[pl.ds((slot * NBR + entry) * 8, 8), :] for entry in group]
                other = jnp.concatenate([other_features(tile) for tile in tiles], axis=1)
                squares = jnp.dot(left_side, other, preferred_element_type=f32)
                for place, entry in enumerate(group):
                    near = tiles[place]
                    cell = cell_ref[place_of(slot, entry)]
                    found = jnp.int32(-1)
                    for s in range(slots):
                        found = jnp.where(cell == left[s], s, found)
                        found = jnp.where(cell == right[s], slots + s, found)
                    list_ref[at + 1] = (slot * NBR + entry) * (2 * slots) + found
                    at = at + jnp.where(jnp.logical_and(found >= 0, live), 1, 0)

                    beta = tab_ref[pl.ds(cell * 8 + 7, 1), :]
                    slope = beta * near[6:7, :]
                    square = jnp.maximum(squares[:, place * P_SIZE : (place + 1) * P_SIZE], near[6:7, :] * TINY)
                    inverse = lax.rsqrt(square)
                    distance = square * inverse
                    pull = spline(own_base, own_slope, distance) + spline(beta, slope, distance)
                    pull = pull * inverse
                    pulls.append(pull)
                    nears.append(near)
            sums = sums + pull_sums(pulls, nears)
        flat = sums.T
        flat = flat[0:8, :] + flat[8:16, :] + flat[16:24, :]
        made = jnp.where(live, own * flat[3:4, :] - flat, 0.0)
        for axis in range(3):
            acc_out[axis, slot : slot + 1, :] = made[axis : axis + 1, :]
    list_ref[0] = at
    for copy in copies:
        copy.wait()


def finish_kernel(
    capacity,
    tab_ref,
    near_ref,
    part_ref,
    got_ref,
    pick_ref,
    left_ref,
    list_ref,
    act_ref,
    acc_out,
    arrive_ref,
    late_ref,
):
    cells = tab_ref.shape[0] // 8 - 2 * RIM
    me = own_index()
    slots = act_ref.shape[0]
    targets = got_ref.shape[0] // 8
    acc_out[...] = part_ref[...]
    rows = got_ref[pl.ds(0, targets, stride=8), :]
    width = targets * capacity
    sender = lax.broadcasted_iota(jnp.int32, (targets, width), 1) // capacity
    mask = sender == lax.broadcasted_iota(jnp.int32, (targets, width), 0)
    pieces = jnp.concatenate(split(rows), axis=0).astype(bf16)
    spread = jnp.dot(pieces, pick_ref[...], preferred_element_type=f32)
    spread = spread[0:targets] + spread[targets : 2 * targets] + spread[2 * targets :]
    for index in range(STATE):
        part = spread[:, index * width : (index + 1) * width]
        arrive_ref[index : index + 1, :] = jnp.sum(jnp.where(mask, part, 0.0), axis=0, keepdims=True)

    count = list_ref[0]

    @pl.when(count > 0)
    def _():
        late_ref[...] = jnp.zeros_like(late_ref)

        @pl.loop(0, (count + ITEMS - 1) // ITEMS)
        def _(block):
            made = []
            for step in range(ITEMS):
                item = block * ITEMS + step
                word = list_ref[jnp.minimum(item, count - 1) + 1]
                found = word % (2 * slots)
                place = word // (2 * slots)
                slot = place // NBR
                span = pl.ds(pl.multiple_of(slot * P_SIZE, P_SIZE), P_SIZE)
                other = jnp.where(found < slots, me - 1, me + 1)
                near = near_ref[pl.ds(pl.multiple_of(place * 8, 8), 8), :]
                beta = got_ref[pl.ds(other * 8 + 1 + found % slots, 1), :]
                beta = beta * jnp.where(item < count, 1.0, 0.0)
                square = jnp.dot(
                    left_ref[span, :], other_features(near), preferred_element_type=f32
                )
                square = jnp.maximum(square, near[6:7, :] * TINY)
                inverse = lax.rsqrt(square)
                pull = spline(beta, beta * near[6:7, :], square * inverse) * inverse
                made.append((span, pull_sums([pull], [near])))
            for span, sums in made:
                late_ref[span, :] = late_ref[span, :] + sums

        for slot in range(slots):
            own = tile_of(tab_ref, RIM + act_ref[slot] - me * cells)
            flat = late_ref[pl.ds(slot * P_SIZE, P_SIZE), :].T
            flat = flat[0:8, :] + flat[8:16, :] + flat[16:24, :]
            made = own * flat[3:4, :] - flat
            for axis in range(3):
                acc_out[axis, slot : slot + 1, :] += made[axis : axis + 1, :]


def local(
    positions,
    masses,
    smoothing,
    entropy,
    density,
    active_cells,
    active_count,
    neighbours,
    mig_source,
    mig_dest,
):
    cells = masses.shape[0]
    slots = active_cells.shape[0]
    devices = lax.axis_size(AXES)
    mig_rows = mig_source.shape[0]
    capacity = max(2, 2 * mig_rows // devices)
    shape = jax.ShapeDtypeStruct
    rim_shape = shape((PLANES * RIM + 8, P_SIZE), f32)
    tab_shape = pltpu.VMEM(((cells + 2 * RIM) * 8, P_SIZE), f32)
    near_shape = pltpu.VMEM(((slots * NBR + 1) * 8, P_SIZE), f32)
    name_shape = pltpu.SMEM((8, P_SIZE), f32)
    fields = (positions, masses, smoothing, entropy, density)
    rows = (mig_source.reshape(1, mig_rows), mig_dest.reshape(1, mig_rows))
    lists = (active_cells, neighbours)

    raw = [in_hbm(v) for v in fields]
    send_b, send_a, active, near_ids = pl.pallas_call(
        pack_kernel,
        out_shape=(rim_shape, rim_shape) + tuple(pltpu.SMEM(v.shape, v.dtype) for v in lists),
        in_specs=[HBM] * 7,
        out_specs=(VMEM,) * 2 + (SMEM,) * 2,
        scratch_shapes=[
            pltpu.VMEM((2, 3, RIM, P_SIZE), f32),
            pltpu.SemaphoreType.DMA((16,)),
        ],
        compiler_params=PARAMS,
        name="pack",
    )(*raw, *[in_hbm(v) for v in lists])
    send_b, active_count = lax.optimization_barrier((send_b, active_count))

    pairs_a = [(i ^ 1, i) for i in range(devices) if i ^ 1 < devices]
    pairs_b = []
    for i in range(1, devices - 1, 2):
        pairs_b += [(i, i + 1), (i + 1, i)]
    got_b = lax.ppermute(send_b, AXES, pairs_b)
    got_a = lax.ppermute(send_a, AXES, pairs_a)

    ent, rho, dest, table, base, code, place, pick, near, left, total, offsets, *found = pl.pallas_call(
        functools.partial(migrant_kernel, capacity),
        out_shape=(
            pltpu.VMEM((cells, P_SIZE), f32),
            pltpu.VMEM((cells, P_SIZE), f32),
            pltpu.VMEM((1, mig_rows), jnp.int32),
            tab_shape,
            pltpu.VMEM((devices, P_SIZE), f32),
            pltpu.VMEM((mig_rows, P_SIZE), f32),
            pltpu.VMEM((mig_rows, P_SIZE), f32),
            pltpu.VMEM((P_SIZE, STATE * devices * capacity), bf16),
            near_shape,
            pltpu.VMEM((slots * P_SIZE, 48), bf16),
            pltpu.VMEM((slots * P_SIZE, P_SIZE), f32),
            pltpu.VMEM((NBR * 8, P_SIZE), f32),
            pltpu.SMEM((slots * NBR,), jnp.int32),
            pltpu.SMEM((slots * NBR,), jnp.int32),
            pltpu.SMEM((slots * NBR + 2,), jnp.int32),
            pltpu.SMEM((slots * NBR + 1,), jnp.int32),
        ),
        in_specs=[HBM] * 7 + [SMEM] * 3,
        out_specs=(VMEM,) * 12 + (SMEM,) * 4,
        scratch_shapes=[
            pltpu.VMEM((3, cells, P_SIZE), f32),
            pltpu.VMEM((cells, P_SIZE), f32),
            pltpu.VMEM((cells, P_SIZE), f32),
            pltpu.VMEM((1, mig_rows), jnp.int32),
            pltpu.SemaphoreType.DMA((7,)),
        ],
        compiler_params=PARAMS,
        name="migrants",
    )(*raw, *[in_hbm(v) for v in rows], active, active_count, near_ids)

    made, outgoing, table, near, _, names_a, names_b = pl.pallas_call(
        density_kernel,
        out_shape=(
            pltpu.VMEM((cells, P_SIZE), f32),
            shape((devices * 8, P_SIZE), f32),
            tab_shape,
            near_shape,
            pltpu.VMEM((slots * P_SIZE, P_SIZE), f32),
            name_shape,
            name_shape,
        ),
        in_specs=[VMEM] * 13 + [SMEM] * 6,
        out_specs=(VMEM,) * 5 + (SMEM,) * 2,
        input_output_aliases={0: 0, 4: 2, 5: 3, 11: 4},
        scratch_shapes=[
            pltpu.VMEM((8, P_SIZE), f32),
            pltpu.VMEM((8, P_SIZE), f32),
            pltpu.SemaphoreType.DMA((2,)),
        ],
        compiler_params=PARAMS,
        name="density",
    )(
        rho,
        ent,
        got_a,
        got_b,
        table,
        near,
        base,
        code,
        place,
        dest,
        left,
        total,
        offsets,
        active,
        active_count,
        *found,
    )

    incoming = lax.all_to_all(outgoing, AXES, split_axis=0, concat_axis=0, tiled=True)

    todo_len = pl.cdiv(slots * NBR + 2, P_SIZE) * P_SIZE
    partial, todo, new_density, left = pl.pallas_call(
        force_kernel,
        out_shape=(
            shape((3, slots, P_SIZE), f32),
            pltpu.SMEM((todo_len,), jnp.int32),
            shape((cells, P_SIZE), f32),
            pltpu.VMEM((slots * P_SIZE, 48), bf16),
        ),
        in_specs=[VMEM] * 3 + [SMEM] * 5,
        out_specs=(VMEM, SMEM, HBM, VMEM),
        scratch_shapes=[
            pltpu.SemaphoreType.DMA((1,)),
        ],
        compiler_params=PARAMS,
        name="force",
    )(table, near, made, names_a, names_b, active, active_count, found[0])

    acceleration, arrivals = pl.pallas_call(
        functools.partial(finish_kernel, capacity),
        out_shape=(
            shape((3, slots, P_SIZE), f32),
            shape((STATE, devices * capacity), f32),
        ),
        in_specs=[VMEM] * 6 + [SMEM] * 2,
        out_specs=(VMEM, VMEM),
        scratch_shapes=[pltpu.VMEM((slots * P_SIZE, 24), f32)],
        compiler_params=PARAMS,
        name="finish",
    )(table, near, partial, incoming, pick, left, todo, active)
    return (new_density, acceleration, arrivals)


def solution(mesh):
    placed = (
        P(None, AXES, None),
        P(AXES, None),
        P(AXES, None),
        P(AXES, None),
        P(AXES, None),
        P(AXES),
        P(AXES),
        P(AXES, None),
        P(AXES),
        P(AXES, None),
    )
    return jax.shard_map(
        local,
        mesh=mesh,
        in_specs=placed,
        out_specs=(P(AXES, None), P(None, AXES, None), P(None, AXES)),
        check_vma=False,
    )
```

```python
import functools
import math

import jax
import jax.numpy as jnp
from jax import lax
from jax.experimental import pallas as pl
from jax.experimental.pallas import tpu as pltpu
from jax.sharding import PartitionSpec as P

P_SIZE = 128
NBR = 27
RIM = 64
STATE = 7
PLANES = 6
SUM_GROUP = 8
EARLY_FIRST = 6
EARLY = 13
JOBS = 10
ITEMS = 4
TINY = 1e-9
AXES = ("gx", "gy")

kernel_norm = 8.0 / math.pi
log_six_norm = math.log(6.0 * kernel_norm)
f32 = jnp.float32
bf16 = jnp.bfloat16
VMEM = pl.BlockSpec(memory_space=pltpu.VMEM)
SMEM = pl.BlockSpec(memory_space=pltpu.SMEM)
HBM = pl.BlockSpec(memory_space=pltpu.HBM)
PARAMS = pltpu.CompilerParams(vmem_limit_bytes=16 << 20)


def in_hbm(value):
    return pltpu.with_memory_space_constraint(value, pltpu.HBM)


def own_index():
    return lax.axis_index("gx") * lax.axis_size("gy") + lax.axis_index("gy")


def beta_of(inverse_len, entropy, density):
    power = 0.5 * (log_six_norm + jnp.log(entropy)) - jnp.log(density) * (1.0 / 6.0)
    return inverse_len * inverse_len * jnp.exp(power)


def row_sums(block):
    return jnp.sum(block.T, axis=0, keepdims=True)


def offset_tile(entry):
    row = lax.broadcasted_iota(jnp.int32, (8, P_SIZE), 0)
    shift = (entry // 9 - 1, entry // 3 % 3 - 1, entry % 3 - 1)
    tile = jnp.zeros((8, P_SIZE), f32)
    for axis in range(3):
        if shift[axis]:
            tile = jnp.where(row == axis, float(shift[axis]), tile)
    return tile


def split(value):
    high = value.astype(bf16).astype(f32)
    rest = value - high
    middle = rest.astype(bf16).astype(f32)
    return high, middle, rest - middle


def start_copies(pairs, sems):
    copies = [pltpu.make_async_copy(src, dst, sems.at[i]) for i, (src, dst) in enumerate(pairs)]
    for copy in copies:
        copy.start()
    return copies


def put(tab_ref, cell, count, row, plane):
    tab_ref[pl.ds(cell * 8 + row, count, stride=8), :] = plane


def tile_of(tab_ref, cell):
    return tab_ref[pl.ds(pl.multiple_of(cell * 8, 8), 8), :]


def put_table(tab_ref, cell, count, x, y, z, mass, inverse_len, beta):
    cube_root = jnp.exp(jnp.log(mass) * (1.0 / 3.0))
    planes = (x - 0.5, y - 0.5, z - 0.5, None, cube_root, mass, inverse_len, beta)
    for row, plane in enumerate(planes):
        if plane is not None:
            put(tab_ref, cell, count, row, plane)


def pack_kernel(
    pos_hbm,
    mass_hbm,
    len_hbm,
    ent_hbm,
    rho_hbm,
    act_hbm,
    nbr_hbm,
    b_ref,
    a_ref,
    act_ref,
    nbr_ref,
    rim_ref,
    sems,
):
    cells = mass_hbm.shape[0]
    me = own_index()
    odd = me % 2
    start_a = pl.multiple_of((1 - odd) * (cells - RIM), RIM)
    start_b = pl.multiple_of(odd * (cells - RIM), RIM)
    sides = ((b_ref, start_b), (a_ref, start_a))
    pairs = [(act_hbm, act_ref)]
    for side, (out_ref, start) in enumerate(sides):
        rows = pl.ds(start, RIM)
        for index, ref in enumerate((len_hbm, ent_hbm, rho_hbm)):
            pairs.append((ref.at[rows, :], rim_ref.at[side, index]))
    first = len(pairs)
    for out_ref, start in sides:
        rows = pl.ds(start, RIM)
        for axis in range(3):
            pairs.append((pos_hbm.at[axis, rows, :], out_ref.at[pl.ds(axis * RIM, RIM), :]))
        pairs.append((mass_hbm.at[rows, :], out_ref.at[pl.ds(3 * RIM, RIM), :]))
    pairs.append((nbr_hbm, nbr_ref))
    copies = start_copies(pairs, sems)
    for copy in copies[:first]:
        copy.wait()
    lane = lax.broadcasted_iota(jnp.int32, (8, P_SIZE), 1)
    names = jnp.full((8, P_SIZE), -1.0, f32)
    slots = act_ref.shape[0]
    for slot in range(slots):
        mine = act_ref[slot] - me * cells
        names = jnp.where(lane == slot, mine.astype(f32), names)
    cell = lax.broadcasted_iota(jnp.int32, (RIM, P_SIZE), 0)
    for side, (out_ref, start) in enumerate(sides):
        inverse_len = 1.0 / rim_ref[side, 0]
        beta = beta_of(inverse_len, rim_ref[side, 1], rim_ref[side, 2])
        for slot in range(slots):
            beta = jnp.where(cell == act_ref[slot] - me * cells - start, 0.0, beta)
        out_ref[pl.ds(4 * RIM, RIM), :] = inverse_len
        out_ref[pl.ds(5 * RIM, RIM), :] = beta
        out_ref[pl.ds(PLANES * RIM, 8), :] = names
    for copy in copies[first:]:
        copy.wait()


def squared_length(tile):
    square = tile * tile
    return square[0:1, :] + square[1:2, :] + square[2:3, :]


def row_ids():
    return lax.broadcasted_iota(jnp.int32, (8, P_SIZE), 0)


def own_features(tile, scale):
    row = row_ids()
    lead = jnp.where(row < 3, -2.0 * tile, 1.0)
    lead = jnp.where(row == 4, squared_length(tile), lead)
    lead = jnp.where(row < 5, lead * scale, 0.0)
    high, middle, low = split(lead)
    return jnp.concatenate([high, high, middle, middle, high, low], axis=0).T.astype(bf16)


def other_features(tile):
    high, middle, low = split(tile)
    return jnp.concatenate([high, middle, high, middle, low, high], axis=0).astype(bf16)


def groups(size):
    return [range(first, min(first + size, NBR)) for first in range(0, NBR, size)]


def early(slot):
    return EARLY if slot else EARLY_FIRST


def stencil_tile(tab_ref, off_ref, cell, offset):
    tile = tile_of(tab_ref, cell) + tile_of(off_ref, offset)
    return jnp.where(row_ids() == 3, squared_length(tile), tile)


def density_terms(left, tiles, weights):
    row = row_ids()
    parts, roots, kept = [], [], []
    for tile, weight in zip(tiles, weights):
        root = tile[4:5, :] if weight is None else tile[4:5, :] * weight
        one = jnp.where(row == 4, 1.0, tile)
        parts.append(other_features(one * (root * root)))
        roots.append(root)
        kept.append(one)
    squares = jnp.dot(left, jnp.concatenate(parts, axis=1), preferred_element_type=f32)
    outer_sum = inner_sum = None
    for place, root in enumerate(roots):
        square = squares[:, place * P_SIZE : (place + 1) * P_SIZE]
        square = jnp.maximum(square, kept[place][6:7, :] * TINY)
        ratio = square * lax.rsqrt(square)
        outer = jnp.maximum(root - ratio, 0.0)
        inner = jnp.maximum(0.5 * root - ratio, 0.0)
        outer, inner = outer * outer * outer, inner * inner * inner
        outer_sum = outer if outer_sum is None else outer_sum + outer
        inner_sum = inner if inner_sum is None else inner_sum + inner
    return outer_sum, inner_sum, kept


def place_of(slot, position):
    return slot * NBR + position


def migrant_kernel(
    capacity,
    pos_hbm,
    mass_hbm,
    len_hbm,
    ent_hbm,
    rho_hbm,
    source_hbm,
    dest_hbm,
    act_ref,
    cnt_ref,
    nbr_ref,
    ent_ref,
    rho_ref,
    dest_ref,
    tab_ref,
    base_ref,
    code_ref,
    place_ref,
    pick_ref,
    near_ref,
    left_ref,
    total_ref,
    off_ref,
    cell_ref,
    offset_ref,
    job_ref,
    span_ref,
    pos_ref,
    mass_ref,
    len_ref,
    source_ref,
    sems,
):
    cells = mass_hbm.shape[0]
    me = own_index()
    targets = base_ref.shape[0]
    slots = act_ref.shape[0]
    base = me * cells - RIM
    copies = start_copies(
        (
            (len_hbm, len_ref),
            (ent_hbm, ent_ref),
            (rho_hbm, rho_ref),
            (pos_hbm, pos_ref),
            (mass_hbm, mass_ref),
            (source_hbm, source_ref),
            (dest_hbm, dest_ref),
        ),
        sems,
    )
    for entry in range(NBR):
        off_ref[pl.ds(entry * 8, 8), :] = offset_tile(entry)
    owned = []
    for slot in range(slots):
        mine = jnp.int32(0)
        for entry in range(NBR):
            cell = nbr_ref[slot, entry] - base
            near_by = jnp.logical_and(cell >= RIM, cell < RIM + cells)
            at = jnp.where(near_by, mine, NBR - 1 - entry + mine)
            cell_ref[place_of(slot, at)] = cell
            offset_ref[place_of(slot, at)] = entry
            mine = mine + jnp.where(near_by, 1, 0)
        owned.append(mine)
    at = jnp.int32(0)
    for slot in range(slots):
        for position in range(early(slot)):
            job_ref[at + 1] = place_of(slot, position)
            span_ref[at] = slot * P_SIZE
            at = at + jnp.where(position >= owned[slot], 1, 0)
    job_ref[0] = at
    width = targets * capacity
    column = lax.broadcasted_iota(jnp.int32, (P_SIZE, width), 1)
    spot_of = lax.broadcasted_iota(jnp.int32, (P_SIZE, width), 0) - column % capacity
    for index in range(STATE):
        hit = jnp.where(spot_of == index * capacity, 1.0, 0.0)
        pick_ref[:, pl.ds(index * width, width)] = hit.astype(bf16)
    for copy in copies:
        copy.wait()
    inverse_len = 1.0 / len_ref[...]
    beta = beta_of(inverse_len, ent_ref[...], rho_ref[...])
    put_table(
        tab_ref, RIM, cells, pos_ref[0], pos_ref[1], pos_ref[2], mass_ref[...], inverse_len, beta
    )
    for slot in range(slots):
        home = act_ref[slot] - base
        own = tile_of(tab_ref, home)
        inverse_len = own[6:7, :]
        left = own_features(own, inverse_len * inverse_len)
        left_ref[pl.ds(slot * P_SIZE, P_SIZE), :] = left
        outer_sum = jnp.zeros((P_SIZE, P_SIZE), f32)
        inner_sum = jnp.zeros((P_SIZE, P_SIZE), f32)
        for first in range(0, early(slot), 2):
            tiles, weights = [], []
            positions = range(first, min(first + 2, early(slot)))
            for position in positions:
                valid = position < owned[slot]
                cell = jnp.where(valid, cell_ref[place_of(slot, position)], home)
                offset = jnp.where(valid, offset_ref[place_of(slot, position)], 0)
                tiles.append(stencil_tile(tab_ref, off_ref, cell, offset))
                weights.append(jnp.where(valid, 1.0, 0.0))
            outer, inner, kept = density_terms(left, tiles, weights)
            outer_sum, inner_sum = outer_sum + outer, inner_sum + inner
            for position, tile in zip(positions, kept):
                near_ref[pl.ds(place_of(slot, position) * 8, 8), :] = tile
        total_ref[pl.ds(slot * P_SIZE, P_SIZE), :] = outer_sum - 4.0 * inner_sum
    source = source_ref[...]
    cell_row = source // P_SIZE
    code_row = jnp.zeros_like(source)
    for slot in range(act_ref.shape[0]):
        mine = act_ref[slot] - me * cells
        named = jnp.logical_and(cell_row == mine, slot < cnt_ref[0])
        code_row = jnp.where(named, slot + 1, code_row)
    row_id = lax.broadcasted_iota(jnp.int32, (8, P_SIZE), 0)
    stack = jnp.zeros((8, P_SIZE), f32)
    for index, part in enumerate((cell_row, source % P_SIZE, dest_ref[...], code_row)):
        stack = jnp.where(row_id == index, part.astype(f32), stack)
    columns = stack.T
    shape = (P_SIZE, P_SIZE)
    cell, lane_of, dest, code = [jnp.broadcast_to(columns[:, i : i + 1], shape) for i in range(4)]
    lane = lax.broadcasted_iota(jnp.int32, shape, 1)
    row = lax.broadcasted_iota(jnp.int32, shape, 0)
    lane_f = lane.astype(f32)
    hit = lane_f == lane_of
    same = jnp.logical_and(dest == dest_ref[...].astype(f32), lane < row)
    rank = jnp.sum(jnp.where(same, 1.0, 0.0), axis=1, keepdims=True)
    wide = lax.broadcasted_iota(jnp.int32, (P_SIZE, cells), 1).astype(f32)
    pick = jnp.where(wide == columns[:, 0:1], 1.0, 0.0).astype(bf16)
    spot = lane_f - rank
    sent = jnp.zeros(shape, f32)
    planes = [pos_ref[0], pos_ref[1], pos_ref[2], mass_ref[...], len_ref[...], ent_ref[...], rho_ref[...]]
    for index, plane in enumerate(planes):
        found = sum(
            jnp.dot(pick, piece.astype(bf16), preferred_element_type=f32) for piece in split(plane)
        )
        keep = jnp.logical_and(hit, code == 0.0) if index == STATE - 1 else hit
        value = jnp.sum(jnp.where(keep, found, 0.0), axis=1, keepdims=True)
        sent = jnp.where(spot == float(index * capacity), value, sent)
    aim = lax.broadcasted_iota(jnp.int32, (targets, P_SIZE), 0) == dest_ref[...]
    aim = jnp.where(aim, 1.0, 0.0)
    base_ref[...] = jnp.dot(aim, sent, precision=lax.Precision.HIGHEST, preferred_element_type=f32)
    code_ref[...] = jnp.where(hit, code, 0.0)
    place_ref[...] = jnp.where(spot == float((STATE - 1) * capacity), 1.0, 0.0)


def density_kernel(
    rho_in,
    ent_ref,
    a_ref,
    b_ref,
    tab_in,
    near_in,
    base_ref,
    code_ref,
    place_ref,
    dest_ref,
    left_ref,
    total_in,
    off_ref,
    act_ref,
    cnt_ref,
    cell_ref,
    offset_ref,
    job_ref,
    span_ref,
    new_ref,
    out_ref,
    tab_ref,
    near_ref,
    total_ref,
    names_a,
    names_b,
    made_ref,
    beta_ref,
    sems,
):
    cells = new_ref.shape[0]
    slots = act_ref.shape[0]
    me = own_index()
    odd = me % 2
    copies = start_copies(
        [
            (ref.at[pl.ds(PLANES * RIM, 8), :], names)
            for ref, names in ((a_ref, names_a), (b_ref, names_b))
        ],
        sems,
    )
    start_of_a = (1 - odd) * (cells + RIM)
    for in_ref, start in ((a_ref, start_of_a), (b_ref, cells + RIM - start_of_a)):
        put_table(tab_ref, start, RIM, *[in_ref[pl.ds(i * RIM, RIM), :] for i in range(PLANES)])

    jobs = job_ref[0]

    def late_entry(job, place, weight):
        tile = stencil_tile(tab_ref, off_ref, cell_ref[place], offset_ref[place])
        span = pl.ds(pl.multiple_of(span_ref[job], P_SIZE), P_SIZE)
        outer, inner, kept = density_terms(left_ref[span, :], [tile], [weight])
        total_ref[span, :] = total_ref[span, :] + (outer - 4.0 * inner)
        return kept[0]

    @pl.loop(JOBS, jobs)
    def _(job):
        place = job_ref[job + 1]
        near_ref[pl.ds(pl.multiple_of(place * 8, 8), 8), :] = late_entry(job, place, None)

    for turn in range(JOBS):
        valid = turn < jobs
        job = jnp.where(valid, turn, 0)
        place = jnp.where(valid, job_ref[turn + 1], 0)
        kept = late_entry(job, place, jnp.where(valid, 1.0, 0.0))
        target = jnp.where(valid, place, slots * NBR)
        near_ref[pl.ds(pl.multiple_of(target * 8, 8), 8), :] = kept

    for slot in range(slots):
        mine = act_ref[slot] - me * cells
        inverse_len = tile_of(tab_ref, RIM + mine)[6:7, :]
        span = pl.ds(slot * P_SIZE, P_SIZE)
        left = left_ref[span, :]
        outer_sum = jnp.zeros((P_SIZE, P_SIZE), f32)
        inner_sum = jnp.zeros((P_SIZE, P_SIZE), f32)
        for first in range(early(slot), NBR, 2):
            positions = range(first, min(first + 2, NBR))
            tiles = []
            for position in positions:
                place = place_of(slot, position)
                tiles.append(stencil_tile(tab_ref, off_ref, cell_ref[place], offset_ref[place]))
            outer, inner, kept = density_terms(left, tiles, [None] * len(tiles))
            outer_sum, inner_sum = outer_sum + outer, inner_sum + inner
            for position, tile in zip(positions, kept):
                near_ref[pl.ds(place_of(slot, position) * 8, 8), :] = tile
        total = total_ref[span, :] + (outer_sum - 4.0 * inner_sum)
        made = row_sums(total) * (2.0 * kernel_norm) * inverse_len * inverse_len * inverse_len
        made = jnp.where(slot < cnt_ref[0], made, new_ref[pl.ds(mine, 1), :])
        beta = beta_of(inverse_len, ent_ref[pl.ds(mine, 1), :], made)
        made_ref[slot : slot + 1, :] = made
        beta_ref[slot : slot + 1, :] = beta

    for slot in range(slots):
        mine = act_ref[slot] - me * cells
        new_ref[pl.ds(mine, 1), :] = made_ref[slot : slot + 1, :]
        tab_ref[pl.ds((RIM + mine) * 8 + 7, 1), :] = beta_ref[slot : slot + 1, :]
    code = code_ref[...]
    chosen = jnp.zeros_like(code)
    for slot in range(slots):
        chosen = jnp.where(code == float(slot + 1), made_ref[slot : slot + 1, :], chosen)
    late = place_ref[...] * jnp.sum(chosen, axis=1, keepdims=True)
    targets = base_ref.shape[0]
    aim = lax.broadcasted_iota(jnp.int32, (targets, P_SIZE), 0) == dest_ref[...]
    aim = jnp.where(aim, 1.0, 0.0)
    for slot in range(slots):
        out_ref[:, 1 + slot, 0, :] = jnp.broadcast_to(beta_ref[slot : slot + 1, :], (targets, P_SIZE))
    sent = base_ref[...] + jnp.dot(
        aim, late, precision=lax.Precision.HIGHEST, preferred_element_type=f32
    )
    out_ref[:, 0, 0, :] = sent
    for copy in copies:
        copy.wait()


def spline(base, slope, distance):
    step = distance * slope
    outer = jnp.maximum(base - step, 0.0)
    least = jnp.minimum(step, outer)
    return least * (outer + (outer - least))


def pull_sums(pulls, nears):
    row = row_ids()
    highs = [pull.astype(bf16) for pull in pulls]
    lows = [(pull - high.astype(f32)).astype(bf16) for pull, high in zip(pulls, highs)]
    sides = []
    for near in nears:
        weighed = jnp.where(row < 3, near, 1.0) * near[5:6, :]
        sides.append(jnp.concatenate(split(weighed), axis=0).astype(bf16))
    return lax.dot_general(
        jnp.concatenate(highs + lows, axis=1),
        jnp.concatenate(sides + sides, axis=1),
        (((1,), (1,)), ((), ())),
        preferred_element_type=f32,
    )


def force_kernel(
    tab_ref,
    near_ref,
    new_ref,
    names_a,
    names_b,
    act_ref,
    cnt_ref,
    cell_ref,
    acc_out,
    list_ref,
    new_out,
    left_ref,
    sems,
):
    cells = tab_ref.shape[0] // 8 - 2 * RIM
    me = own_index()
    odd = me % 2
    slots = act_ref.shape[0]
    copies = start_copies([(new_ref, new_out)], sems)
    fa = [names_a[0, s].astype(jnp.int32) for s in range(slots)]
    fb = [names_b[0, s].astype(jnp.int32) for s in range(slots)]
    left = [jnp.where(odd == 1, fa[s], fb[s]) for s in range(slots)]
    right = [jnp.where(odd == 1, fb[s], fa[s]) for s in range(slots)]
    left = [jnp.where(v >= cells - RIM, v - (cells - RIM), -1) for v in left]
    right = [jnp.where(jnp.logical_and(v >= 0, v < RIM), v + cells + RIM, -1) for v in right]
    at = jnp.int32(0)
    for slot in range(slots):
        live = slot < cnt_ref[0]
        mine = act_ref[slot] - me * cells
        own = tile_of(tab_ref, RIM + mine)
        columns = own.T
        own_base = jnp.broadcast_to(columns[:, 7:8], (P_SIZE, P_SIZE))
        own_slope = own_base * jnp.broadcast_to(columns[:, 6:7], (P_SIZE, P_SIZE))
        left_side = own_features(own, 1.0)
        left_ref[pl.ds(slot * P_SIZE, P_SIZE), :] = left_side
        sums = jnp.zeros((P_SIZE, 24), f32)
        for block in groups(SUM_GROUP):
            pulls, nears = [], []
            for first in range(block.start, block.stop, 2):
                group = range(first, min(first + 2, block.stop))
                tiles = [near_ref[pl.ds((slot * NBR + entry) * 8, 8), :] for entry in group]
                other = jnp.concatenate([other_features(tile) for tile in tiles], axis=1)
                squares = jnp.dot(left_side, other, preferred_element_type=f32)
                for place, entry in enumerate(group):
                    near = tiles[place]
                    cell = cell_ref[place_of(slot, entry)]
                    found = jnp.int32(-1)
                    for s in range(slots):
                        found = jnp.where(cell == left[s], s, found)
                        found = jnp.where(cell == right[s], slots + s, found)
                    list_ref[at + 1] = (slot * NBR + entry) * (2 * slots) + found
                    at = at + jnp.where(jnp.logical_and(found >= 0, live), 1, 0)

                    beta = tab_ref[pl.ds(cell * 8 + 7, 1), :]
                    slope = beta * near[6:7, :]
                    square = jnp.maximum(squares[:, place * P_SIZE : (place + 1) * P_SIZE], near[6:7, :] * TINY)
                    inverse = lax.rsqrt(square)
                    distance = square * inverse
                    pull = spline(own_base, own_slope, distance) + spline(beta, slope, distance)
                    pull = pull * inverse
                    pulls.append(pull)
                    nears.append(near)
            sums = sums + pull_sums(pulls, nears)
        flat = sums.T
        flat = flat[0:8, :] + flat[8:16, :] + flat[16:24, :]
        made = jnp.where(live, own * flat[3:4, :] - flat, 0.0)
        for axis in range(3):
            acc_out[axis, slot : slot + 1, :] = made[axis : axis + 1, :]
    list_ref[0] = at
    for copy in copies:
        copy.wait()


def finish_kernel(
    capacity,
    tab_ref,
    near_ref,
    part_ref,
    got_ref,
    pick_ref,
    left_ref,
    list_ref,
    act_ref,
    acc_out,
    arrive_ref,
    late_ref,
):
    cells = tab_ref.shape[0] // 8 - 2 * RIM
    me = own_index()
    slots = act_ref.shape[0]
    targets = got_ref.shape[0]
    acc_out[...] = part_ref[...]
    rows = got_ref[:, 0, 0, :]
    width = targets * capacity
    sender = lax.broadcasted_iota(jnp.int32, (targets, width), 1) // capacity
    mask = sender == lax.broadcasted_iota(jnp.int32, (targets, width), 0)
    pieces = jnp.concatenate(split(rows), axis=0).astype(bf16)
    spread = jnp.dot(pieces, pick_ref[...], preferred_element_type=f32)
    spread = spread[0:targets] + spread[targets : 2 * targets] + spread[2 * targets :]
    for index in range(STATE):
        part = spread[:, index * width : (index + 1) * width]
        arrive_ref[index : index + 1, :] = jnp.sum(jnp.where(mask, part, 0.0), axis=0, keepdims=True)

    count = list_ref[0]

    @pl.when(count > 0)
    def _():
        late_ref[...] = jnp.zeros_like(late_ref)

        @pl.loop(0, (count + ITEMS - 1) // ITEMS)
        def _(block):
            made = []
            for step in range(ITEMS):
                item = block * ITEMS + step
                word = list_ref[jnp.minimum(item, count - 1) + 1]
                found = word % (2 * slots)
                place = word // (2 * slots)
                slot = place // NBR
                span = pl.ds(pl.multiple_of(slot * P_SIZE, P_SIZE), P_SIZE)
                other = jnp.where(found < slots, me - 1, me + 1)
                near = near_ref[pl.ds(pl.multiple_of(place * 8, 8), 8), :]
                beta = got_ref[other, 1 + found % slots]
                beta = beta * jnp.where(item < count, 1.0, 0.0)
                square = jnp.dot(
                    left_ref[span, :], other_features(near), preferred_element_type=f32
                )
                square = jnp.maximum(square, near[6:7, :] * TINY)
                inverse = lax.rsqrt(square)
                pull = spline(beta, beta * near[6:7, :], square * inverse) * inverse
                made.append((span, pull_sums([pull], [near])))
            for span, sums in made:
                late_ref[span, :] = late_ref[span, :] + sums

        for slot in range(slots):
            own = tile_of(tab_ref, RIM + act_ref[slot] - me * cells)
            flat = late_ref[pl.ds(slot * P_SIZE, P_SIZE), :].T
            flat = flat[0:8, :] + flat[8:16, :] + flat[16:24, :]
            made = own * flat[3:4, :] - flat
            for axis in range(3):
                acc_out[axis, slot : slot + 1, :] += made[axis : axis + 1, :]


def local(
    positions,
    masses,
    smoothing,
    entropy,
    density,
    active_cells,
    active_count,
    neighbours,
    mig_source,
    mig_dest,
):
    cells = masses.shape[0]
    slots = active_cells.shape[0]
    devices = lax.axis_size(AXES)
    mig_rows = mig_source.shape[0]
    capacity = max(2, 2 * mig_rows // devices)
    shape = jax.ShapeDtypeStruct
    rim_shape = shape((PLANES * RIM + 8, P_SIZE), f32)
    tab_shape = pltpu.VMEM(((cells + 2 * RIM) * 8, P_SIZE), f32)
    near_shape = pltpu.VMEM(((slots * NBR + 1) * 8, P_SIZE), f32)
    name_shape = pltpu.SMEM((8, P_SIZE), f32)
    fields = (positions, masses, smoothing, entropy, density)
    rows = (mig_source.reshape(1, mig_rows), mig_dest.reshape(1, mig_rows))
    lists = (active_cells, neighbours)

    raw = [in_hbm(v) for v in fields]
    send_b, send_a, active, near_ids = pl.pallas_call(
        pack_kernel,
        out_shape=(rim_shape, rim_shape) + tuple(pltpu.SMEM(v.shape, v.dtype) for v in lists),
        in_specs=[HBM] * 7,
        out_specs=(VMEM,) * 2 + (SMEM,) * 2,
        scratch_shapes=[
            pltpu.VMEM((2, 3, RIM, P_SIZE), f32),
            pltpu.SemaphoreType.DMA((16,)),
        ],
        compiler_params=PARAMS,
        name="pack",
    )(*raw, *[in_hbm(v) for v in lists])
    send_b, active_count = lax.optimization_barrier((send_b, active_count))

    pairs_a = [(i ^ 1, i) for i in range(devices) if i ^ 1 < devices]
    pairs_b = []
    for i in range(1, devices - 1, 2):
        pairs_b += [(i, i + 1), (i + 1, i)]
    got_b = lax.ppermute(send_b, AXES, pairs_b)
    got_a = lax.ppermute(send_a, AXES, pairs_a)

    ent, rho, dest, table, base, code, place, pick, near, left, total, offsets, *found = pl.pallas_call(
        functools.partial(migrant_kernel, capacity),
        out_shape=(
            pltpu.VMEM((cells, P_SIZE), f32),
            pltpu.VMEM((cells, P_SIZE), f32),
            pltpu.VMEM((1, mig_rows), jnp.int32),
            tab_shape,
            pltpu.VMEM((devices, P_SIZE), f32),
            pltpu.VMEM((mig_rows, P_SIZE), f32),
            pltpu.VMEM((mig_rows, P_SIZE), f32),
            pltpu.VMEM((P_SIZE, STATE * devices * capacity), bf16),
            near_shape,
            pltpu.VMEM((slots * P_SIZE, 48), bf16),
            pltpu.VMEM((slots * P_SIZE, P_SIZE), f32),
            pltpu.VMEM((NBR * 8, P_SIZE), f32),
            pltpu.SMEM((slots * NBR,), jnp.int32),
            pltpu.SMEM((slots * NBR,), jnp.int32),
            pltpu.SMEM((slots * NBR + 2,), jnp.int32),
            pltpu.SMEM((slots * NBR + 1,), jnp.int32),
        ),
        in_specs=[HBM] * 7 + [SMEM] * 3,
        out_specs=(VMEM,) * 12 + (SMEM,) * 4,
        scratch_shapes=[
            pltpu.VMEM((3, cells, P_SIZE), f32),
            pltpu.VMEM((cells, P_SIZE), f32),
            pltpu.VMEM((cells, P_SIZE), f32),
            pltpu.VMEM((1, mig_rows), jnp.int32),
            pltpu.SemaphoreType.DMA((7,)),
        ],
        compiler_params=PARAMS,
        name="migrants",
    )(*raw, *[in_hbm(v) for v in rows], active, active_count, near_ids)

    made, outgoing, table, near, _, names_a, names_b = pl.pallas_call(
        density_kernel,
        out_shape=(
            pltpu.VMEM((cells, P_SIZE), f32),
            shape((devices, 1 + slots, 1, P_SIZE), f32),
            tab_shape,
            near_shape,
            pltpu.VMEM((slots * P_SIZE, P_SIZE), f32),
            name_shape,
            name_shape,
        ),
        in_specs=[VMEM] * 13 + [SMEM] * 6,
        out_specs=(VMEM,) * 5 + (SMEM,) * 2,
        input_output_aliases={0: 0, 4: 2, 5: 3, 11: 4},
        scratch_shapes=[
            pltpu.VMEM((8, P_SIZE), f32),
            pltpu.VMEM((8, P_SIZE), f32),
            pltpu.SemaphoreType.DMA((2,)),
        ],
        compiler_params=PARAMS,
        name="density",
    )(
        rho,
        ent,
        got_a,
        got_b,
        table,
        near,
        base,
        code,
        place,
        dest,
        left,
        total,
        offsets,
        active,
        active_count,
        *found,
    )

    incoming = lax.all_to_all(outgoing, AXES, split_axis=0, concat_axis=0, tiled=True)

    todo_len = pl.cdiv(slots * NBR + 2, P_SIZE) * P_SIZE
    partial, todo, new_density, left = pl.pallas_call(
        force_kernel,
        out_shape=(
            shape((3, slots, P_SIZE), f32),
            pltpu.SMEM((todo_len,), jnp.int32),
            shape((cells, P_SIZE), f32),
            pltpu.VMEM((slots * P_SIZE, 48), bf16),
        ),
        in_specs=[VMEM] * 3 + [SMEM] * 5,
        out_specs=(VMEM, SMEM, HBM, VMEM),
        scratch_shapes=[
            pltpu.SemaphoreType.DMA((1,)),
        ],
        compiler_params=PARAMS,
        name="force",
    )(table, near, made, names_a, names_b, active, active_count, found[0])

    acceleration, arrivals = pl.pallas_call(
        functools.partial(finish_kernel, capacity),
        out_shape=(
            shape((3, slots, P_SIZE), f32),
            shape((STATE, devices * capacity), f32),
        ),
        in_specs=[VMEM] * 6 + [SMEM] * 2,
        out_specs=(VMEM, VMEM),
        scratch_shapes=[pltpu.VMEM((slots * P_SIZE, 24), f32)],
        compiler_params=PARAMS,
        name="finish",
    )(table, near, partial, incoming, pick, left, todo, active)
    return (new_density, acceleration, arrivals)


def solution(mesh):
    placed = (
        P(None, AXES, None),
        P(AXES, None),
        P(AXES, None),
        P(AXES, None),
        P(AXES, None),
        P(AXES),
        P(AXES),
        P(AXES, None),
        P(AXES),
        P(AXES, None),
    )
    return jax.shard_map(
        local,
        mesh=mesh,
        in_specs=placed,
        out_specs=(P(AXES, None), P(None, AXES, None), P(None, AXES)),
        check_vma=False,
    )
```
